128 devices in a mesh: stream: 32 (over z, y, x_lo), span: 4 (over x_hi, core).
Axes of the slice: x: 4 (x_hi: 2, x_lo: 2; x = x_hi * 2 + x_lo), y: 4, z: 4, core: 2. Of those that a mesh axis runs over, the one named last changes fastest.
Arguments:
- rhs: float32 [128, 4, 64, 4096], P('stream', None, None, 'span'), may hold values from -0.15625 to 0.15625
- lagged: float32 [128, 4, 64, 4096], P('stream', None, None, 'span'), may hold values from -6 to 6
- face_types: int32 [3, 128, 4096], P(None, 'stream', 'span'), may hold values from 0 to 5
- stream_scale: float32 [128, 4096], P('stream', 'span'), may hold values from 1 to 4
- span_scale: float32 [2, 128, 4096], P(None, 'stream', 'span'), may hold values from 0.004 to 0.016
- absorb: float32 [128, 4096], P('stream', 'span'), may hold values from 0.002 to 0.008
- up_blocks: float32 [6, 64, 64], replicated, may hold values from -1 to 0.03
- down_blocks: float32 [6, 64, 64], replicated, may hold values from -1 to 0.03
- diag_inverse: float32 [64, 64], replicated, may hold values from -0.012 to 1
Outputs:
- increment: float32 [128, 4, 64, 4096], P('stream', None, None, 'span')
The draws below stay inside these ranges and needn't reach their ends.
All inputs are finite; a program needn't handle non-finite values.
Results may differ from the reference program's by a relative error of at most 0.00023.
Values sent between devices are 32-bit elements; how exact they have to be, the bound alone decides.
A program may use at most 64 MiB of HBM per device.

```python
import math
import jax
import jax.numpy as jnp
from jax import lax

P_DOF = 64
TRACERS = 4
NTYPES = 6
NS = 128
NC = 4096


def make_blocks(key, spread, limit):
    key_rates, key_types, key_noise = jax.random.split(key, 3)
    low_loss = jnp.log(0.001)
    high_loss = jnp.log(0.08)
    losses = jnp.exp(jax.random.uniform(key_rates, (P_DOF,), jnp.float32, low_loss, high_loss))
    factors = jax.random.uniform(key_types, (NTYPES, P_DOF), jnp.float32, 0.8, 1.2)
    decays = 1.0 - losses[None, :] * factors
    jitter = jnp.clip(spread * jax.random.normal(key_noise, (NTYPES, P_DOF, P_DOF), jnp.float32), -limit, limit)
    identity = jnp.eye(P_DOF, dtype=jnp.float32)
    return -(decays[:, :, None] * identity) + jitter * (1.0 - identity)


def draw_up_blocks(key, part):
    return make_blocks(jax.random.fold_in(key, 11), 0.01, 0.03)


def draw_down_blocks(key, part):
    return make_blocks(jax.random.fold_in(key, 23), 0.01, 0.03)


def draw_diag_inverse(key, part):
    key_rates, key_noise = jax.random.split(jax.random.fold_in(key, 37))
    losses = jnp.exp(jax.random.uniform(key_rates, (P_DOF,), jnp.float32, jnp.log(0.0005), jnp.log(0.01)))
    jitter = jnp.clip(0.004 * jax.random.normal(key_noise, (P_DOF, P_DOF), jnp.float32), -0.012, 0.012)
    identity = jnp.eye(P_DOF, dtype=jnp.float32)
    return (1.0 - losses)[:, None] * identity + jitter * (1.0 - identity)


def set_ends(values, rng, low, top_value):
    place = [jax.random.randint(jax.random.fold_in(rng, axis), (), 0, length) for axis, length in enumerate(values.shape)]
    longest = values.shape.index(max(values.shape))
    beside = place[:longest] + [(place[longest] + 1) % values.shape[longest]] + place[longest + 1:]
    return values.at[tuple(place)].set(low).at[tuple(beside)].set(top_value)


def shard_levels(own_key, dims, shards, smallest, top_value):
    factor_of, own = 1.0, jax.random.fold_in(own_key, 6)
    for axis_at, parts in shards:
        steps = jnp.exp(jax.random.uniform(jax.random.fold_in(own, axis_at), (parts,), jnp.float32, smallest / len(shards), top_value / len(shards)))
        factor_of = factor_of * jnp.repeat(steps, dims[axis_at] // parts).reshape([-1 if axis == axis_at else 1 for axis in range(len(dims))])
    return factor_of


def scatter_about(key, shape, width, most, cuts=(), held_as=jnp.bfloat16):
    array = jax.random.normal(key, shape, jnp.float32) * width
    if len(cuts) > 0:
        array = shard_levels(key, shape, cuts, -0.22, 0.18) * array
    return jnp.clip(array, min=-most, max=most).astype(held_as)


def setup_inputs(seed: int = 0) -> dict:
    streams_of = jax.random.split(jax.random.key(seed), 10)
    rhs = scatter_about(streams_of[0], (NS, TRACERS, P_DOF, NC), 0.01, 0.15625, ((0, 32), (3, 4)), jnp.float32)
    lagged = scatter_about(streams_of[1], (NS, TRACERS, P_DOF, NC), 1.0, 6.0, ((0, 32), (3, 4)), jnp.float32)
    face_types = set_ends(jax.random.randint(streams_of[2], (3, NS, NC), 0, NTYPES), jax.random.fold_in(streams_of[2], 1), 0, NTYPES - 1).astype(jnp.int32)
    stream_scale = jnp.clip(jnp.exp(math.log(4.0) - 1.3862944 * jax.random.uniform(streams_of[3], (NS, NC), jnp.float32) ** shard_levels(streams_of[3], (NS, NC), ((0, 32), (1, 4)), -0.2, 0.2)), 1.0, 4.0)
    span_scale = jnp.clip(jnp.exp(math.log(0.016) - 1.3862944 * jax.random.uniform(streams_of[4], (2, NS, NC), jnp.float32) ** shard_levels(streams_of[4], (2, NS, NC), ((1, 32), (2, 4)), -0.2, 0.2)), 0.004, 0.016)
    absorb = jnp.clip(jnp.exp(math.log(0.008) - 1.3862944 * jax.random.uniform(streams_of[5], (NS, NC), jnp.float32) ** shard_levels(streams_of[5], (NS, NC), ((0, 32), (1, 4)), -0.2, 0.2)), 0.002, 0.008)
    up_blocks = draw_up_blocks(jax.random.fold_in(streams_of[9], 71), 0)
    down_blocks = draw_down_blocks(jax.random.fold_in(streams_of[9], 71), 0)
    diag_inverse = draw_diag_inverse(jax.random.fold_in(streams_of[9], 71), 0)
    return {"rhs": rhs, "lagged": lagged, "face_types": face_types, "stream_scale": stream_scale, "span_scale": span_scale, "absorb": absorb, "up_blocks": up_blocks, "down_blocks": down_blocks, "diag_inverse": diag_inverse}


precise = lax.Precision.HIGHEST


def typed_apply(blocks_table, type_ids, state_in):
    matrices = blocks_table[type_ids]
    return jnp.einsum('cpq,rqc->rpc', matrices, state_in, precision=precise)


def inverse_apply(diag_inverse, balance, denom_row):
    return jnp.einsum('pq,rqc->rpc', diag_inverse, balance, precision=precise) / denom_row


def reference(rhs, lagged, face_types, stream_scale, span_scale, absorb, up_blocks, down_blocks, diag_inverse):
    denominator = stream_scale + span_scale[0] + span_scale[1] + absorb
    zero_column = jnp.zeros_like(lagged[..., :1])
    lower_side = jnp.concatenate([zero_column, lagged[..., :-1]], axis=3)
    upper_side = jnp.concatenate([lagged[..., 1:], zero_column], axis=3)

    def span_row(pieces):
        low_state, high_state, low_type, high_type, low_scale, high_scale = pieces
        return low_scale * typed_apply(up_blocks, low_type, low_state) + high_scale * typed_apply(up_blocks, high_type, high_state)

    span_terms = lax.map(span_row, (lower_side, upper_side, face_types[1], face_types[2], span_scale[0], span_scale[1]))

    def forward_row(previous, pieces):
        rhs_row, span_here, type_row, scale_row, denom_row = pieces
        balance = rhs_row - span_here - scale_row * typed_apply(up_blocks, type_row, previous)
        solved = inverse_apply(diag_inverse, balance, denom_row)
        return solved, solved

    start_state = jnp.zeros_like(rhs[0])
    unused, forward_part = lax.scan(forward_row, start_state, (rhs, span_terms, face_types[0], stream_scale, denominator))

    def backward_row(carried, pieces):
        part_row, type_row, scale_row, denom_row = pieces
        result = part_row - inverse_apply(diag_inverse, carried, denom_row)
        return scale_row * typed_apply(down_blocks, type_row, result), result

    unused_two, increment = lax.scan(backward_row, start_state, (forward_part, face_types[0], stream_scale, denominator), reverse=True)
    return increment
```

```python
import functools

import jax
import jax.numpy as jnp
from jax import lax
from jax.experimental import pallas as pl
from jax.experimental.pallas import tpu as pltpu
from jax.sharding import PartitionSpec as P

precise = lax.Precision.HIGHEST
LANES = 128


def padded_2(block, sides, width):
    for axis, dim in sides:
        count = lax.axis_size(axis)
        forward = [(i, i + 1) for i in range(count - 1)]
        backward = [(target, source) for source, target in forward]
        low = lax.ppermute(
            lax.slice_in_dim(block, block.shape[dim] - width, None, axis=dim), axis, forward
        )
        high = lax.ppermute(lax.slice_in_dim(block, 0, width, axis=dim), axis, backward)
        block = jnp.concatenate([low, block, high], axis=dim)
    return block


def typed_product(blocks_table, type_ids, state_in):
    products = jnp.einsum("tpq,rqw->trpw", blocks_table, state_in, precision=precise)
    kinds = jnp.arange(blocks_table.shape[0], dtype=jnp.int32)
    selector = (type_ids[None, :] == kinds[:, None]).astype(jnp.float32)
    return jnp.sum(products * selector[:, None, None, :], axis=0)


def span_block(padded, face_types, span_scale, up_blocks, offset, breadth):
    lower_side = lax.dynamic_slice_in_dim(padded, offset, breadth, 3)
    upper_side = lax.dynamic_slice_in_dim(padded, offset + 2, breadth, 3)
    lower_types = face_types[1]
    upper_types = face_types[2]
    lower_scale = span_scale[0]
    upper_scale = span_scale[1]
    results = []
    for row_index in range(padded.shape[0]):
        lower_term = lower_scale[row_index] * typed_product(
            up_blocks, lower_types[row_index], lower_side[row_index]
        )
        upper_term = upper_scale[row_index] * typed_product(
            up_blocks, upper_types[row_index], upper_side[row_index]
        )
        results.append(lower_term + upper_term)
    return jnp.stack(results)


def kernel_typed(table_ref, types, state):
    dof = state.shape[0]
    products = jnp.dot(table_ref[...], state, precision=precise, preferred_element_type=jnp.float32)
    picked = jnp.zeros_like(state)
    for kind in range(table_ref.shape[0] // dof):
        picked = jnp.where(types == kind, products[kind * dof:(kind + 1) * dof], picked)
    return picked


def barrier_with_neighbours(me, length):
    barrier = pltpu.get_barrier_semaphore()

    @pl.when(me > 0)
    def _():
        pl.semaphore_signal(barrier, inc=1, device_id={"stream": me - 1},
                            device_id_type=pl.DeviceIdType.MESH)

    @pl.when(me < length - 1)
    def _():
        pl.semaphore_signal(barrier, inc=1, device_id={"stream": me + 1},
                            device_id_type=pl.DeviceIdType.MESH)

    ends = jnp.logical_or(me == 0, me == length - 1)

    @pl.when(ends)
    def _():
        pl.semaphore_wait(barrier, 1)

    @pl.when(jnp.logical_not(ends))
    def _():
        pl.semaphore_wait(barrier, 2)


def sweep_kernel(length, direction, balance_ref, types_ref, scale_ref, denom_ref, table_ref, inverse_ref,
                 out_ref, recv_ref, send_ref, send_sem, recv_sem):
    me = lax.axis_index("stream")
    rows, tracers, dof, columns = balance_ref.shape
    groups = columns // LANES
    blocks = tracers * groups
    if direction > 0:
        has_source = me > 0
        has_target = me < length - 1
        target = me + 1
    else:
        has_source = me < length - 1
        has_target = me > 0
        target = me - 1

    @pl.when(jnp.logical_not(has_source))
    def _():
        recv_ref[...] = jnp.zeros(recv_ref.shape, jnp.float32)

    barrier_with_neighbours(me, length)

    def copy_of(k):
        return pltpu.make_async_remote_copy(
            src_ref=send_ref.at[k],
            dst_ref=recv_ref.at[k],
            send_sem=send_sem.at[k],
            recv_sem=recv_sem.at[k],
            device_id={"stream": target},
            device_id_type=pl.DeviceIdType.MESH,
        )

    row_order = list(range(rows)) if direction > 0 else list(range(rows - 1, -1, -1))

    def block_step(k, carry):
        tracer = k % tracers
        group = k // tracers
        cols = pl.ds(pl.multiple_of(group * LANES, LANES), LANES)

        @pl.when(has_source)
        def _():
            copy_of(k).wait_recv()

        state = recv_ref[k]
        for row in row_order:
            types = types_ref[pl.ds(row, 1), cols]
            scale = scale_ref[pl.ds(row, 1), cols]
            denom = denom_ref[pl.ds(row, 1), cols]
            if direction > 0:
                balance = balance_ref[row, tracer, :, cols] - scale * kernel_typed(table_ref, types, state)
                state = jnp.dot(inverse_ref[...], balance, precision=precise,
                                preferred_element_type=jnp.float32) / denom
                out_ref[row, tracer, :, cols] = state
            else:
                solved = balance_ref[row, tracer, :, cols] - jnp.dot(
                    inverse_ref[...], state, precision=precise, preferred_element_type=jnp.float32) / denom
                out_ref[row, tracer, :, cols] = solved
                state = scale * kernel_typed(table_ref, types, solved)
        send_ref[k] = state

        @pl.when(has_target)
        def _():
            copy_of(k).start()

        return carry

    lax.fori_loop(0, blocks, block_step, 0)

    def drain(k, carry):
        copy_of(k).wait_send()
        return carry

    @pl.when(has_target)
    def _():
        lax.fori_loop(0, blocks, drain, 0)


def sweep(direction, collective_id, balance, types, scale, denom, table, inverse):
    rows, tracers, dof, columns = balance.shape
    length = lax.axis_size("stream")
    blocks = tracers * (columns // LANES)
    vmem = pltpu.VMEM
    return pl.pallas_call(
        functools.partial(sweep_kernel, length, direction),
        out_shape=jax.ShapeDtypeStruct(balance.shape, jnp.float32),
        in_specs=[pl.BlockSpec(memory_space=vmem)] * 6,
        out_specs=pl.BlockSpec(memory_space=vmem),
        scratch_shapes=[
            pltpu.VMEM((blocks, dof, LANES), jnp.float32),
            pltpu.VMEM((blocks, dof, LANES), jnp.float32),
            pltpu.SemaphoreType.DMA((blocks,)),
            pltpu.SemaphoreType.DMA((blocks,)),
        ],
        compiler_params=pltpu.CompilerParams(
            collective_id=collective_id, has_side_effects=True, vmem_limit_bytes=60 * 1024 * 1024
        ),
    )(balance, types, scale, denom, table, inverse)


def per_device(
    rhs, lagged, face_types, stream_scale, span_scale, absorb, up_blocks, down_blocks, diag_inverse
):
    columns = rhs.shape[3]
    padded = padded_2(lagged, (("span", 3),), 1)
    denominator = stream_scale + span_scale[0] + span_scale[1] + absorb
    span_terms = span_block(padded, face_types, span_scale, up_blocks, 0, columns)
    dof = up_blocks.shape[1]
    up_table = up_blocks.reshape(-1, dof)
    down_table = down_blocks.reshape(-1, dof)
    forward_part = sweep(1, 0, rhs - span_terms, face_types[0], stream_scale, denominator, up_table,
                         diag_inverse)
    increment = sweep(-1, 1, forward_part, face_types[0], stream_scale, denominator, down_table,
                      diag_inverse)
    return increment


def solution(mesh):
    return jax.shard_map(
        per_device,
        mesh=mesh,
        in_specs=(
            P("stream", None, None, "span"),
            P("stream", None, None, "span"),
            P(None, "stream", "span"),
            P("stream", "span"),
            P(None, "stream", "span"),
            P("stream", "span"),
            P(),
            P(),
            P(),
        ),
        out_specs=P("stream", None, None, "span"),
        check_vma=False,
    )
```

```python
import functools

import jax
import jax.numpy as jnp
from jax import lax
from jax.experimental import pallas as pl
from jax.experimental.pallas import tpu as pltpu
from jax.sharding import PartitionSpec as P

precise = lax.Precision.HIGHEST
LANES = 128


def padded_2(block, sides, width):
    for axis, dim in sides:
        count = lax.axis_size(axis)
        forward = [(i, i + 1) for i in range(count - 1)]
        backward = [(target, source) for source, target in forward]
        low = lax.ppermute(
            lax.slice_in_dim(block, block.shape[dim] - width, None, axis=dim), axis, forward
        )
        high = lax.ppermute(lax.slice_in_dim(block, 0, width, axis=dim), axis, backward)
        block = jnp.concatenate([low, block, high], axis=dim)
    return block


def typed_product(blocks_table, type_ids, state_in):
    products = jnp.einsum("tpq,rqw->trpw", blocks_table, state_in, precision=precise)
    kinds = jnp.arange(blocks_table.shape[0], dtype=jnp.int32)
    selector = (type_ids[None, :] == kinds[:, None]).astype(jnp.float32)
    return jnp.sum(products * selector[:, None, None, :], axis=0)


def span_block(padded, face_types, span_scale, up_blocks, offset, breadth):
    lower_side = lax.dynamic_slice_in_dim(padded, offset, breadth, 3)
    upper_side = lax.dynamic_slice_in_dim(padded, offset + 2, breadth, 3)
    lower_types = face_types[1]
    upper_types = face_types[2]
    lower_scale = span_scale[0]
    upper_scale = span_scale[1]
    results = []
    for row_index in range(padded.shape[0]):
        lower_term = lower_scale[row_index] * typed_product(
            up_blocks, lower_types[row_index], lower_side[row_index]
        )
        upper_term = upper_scale[row_index] * typed_product(
            up_blocks, upper_types[row_index], upper_side[row_index]
        )
        results.append(lower_term + upper_term)
    return jnp.stack(results)


def split_table(table):
    high = lax.reduce_precision(table, exponent_bits=8, mantissa_bits=7)
    low = table - high
    high = high.astype(jnp.bfloat16)
    low = low.astype(jnp.bfloat16)
    return jnp.concatenate([high, low, high], axis=1)


def kernel_typed(table_ref, types, state):
    dof = state.shape[0]
    high = state.astype(jnp.bfloat16)
    low = (state - high.astype(jnp.float32)).astype(jnp.bfloat16)
    stacked = jnp.concatenate([high, high, low], axis=0)
    products = jnp.dot(table_ref[...], stacked, preferred_element_type=jnp.float32)
    picked = products[0:dof]
    for kind in range(1, table_ref.shape[0] // dof):
        picked = jnp.where(types == kind, products[kind * dof:(kind + 1) * dof], picked)
    return picked


def barrier_with_neighbours(me, length):
    barrier = pltpu.get_barrier_semaphore()

    @pl.when(me > 0)
    def _():
        pl.semaphore_signal(barrier, inc=1, device_id={"stream": me - 1},
                            device_id_type=pl.DeviceIdType.MESH)

    @pl.when(me < length - 1)
    def _():
        pl.semaphore_signal(barrier, inc=1, device_id={"stream": me + 1},
                            device_id_type=pl.DeviceIdType.MESH)

    ends = jnp.logical_or(me == 0, me == length - 1)

    @pl.when(ends)
    def _():
        pl.semaphore_wait(barrier, 1)

    @pl.when(jnp.logical_not(ends))
    def _():
        pl.semaphore_wait(barrier, 2)


def sweep_kernel(length, direction, width, grouped, start_ref, types_ref, coeff_ref, denom_ref, table_ref,
                 out_ref, recv_ref, send_ref, send_sem, recv_sem):
    me = lax.axis_index("stream")
    rows, tracers, dof, columns = start_ref.shape
    sets = tracers // grouped
    blocks = sets * (columns // width)
    if direction > 0:
        has_source = me > 0
        has_target = me < length - 1
        target = me + 1
    else:
        has_source = me < length - 1
        has_target = me > 0
        target = me - 1

    @pl.when(jnp.logical_not(has_source))
    def _():
        recv_ref[...] = jnp.zeros(recv_ref.shape, jnp.float32)

    barrier_with_neighbours(me, length)

    def copy_of(k):
        return pltpu.make_async_remote_copy(
            src_ref=send_ref.at[k],
            dst_ref=recv_ref.at[k],
            send_sem=send_sem.at[k],
            recv_sem=recv_sem.at[k],
            device_id={"stream": target},
            device_id_type=pl.DeviceIdType.MESH,
        )

    row_order = list(range(rows)) if direction > 0 else list(range(rows - 1, -1, -1))

    def gathered(ref, row, first, cols):
        return jnp.concatenate([ref[row, first + tracer, :, cols] for tracer in range(grouped)], axis=1)

    def lanes(ref, row, cols):
        return jnp.concatenate([ref[pl.ds(row, 1), cols]] * grouped, axis=1)

    def block_step(k, carry):
        first = (k % sets) * grouped
        cols = pl.ds(pl.multiple_of((k // sets) * width, width), width)

        @pl.when(has_source)
        def _():
            copy_of(k).wait_recv()

        state = recv_ref[k]
        for row in row_order:
            types = lanes(types_ref, row, cols)
            coeff = lanes(coeff_ref, row, cols)
            if direction > 0:
                state = gathered(start_ref, row, first, cols) - coeff * kernel_typed(table_ref, types, state)
                solved = state
            else:
                solved = gathered(start_ref, row, first, cols) - state / lanes(denom_ref, row, cols)
                state = coeff * kernel_typed(table_ref, types, solved)
            for tracer in range(grouped):
                out_ref[row, first + tracer, :, cols] = solved[:, tracer * width:(tracer + 1) * width]
        send_ref[k] = state

        @pl.when(has_target)
        def _():
            copy_of(k).start()

        return carry

    lax.fori_loop(0, blocks, block_step, 0)

    def drain(k, carry):
        copy_of(k).wait_send()
        return carry

    @pl.when(has_target)
    def _():
        lax.fori_loop(0, blocks, drain, 0)


def sweep(direction, collective_id, width, grouped, start, types, coeff, denom, table):
    rows, tracers, dof, columns = start.shape
    blocks = (tracers // grouped) * (columns // width)
    length = lax.axis_size("stream")
    vmem = pltpu.VMEM
    return pl.pallas_call(
        functools.partial(sweep_kernel, length, direction, width, grouped),
        out_shape=jax.ShapeDtypeStruct(start.shape, jnp.float32),
        in_specs=[pl.BlockSpec(memory_space=vmem)] * 5,
        out_specs=pl.BlockSpec(memory_space=vmem),
        scratch_shapes=[
            pltpu.VMEM((blocks, dof, grouped * width), jnp.float32),
            pltpu.VMEM((blocks, dof, grouped * width), jnp.float32),
            pltpu.SemaphoreType.DMA((blocks,)),
            pltpu.SemaphoreType.DMA((blocks,)),
        ],
        compiler_params=pltpu.CompilerParams(
            collective_id=collective_id, has_side_effects=True, vmem_limit_bytes=60 * 1024 * 1024
        ),
    )(start, types, coeff, denom, table)


def per_device(
    rhs, lagged, face_types, stream_scale, span_scale, absorb, up_blocks, down_blocks, diag_inverse
):
    columns = rhs.shape[3]
    dof = up_blocks.shape[1]
    padded = padded_2(lagged, (("span", 3),), 1)
    denominator = stream_scale + span_scale[0] + span_scale[1] + absorb
    span_terms = span_block(padded, face_types, span_scale, up_blocks, 0, columns)
    start = jnp.einsum("pq,nrqc->nrpc", diag_inverse, rhs - span_terms, precision=precise)
    start = start / denominator[:, None, None, :]
    coeff = stream_scale / denominator
    up_table = split_table(jnp.einsum("pq,tqs->tps", diag_inverse, up_blocks, precision=precise).reshape(-1, dof))
    down_table = split_table(jnp.einsum("pq,tqs->tps", diag_inverse, down_blocks, precision=precise).reshape(-1, dof))
    width = LANES
    grouped = 1
    forward_part = sweep(1, 0, width, grouped, start, face_types[0], coeff, denominator, up_table)
    increment = sweep(-1, 1, width, grouped, forward_part, face_types[0], stream_scale, denominator, down_table)
    return increment


def solution(mesh):
    return jax.shard_map(
        per_device,
        mesh=mesh,
        in_specs=(
            P("stream", None, None, "span"),
            P("stream", None, None, "span"),
            P(None, "stream", "span"),
            P("stream", "span"),
            P(None, "stream", "span"),
            P("stream", "span"),
            P(),
            P(),
            P(),
        ),
        out_specs=P("stream", None, None, "span"),
        check_vma=False,
    )
```

```python
import functools

import jax
import jax.numpy as jnp
from jax import lax
from jax.experimental import pallas as pl
from jax.experimental.pallas import tpu as pltpu
from jax.sharding import PartitionSpec as P

precise = lax.Precision.HIGHEST
fast = lax.Precision.HIGH
LANES = 128


def padded_2(block, sides, width):
    for axis, dim in sides:
        count = lax.axis_size(axis)
        forward = [(i, i + 1) for i in range(count - 1)]
        backward = [(target, source) for source, target in forward]
        low = lax.ppermute(
            lax.slice_in_dim(block, block.shape[dim] - width, None, axis=dim), axis, forward
        )
        high = lax.ppermute(lax.slice_in_dim(block, 0, width, axis=dim), axis, backward)
        block = jnp.concatenate([low, block, high], axis=dim)
    return block


def typed_product(blocks_table, type_ids, state_in):
    products = jnp.einsum("tpq,rqw->trpw", blocks_table, state_in, precision=fast)
    kinds = jnp.arange(blocks_table.shape[0], dtype=jnp.int32)
    selector = (type_ids[None, :] == kinds[:, None]).astype(jnp.float32)
    return jnp.sum(products * selector[:, None, None, :], axis=0)


def span_block(padded, face_types, span_scale, up_blocks, offset, breadth):
    lower_side = lax.dynamic_slice_in_dim(padded, offset, breadth, 3)
    upper_side = lax.dynamic_slice_in_dim(padded, offset + 2, breadth, 3)
    lower_types = face_types[1]
    upper_types = face_types[2]
    lower_scale = span_scale[0]
    upper_scale = span_scale[1]
    results = []
    for row_index in range(padded.shape[0]):
        lower_term = lower_scale[row_index] * typed_product(
            up_blocks, lower_types[row_index], lower_side[row_index]
        )
        upper_term = upper_scale[row_index] * typed_product(
            up_blocks, upper_types[row_index], upper_side[row_index]
        )
        results.append(lower_term + upper_term)
    return jnp.stack(results)


def split_table(table):
    high = lax.reduce_precision(table, exponent_bits=8, mantissa_bits=7)
    low = table - high
    high = high.astype(jnp.bfloat16)
    low = low.astype(jnp.bfloat16)
    return jnp.concatenate([high, low, high], axis=1)


def kernel_typed(table_ref, types, state):
    dof = state.shape[0]
    high = state.astype(jnp.bfloat16)
    low = (state - high.astype(jnp.float32)).astype(jnp.bfloat16)
    stacked = jnp.concatenate([high, high, low], axis=0)
    products = jnp.dot(table_ref[...], stacked, preferred_element_type=jnp.float32)
    picked = products[0:dof]
    for kind in range(1, table_ref.shape[0] // dof):
        picked = jnp.where(types == kind, products[kind * dof:(kind + 1) * dof], picked)
    return picked


def barrier_with_neighbours(me, length):
    barrier = pltpu.get_barrier_semaphore()

    @pl.when(me > 0)
    def _():
        pl.semaphore_signal(barrier, inc=1, device_id={"stream": me - 1},
                            device_id_type=pl.DeviceIdType.MESH)

    @pl.when(me < length - 1)
    def _():
        pl.semaphore_signal(barrier, inc=1, device_id={"stream": me + 1},
                            device_id_type=pl.DeviceIdType.MESH)

    ends = jnp.logical_or(me == 0, me == length - 1)

    @pl.when(ends)
    def _():
        pl.semaphore_wait(barrier, 1)

    @pl.when(jnp.logical_not(ends))
    def _():
        pl.semaphore_wait(barrier, 2)


def sweep_kernel(length, direction, width, grouped, start_ref, types_ref, coeff_ref, denom_ref, table_ref,
                 out_ref, recv_ref, send_ref, send_sem, recv_sem):
    me = lax.axis_index("stream")
    rows, tracers, dof, columns = start_ref.shape
    sets = tracers // grouped
    blocks = sets * (columns // width)
    if direction > 0:
        has_source = me > 0
        has_target = me < length - 1
        target = me + 1
    else:
        has_source = me < length - 1
        has_target = me > 0
        target = me - 1

    @pl.when(jnp.logical_not(has_source))
    def _():
        recv_ref[...] = jnp.zeros(recv_ref.shape, jnp.float32)

    barrier_with_neighbours(me, length)

    def copy_of(k):
        return pltpu.make_async_remote_copy(
            src_ref=send_ref.at[k],
            dst_ref=recv_ref.at[k],
            send_sem=send_sem.at[k],
            recv_sem=recv_sem.at[k],
            device_id={"stream": target},
            device_id_type=pl.DeviceIdType.MESH,
        )

    row_order = list(range(rows)) if direction > 0 else list(range(rows - 1, -1, -1))

    def gathered(ref, row, first, cols):
        return jnp.concatenate([ref[row, first + tracer, :, cols] for tracer in range(grouped)], axis=1)

    def lanes(ref, row, cols):
        return jnp.concatenate([ref[pl.ds(row, 1), cols]] * grouped, axis=1)

    def block_step(k, carry):
        first = (k % sets) * grouped
        cols = pl.ds(pl.multiple_of((k // sets) * width, width), width)

        @pl.when(has_source)
        def _():
            copy_of(k).wait_recv()

        state = recv_ref[k]
        for row in row_order:
            types = lanes(types_ref, row, cols)
            coeff = lanes(coeff_ref, row, cols)
            if direction > 0:
                state = gathered(start_ref, row, first, cols) - coeff * kernel_typed(table_ref, types, state)
                solved = state
            else:
                solved = gathered(start_ref, row, first, cols) - state / lanes(denom_ref, row, cols)
                state = coeff * kernel_typed(table_ref, types, solved)
            for tracer in range(grouped):
                out_ref[row, first + tracer, :, cols] = solved[:, tracer * width:(tracer + 1) * width]
        send_ref[k] = state

        @pl.when(has_target)
        def _():
            copy_of(k).start()

        return carry

    lax.fori_loop(0, blocks, block_step, 0)

    def drain(k, carry):
        copy_of(k).wait_send()
        return carry

    @pl.when(has_target)
    def _():
        lax.fori_loop(0, blocks, drain, 0)


def sweep(direction, collective_id, width, grouped, start, types, coeff, denom, table):
    rows, tracers, dof, columns = start.shape
    blocks = (tracers // grouped) * (columns // width)
    length = lax.axis_size("stream")
    vmem = pltpu.VMEM
    return pl.pallas_call(
        functools.partial(sweep_kernel, length, direction, width, grouped),
        out_shape=jax.ShapeDtypeStruct(start.shape, jnp.float32),
        in_specs=[pl.BlockSpec(memory_space=vmem)] * 5,
        out_specs=pl.BlockSpec(memory_space=vmem),
        scratch_shapes=[
            pltpu.VMEM((blocks, dof, grouped * width), jnp.float32),
            pltpu.VMEM((blocks, dof, grouped * width), jnp.float32),
            pltpu.SemaphoreType.DMA((blocks,)),
            pltpu.SemaphoreType.DMA((blocks,)),
        ],
        compiler_params=pltpu.CompilerParams(
            collective_id=collective_id, has_side_effects=True, vmem_limit_bytes=60 * 1024 * 1024
        ),
    )(start, types, coeff, denom, table)


def per_device(
    rhs, lagged, face_types, stream_scale, span_scale, absorb, up_blocks, down_blocks, diag_inverse
):
    columns = rhs.shape[3]
    dof = up_blocks.shape[1]
    padded = padded_2(lagged, (("span", 3),), 1)
    denominator = stream_scale + span_scale[0] + span_scale[1] + absorb
    span_terms = span_block(padded, face_types, span_scale, up_blocks, 0, columns)
    start = jnp.einsum("pq,nrqc->nrpc", diag_inverse, rhs - span_terms, precision=fast)
    start = start / denominator[:, None, None, :]
    coeff = stream_scale / denominator
    up_table = split_table(jnp.einsum("pq,tqs->tps", diag_inverse, up_blocks, precision=precise).reshape(-1, dof))
    down_table = split_table(jnp.einsum("pq,tqs->tps", diag_inverse, down_blocks, precision=precise).reshape(-1, dof))
    width = LANES
    grouped = 1
    forward_part = sweep(1, 0, width, grouped, start, face_types[0], coeff, denominator, up_table)
    increment = sweep(-1, 1, width, grouped, forward_part, face_types[0], stream_scale, denominator, down_table)
    return increment


def solution(mesh):
    return jax.shard_map(
        per_device,
        mesh=mesh,
        in_specs=(
            P("stream", None, None, "span"),
            P("stream", None, None, "span"),
            P(None, "stream", "span"),
            P("stream", "span"),
            P(None, "stream", "span"),
            P("stream", "span"),
            P(),
            P(),
            P(),
        ),
        out_specs=P("stream", None, None, "span"),
        check_vma=False,
    )
```

```python
import functools

import jax
import jax.numpy as jnp
from jax import lax
from jax.experimental import pallas as pl
from jax.experimental.pallas import tpu as pltpu
from jax.sharding import PartitionSpec as P

precise = lax.Precision.HIGHEST
fast = lax.Precision.HIGH
LANES = 128


def padded_2(block, sides, width):
    for axis, dim in sides:
        count = lax.axis_size(axis)
        forward = [(i, i + 1) for i in range(count - 1)]
        backward = [(target, source) for source, target in forward]
        low = lax.ppermute(
            lax.slice_in_dim(block, block.shape[dim] - width, None, axis=dim), axis, forward
        )
        high = lax.ppermute(lax.slice_in_dim(block, 0, width, axis=dim), axis, backward)
        block = jnp.concatenate([low, block, high], axis=dim)
    return block


def typed_product(blocks_table, type_ids, state_in):
    products = jnp.einsum("tpq,rqw->trpw", blocks_table, state_in, precision=fast)
    kinds = jnp.arange(blocks_table.shape[0], dtype=jnp.int32)
    selector = (type_ids[None, :] == kinds[:, None]).astype(jnp.float32)
    return jnp.sum(products * selector[:, None, None, :], axis=0)


def span_block(padded, face_types, span_scale, up_blocks, offset, breadth):
    lower_side = lax.dynamic_slice_in_dim(padded, offset, breadth, 3)
    upper_side = lax.dynamic_slice_in_dim(padded, offset + 2, breadth, 3)
    lower_types = face_types[1]
    upper_types = face_types[2]
    lower_scale = span_scale[0]
    upper_scale = span_scale[1]
    results = []
    for row_index in range(padded.shape[0]):
        lower_term = lower_scale[row_index] * typed_product(
            up_blocks, lower_types[row_index], lower_side[row_index]
        )
        upper_term = upper_scale[row_index] * typed_product(
            up_blocks, upper_types[row_index], upper_side[row_index]
        )
        results.append(lower_term + upper_term)
    return jnp.stack(results)


def split_table(table):
    high = lax.reduce_precision(table, exponent_bits=8, mantissa_bits=7)
    low = table - high
    high = high.astype(jnp.bfloat16)
    low = low.astype(jnp.bfloat16)
    return jnp.concatenate([high, low, high], axis=1)


def kernel_typed(table_ref, types, state):
    dof = state.shape[0]
    high = state.astype(jnp.bfloat16)
    low = (state - high.astype(jnp.float32)).astype(jnp.bfloat16)
    stacked = jnp.concatenate([high, high, low], axis=0)
    products = jnp.dot(table_ref[...], stacked, preferred_element_type=jnp.float32)
    picked = products[0:dof]
    for kind in range(1, table_ref.shape[0] // dof):
        picked = jnp.where(types == kind, products[kind * dof:(kind + 1) * dof], picked)
    return picked


def barrier_with_neighbours(me, length):
    barrier = pltpu.get_barrier_semaphore()

    @pl.when(me > 0)
    def _():
        pl.semaphore_signal(barrier, inc=1, device_id={"stream": me - 1},
                            device_id_type=pl.DeviceIdType.MESH)

    @pl.when(me < length - 1)
    def _():
        pl.semaphore_signal(barrier, inc=1, device_id={"stream": me + 1},
                            device_id_type=pl.DeviceIdType.MESH)

    ends = jnp.logical_or(me == 0, me == length - 1)

    @pl.when(ends)
    def _():
        pl.semaphore_wait(barrier, 1)

    @pl.when(jnp.logical_not(ends))
    def _():
        pl.semaphore_wait(barrier, 2)


def sweep_kernel(length, direction, width, grouped, start_ref, types_ref, coeff_ref, denom_ref, table_ref,
                 out_ref, recv_ref, send_ref, send_sem, recv_sem):
    me = lax.axis_index("stream")
    rows, tracers, dof, columns = start_ref.shape
    sets = tracers // grouped
    blocks = sets * (columns // width)
    if direction > 0:
        has_source = me > 0
        has_target = me < length - 1
        target = me + 1
    else:
        has_source = me < length - 1
        has_target = me > 0
        target = me - 1

    @pl.when(jnp.logical_not(has_source))
    def _():
        recv_ref[...] = jnp.zeros(recv_ref.shape, jnp.float32)

    barrier_with_neighbours(me, length)

    def copy_of(k):
        return pltpu.make_async_remote_copy(
            src_ref=send_ref.at[k],
            dst_ref=recv_ref.at[k],
            send_sem=send_sem.at[k],
            recv_sem=recv_sem.at[k],
            device_id={"stream": target},
            device_id_type=pl.DeviceIdType.MESH,
        )

    row_order = list(range(rows)) if direction > 0 else list(range(rows - 1, -1, -1))

    def gathered(ref, row, first, cols):
        return jnp.concatenate([ref[row, first + tracer, :, cols] for tracer in range(grouped)], axis=1)

    def lanes(ref, row, cols):
        return jnp.concatenate([ref[pl.ds(row, 1), cols]] * grouped, axis=1)

    def block_step(k, carry):
        first = (k % sets) * grouped
        cols = pl.ds(pl.multiple_of((k // sets) * width, width), width)

        @pl.when(has_source)
        def _():
            copy_of(k).wait_recv()

        state = recv_ref[k]
        for row in row_order:
            types = lanes(types_ref, row, cols)
            coeff = lanes(coeff_ref, row, cols)
            if direction > 0:
                state = gathered(start_ref, row, first, cols) - coeff * kernel_typed(table_ref, types, state)
                solved = state
            else:
                solved = gathered(start_ref, row, first, cols) - state / lanes(denom_ref, row, cols)
                state = coeff * kernel_typed(table_ref, types, solved)
            for tracer in range(grouped):
                out_ref[row, first + tracer, :, cols] = solved[:, tracer * width:(tracer + 1) * width]
        send_ref[k] = state

        @pl.when(has_target)
        def _():
            copy_of(k).start()

        return carry

    lax.fori_loop(0, blocks, block_step, 0)

    def drain(k, carry):
        copy_of(k).wait_send()
        return carry

    @pl.when(has_target)
    def _():
        lax.fori_loop(0, blocks, drain, 0)


def sweep(direction, collective_id, width, grouped, start, types, coeff, denom, table):
    rows, tracers, dof, columns = start.shape
    blocks = (tracers // grouped) * (columns // width)
    length = lax.axis_size("stream")
    vmem = pltpu.VMEM
    return pl.pallas_call(
        functools.partial(sweep_kernel, length, direction, width, grouped),
        out_shape=jax.ShapeDtypeStruct(start.shape, jnp.float32),
        in_specs=[pl.BlockSpec(memory_space=vmem)] * 5,
        out_specs=pl.BlockSpec(memory_space=vmem),
        scratch_shapes=[
            pltpu.VMEM((blocks, dof, grouped * width), jnp.float32),
            pltpu.VMEM((blocks, dof, grouped * width), jnp.float32),
            pltpu.SemaphoreType.DMA((blocks,)),
            pltpu.SemaphoreType.DMA((blocks,)),
        ],
        compiler_params=pltpu.CompilerParams(
            collective_id=collective_id, has_side_effects=True, vmem_limit_bytes=60 * 1024 * 1024
        ),
    )(start, types, coeff, denom, table)


def both_kernel(length, width, start_ref, types_ref, coeff_ref, scale_ref, inverse_ref, up_ref, down_ref,
                out_ref, part_ref, recv_f, send_f, recv_b, send_b, sems):
    me = lax.axis_index("stream")
    rows, tracers, dof, columns = start_ref.shape
    sets = tracers
    blocks = sets * (columns // width)
    first_dev = me == 0
    last_dev = me == length - 1

    @pl.when(first_dev)
    def _():
        recv_f[...] = jnp.zeros(recv_f.shape, jnp.float32)

    @pl.when(last_dev)
    def _():
        recv_b[...] = jnp.zeros(recv_b.shape, jnp.float32)

    barrier_with_neighbours(me, length)

    def copy_f(k):
        return pltpu.make_async_remote_copy(
            src_ref=send_f.at[k], dst_ref=recv_f.at[k], send_sem=sems.at[0, k], recv_sem=sems.at[1, k],
            device_id={"stream": me + 1}, device_id_type=pl.DeviceIdType.MESH)

    def copy_b(k):
        return pltpu.make_async_remote_copy(
            src_ref=send_b.at[k], dst_ref=recv_b.at[k], send_sem=sems.at[2, k], recv_sem=sems.at[3, k],
            device_id={"stream": me - 1}, device_id_type=pl.DeviceIdType.MESH)

    def place(k):
        tracer = k % sets
        cols = pl.ds(pl.multiple_of((k // sets) * width, width), width)
        return tracer, cols

    def forward_block(k):
        tracer, cols = place(k)

        @pl.when(jnp.logical_not(first_dev))
        def _():
            copy_f(k).wait_recv()

        state = recv_f[k]
        for row in range(rows):
            types = types_ref[pl.ds(row, 1), cols]
            coeff = coeff_ref[pl.ds(row, 1), cols]
            state = start_ref[row, tracer, :, cols] - coeff * kernel_typed(up_ref, types, state)
            part_ref[row, tracer, :, cols] = state
        send_f[k] = state

        @pl.when(jnp.logical_not(last_dev))
        def _():
            copy_f(k).start()

    def backward_block(k):
        tracer, cols = place(k)

        @pl.when(jnp.logical_not(last_dev))
        def _():
            copy_b(k).wait_recv()

        state = recv_b[k]
        for row in range(rows - 1, -1, -1):
            types = types_ref[pl.ds(row, 1), cols]
            scale = scale_ref[pl.ds(row, 1), cols]
            solved = part_ref[row, tracer, :, cols] - state * inverse_ref[pl.ds(row, 1), cols]
            out_ref[row, tracer, :, cols] = solved
            state = scale * kernel_typed(down_ref, types, solved)
        send_b[k] = state

        @pl.when(jnp.logical_not(first_dev))
        def _():
            copy_b(k).start()

    lead = jnp.minimum(jnp.maximum(((2 * (length - 1) - 2 * me) * 17) // 6, 1), blocks)
    tail = 2 * blocks - lead

    def step(s, carry):
        paired = jnp.logical_and(s >= lead, s < tail)
        odd = (s - lead) % 2 == 1

        @pl.when(s < lead)
        def _():
            forward_block(s)

        @pl.when(jnp.logical_and(paired, odd))
        def _():
            forward_block(lead + (s - lead) // 2)

        @pl.when(jnp.logical_and(paired, jnp.logical_not(odd)))
        def _():
            backward_block((s - lead) // 2)

        @pl.when(s >= tail)
        def _():
            backward_block(s - blocks)

        return carry

    lax.fori_loop(0, 2 * blocks, step, 0)

    def drain_f(k, carry):
        copy_f(k).wait_send()
        return carry

    def drain_b(k, carry):
        copy_b(k).wait_send()
        return carry

    @pl.when(jnp.logical_not(last_dev))
    def _():
        lax.fori_loop(0, blocks, drain_f, 0)

    @pl.when(jnp.logical_not(first_dev))
    def _():
        lax.fori_loop(0, blocks, drain_b, 0)


def both_sweeps(width, start, types, coeff, scale, inverse, up_table, down_table):
    rows, tracers, dof, columns = start.shape
    blocks = tracers * (columns // width)
    length = lax.axis_size("stream")
    vmem = pltpu.VMEM
    return pl.pallas_call(
        functools.partial(both_kernel, length, width),
        out_shape=jax.ShapeDtypeStruct(start.shape, jnp.float32),
        in_specs=[pl.BlockSpec(memory_space=vmem)] * 7,
        out_specs=pl.BlockSpec(memory_space=vmem),
        scratch_shapes=[
            pltpu.VMEM(start.shape, jnp.float32),
            pltpu.VMEM((blocks, dof, width), jnp.float32),
            pltpu.VMEM((blocks, dof, width), jnp.float32),
            pltpu.VMEM((blocks, dof, width), jnp.float32),
            pltpu.VMEM((blocks, dof, width), jnp.float32),
            pltpu.SemaphoreType.DMA((4, blocks)),
        ],
        compiler_params=pltpu.CompilerParams(
            collective_id=0, has_side_effects=True, vmem_limit_bytes=60 * 1024 * 1024
        ),
    )(start, types, coeff, scale, inverse, up_table, down_table)


def per_device(
    rhs, lagged, face_types, stream_scale, span_scale, absorb, up_blocks, down_blocks, diag_inverse
):
    columns = rhs.shape[3]
    dof = up_blocks.shape[1]
    padded = padded_2(lagged, (("span", 3),), 1)
    denominator = stream_scale + span_scale[0] + span_scale[1] + absorb
    span_terms = span_block(padded, face_types, span_scale, up_blocks, 0, columns)
    start = jnp.einsum("pq,nrqc->nrpc", diag_inverse, rhs - span_terms, precision=fast)
    start = start / denominator[:, None, None, :]
    coeff = stream_scale / denominator
    inverse = 1.0 / denominator
    up_table = split_table(jnp.einsum("pq,tqs->tps", diag_inverse, up_blocks, precision=precise).reshape(-1, dof))
    down_table = split_table(jnp.einsum("pq,tqs->tps", diag_inverse, down_blocks, precision=precise).reshape(-1, dof))
    return both_sweeps(LANES, start, face_types[0], coeff, stream_scale, inverse, up_table, down_table)


def solution(mesh):
    return jax.shard_map(
        per_device,
        mesh=mesh,
        in_specs=(
            P("stream", None, None, "span"),
            P("stream", None, None, "span"),
            P(None, "stream", "span"),
            P("stream", "span"),
            P(None, "stream", "span"),
            P("stream", "span"),
            P(),
            P(),
            P(),
        ),
        out_specs=P("stream", None, None, "span"),
        check_vma=False,
    )
```

```python
import functools

import jax
import jax.numpy as jnp
from jax import lax
from jax.experimental import pallas as pl
from jax.experimental.pallas import tpu as pltpu
from jax.sharding import PartitionSpec as P

precise = lax.Precision.HIGHEST
fast = lax.Precision.HIGH
LANES = 128


def padded_2(block, sides, width):
    for axis, dim in sides:
        count = lax.axis_size(axis)
        forward = [(i, i + 1) for i in range(count - 1)]
        backward = [(target, source) for source, target in forward]
        low = lax.ppermute(
            lax.slice_in_dim(block, block.shape[dim] - width, None, axis=dim), axis, forward
        )
        high = lax.ppermute(lax.slice_in_dim(block, 0, width, axis=dim), axis, backward)
        block = jnp.concatenate([low, block, high], axis=dim)
    return block


def typed_product(blocks_table, type_ids, state_in):
    products = jnp.einsum("tpq,rqw->trpw", blocks_table, state_in, precision=fast)
    kinds = jnp.arange(blocks_table.shape[0], dtype=jnp.int32)
    selector = (type_ids[None, :] == kinds[:, None]).astype(jnp.float32)
    return jnp.sum(products * selector[:, None, None, :], axis=0)


def span_block(padded, face_types, span_scale, up_blocks, offset, breadth):
    lower_side = lax.dynamic_slice_in_dim(padded, offset, breadth, 3)
    upper_side = lax.dynamic_slice_in_dim(padded, offset + 2, breadth, 3)
    lower_types = face_types[1]
    upper_types = face_types[2]
    lower_scale = span_scale[0]
    upper_scale = span_scale[1]
    results = []
    for row_index in range(padded.shape[0]):
        lower_term = lower_scale[row_index] * typed_product(
            up_blocks, lower_types[row_index], lower_side[row_index]
        )
        upper_term = upper_scale[row_index] * typed_product(
            up_blocks, upper_types[row_index], upper_side[row_index]
        )
        results.append(lower_term + upper_term)
    return jnp.stack(results)


def split_table(table):
    high = lax.reduce_precision(table, exponent_bits=8, mantissa_bits=7)
    low = table - high
    high = high.astype(jnp.bfloat16)
    low = low.astype(jnp.bfloat16)
    return jnp.concatenate([high, low, high], axis=1)


def kernel_typed(table_ref, types, state):
    dof = state.shape[0]
    high = state.astype(jnp.bfloat16)
    low = (state - high.astype(jnp.float32)).astype(jnp.bfloat16)
    stacked = jnp.concatenate([high, high, low], axis=0)
    products = jnp.dot(table_ref[...], stacked, preferred_element_type=jnp.float32)
    picked = products[0:dof]
    for kind in range(1, table_ref.shape[0] // dof):
        picked = jnp.where(types == kind, products[kind * dof:(kind + 1) * dof], picked)
    return picked


def barrier_with_neighbours(me, length):
    barrier = pltpu.get_barrier_semaphore()

    @pl.when(me > 0)
    def _():
        pl.semaphore_signal(barrier, inc=1, device_id={"stream": me - 1},
                            device_id_type=pl.DeviceIdType.MESH)

    @pl.when(me < length - 1)
    def _():
        pl.semaphore_signal(barrier, inc=1, device_id={"stream": me + 1},
                            device_id_type=pl.DeviceIdType.MESH)

    ends = jnp.logical_or(me == 0, me == length - 1)

    @pl.when(ends)
    def _():
        pl.semaphore_wait(barrier, 1)

    @pl.when(jnp.logical_not(ends))
    def _():
        pl.semaphore_wait(barrier, 2)


def sweep_kernel(length, direction, width, grouped, start_ref, types_ref, coeff_ref, denom_ref, table_ref,
                 out_ref, recv_ref, send_ref, send_sem, recv_sem):
    me = lax.axis_index("stream")
    rows, tracers, dof, columns = start_ref.shape
    sets = tracers // grouped
    blocks = sets * (columns // width)
    if direction > 0:
        has_source = me > 0
        has_target = me < length - 1
        target = me + 1
    else:
        has_source = me < length - 1
        has_target = me > 0
        target = me - 1

    @pl.when(jnp.logical_not(has_source))
    def _():
        recv_ref[...] = jnp.zeros(recv_ref.shape, jnp.float32)

    barrier_with_neighbours(me, length)

    def copy_of(k):
        return pltpu.make_async_remote_copy(
            src_ref=send_ref.at[k],
            dst_ref=recv_ref.at[k],
            send_sem=send_sem.at[k],
            recv_sem=recv_sem.at[k],
            device_id={"stream": target},
            device_id_type=pl.DeviceIdType.MESH,
        )

    row_order = list(range(rows)) if direction > 0 else list(range(rows - 1, -1, -1))

    def gathered(ref, row, first, cols):
        return jnp.concatenate([ref[row, first + tracer, :, cols] for tracer in range(grouped)], axis=1)

    def lanes(ref, row, cols):
        return jnp.concatenate([ref[pl.ds(row, 1), cols]] * grouped, axis=1)

    def block_step(k, carry):
        first = (k % sets) * grouped
        cols = pl.ds(pl.multiple_of((k // sets) * width, width), width)

        @pl.when(has_source)
        def _():
            copy_of(k).wait_recv()

        state = recv_ref[k]
        for row in row_order:
            types = lanes(types_ref, row, cols)
            coeff = lanes(coeff_ref, row, cols)
            if direction > 0:
                state = gathered(start_ref, row, first, cols) - coeff * kernel_typed(table_ref, types, state)
                solved = state
            else:
                solved = gathered(start_ref, row, first, cols) - state / lanes(denom_ref, row, cols)
                state = coeff * kernel_typed(table_ref, types, solved)
            for tracer in range(grouped):
                out_ref[row, first + tracer, :, cols] = solved[:, tracer * width:(tracer + 1) * width]
        send_ref[k] = state

        @pl.when(has_target)
        def _():
            copy_of(k).start()

        return carry

    lax.fori_loop(0, blocks, block_step, 0)

    def drain(k, carry):
        copy_of(k).wait_send()
        return carry

    @pl.when(has_target)
    def _():
        lax.fori_loop(0, blocks, drain, 0)


def sweep(direction, collective_id, width, grouped, start, types, coeff, denom, table):
    rows, tracers, dof, columns = start.shape
    blocks = (tracers // grouped) * (columns // width)
    length = lax.axis_size("stream")
    vmem = pltpu.VMEM
    return pl.pallas_call(
        functools.partial(sweep_kernel, length, direction, width, grouped),
        out_shape=jax.ShapeDtypeStruct(start.shape, jnp.float32),
        in_specs=[pl.BlockSpec(memory_space=vmem)] * 5,
        out_specs=pl.BlockSpec(memory_space=vmem),
        scratch_shapes=[
            pltpu.VMEM((blocks, dof, grouped * width), jnp.float32),
            pltpu.VMEM((blocks, dof, grouped * width), jnp.float32),
            pltpu.SemaphoreType.DMA((blocks,)),
            pltpu.SemaphoreType.DMA((blocks,)),
        ],
        compiler_params=pltpu.CompilerParams(
            collective_id=collective_id, has_side_effects=True, vmem_limit_bytes=60 * 1024 * 1024
        ),
    )(start, types, coeff, denom, table)


def both_kernel(length, width, start_ref, types_ref, coeff_ref, scale_ref, inverse_ref, up_ref, down_ref,
                out_ref, part_ref, recv_f, send_f, recv_b, send_b, sems):
    me = lax.axis_index("stream")
    rows, tracers, dof, columns = start_ref.shape
    sets = tracers
    blocks = sets * (columns // width)
    first_dev = me == 0
    last_dev = me == length - 1

    @pl.when(first_dev)
    def _():
        recv_f[...] = jnp.zeros(recv_f.shape, jnp.float32)

    @pl.when(last_dev)
    def _():
        recv_b[...] = jnp.zeros(recv_b.shape, jnp.float32)

    barrier_with_neighbours(me, length)

    def copy_f(k):
        return pltpu.make_async_remote_copy(
            src_ref=send_f.at[k], dst_ref=recv_f.at[k], send_sem=sems.at[0, k], recv_sem=sems.at[1, k],
            device_id={"stream": me + 1}, device_id_type=pl.DeviceIdType.MESH)

    def copy_b(k):
        return pltpu.make_async_remote_copy(
            src_ref=send_b.at[k], dst_ref=recv_b.at[k], send_sem=sems.at[2, k], recv_sem=sems.at[3, k],
            device_id={"stream": me - 1}, device_id_type=pl.DeviceIdType.MESH)

    def place(k):
        tracer = k % sets
        cols = pl.ds(pl.multiple_of((k // sets) * width, width), width)
        return tracer, cols

    def forward_block(k):
        tracer, cols = place(k)

        @pl.when(jnp.logical_not(first_dev))
        def _():
            copy_f(k).wait_recv()

        state = recv_f[k]
        for row in range(rows):
            types = types_ref[pl.ds(row, 1), cols]
            coeff = coeff_ref[pl.ds(row, 1), cols]
            state = start_ref[row, tracer, :, cols] - coeff * kernel_typed(up_ref, types, state)
            part_ref[row, tracer, :, cols] = state
        send_f[k] = state

        @pl.when(jnp.logical_not(last_dev))
        def _():
            copy_f(k).start()

    def backward_block(k):
        tracer, cols = place(k)

        @pl.when(jnp.logical_not(last_dev))
        def _():
            copy_b(k).wait_recv()

        state = recv_b[k]
        for row in range(rows - 1, -1, -1):
            types = types_ref[pl.ds(row, 1), cols]
            scale = scale_ref[pl.ds(row, 1), cols]
            solved = part_ref[row, tracer, :, cols] - state * inverse_ref[pl.ds(row, 1), cols]
            out_ref[row, tracer, :, cols] = solved
            state = scale * kernel_typed(down_ref, types, solved)
        send_b[k] = state

        @pl.when(jnp.logical_not(first_dev))
        def _():
            copy_b(k).start()

    lead = jnp.minimum(jnp.maximum(((2 * (length - 1) - 2 * me) * 17) // 6, 1), blocks)
    tail = 2 * blocks - lead

    def step(s, carry):
        paired = jnp.logical_and(s >= lead, s < tail)
        odd = (s - lead) % 2 == 1

        @pl.when(s < lead)
        def _():
            forward_block(s)

        @pl.when(jnp.logical_and(paired, odd))
        def _():
            forward_block(lead + (s - lead) // 2)

        @pl.when(jnp.logical_and(paired, jnp.logical_not(odd)))
        def _():
            backward_block((s - lead) // 2)

        @pl.when(s >= tail)
        def _():
            backward_block(s - blocks)

        return carry

    lax.fori_loop(0, 2 * blocks, step, 0)

    def drain_f(k, carry):
        copy_f(k).wait_send()
        return carry

    def drain_b(k, carry):
        copy_b(k).wait_send()
        return carry

    @pl.when(jnp.logical_not(last_dev))
    def _():
        lax.fori_loop(0, blocks, drain_f, 0)

    @pl.when(jnp.logical_not(first_dev))
    def _():
        lax.fori_loop(0, blocks, drain_b, 0)


def both_sweeps(width, start, types, coeff, scale, inverse, up_table, down_table):
    rows, tracers, dof, columns = start.shape
    blocks = tracers * (columns // width)
    length = lax.axis_size("stream")
    vmem = pltpu.VMEM
    return pl.pallas_call(
        functools.partial(both_kernel, length, width),
        out_shape=jax.ShapeDtypeStruct(start.shape, jnp.float32),
        in_specs=[pl.BlockSpec(memory_space=vmem)] * 7,
        out_specs=pl.BlockSpec(memory_space=vmem),
        scratch_shapes=[
            pltpu.VMEM(start.shape, jnp.float32),
            pltpu.VMEM((blocks, dof, width), jnp.float32),
            pltpu.VMEM((blocks, dof, width), jnp.float32),
            pltpu.VMEM((blocks, dof, width), jnp.float32),
            pltpu.VMEM((blocks, dof, width), jnp.float32),
            pltpu.SemaphoreType.DMA((4, blocks)),
        ],
        compiler_params=pltpu.CompilerParams(
            collective_id=0, has_side_effects=True, vmem_limit_bytes=60 * 1024 * 1024
        ),
    )(start, types, coeff, scale, inverse, up_table, down_table)


def per_device(
    rhs, lagged, face_types, stream_scale, span_scale, absorb, up_blocks, down_blocks, diag_inverse
):
    columns = rhs.shape[3]
    dof = up_blocks.shape[1]
    padded = padded_2(lagged, (("span", 3),), 1)
    denominator = stream_scale + span_scale[0] + span_scale[1] + absorb
    kinds = up_blocks.shape[0]
    lower_side = padded[..., : columns] * span_scale[0][:, None, None, :]
    upper_side = padded[..., 2:] * span_scale[1][:, None, None, :]
    lower_types = face_types[1][:, None, None, :]
    upper_types = face_types[2][:, None, None, :]
    faces = [
        jnp.where(lower_types == kind, lower_side, 0.0) + jnp.where(upper_types == kind, upper_side, 0.0)
        for kind in range(kinds)
    ]
    stacked = jnp.concatenate([rhs] + [-face for face in faces], axis=2)
    tables = jnp.einsum("pq,tqs->tps", diag_inverse, up_blocks, precision=precise)
    combined = jnp.concatenate([diag_inverse] + [tables[kind] for kind in range(kinds)], axis=1)
    start = jnp.einsum("pk,nrkc->nrpc", combined, stacked, precision=fast)
    start = start / denominator[:, None, None, :]
    coeff = stream_scale / denominator
    inverse = 1.0 / denominator
    up_table = split_table(jnp.einsum("pq,tqs->tps", diag_inverse, up_blocks, precision=precise).reshape(-1, dof))
    down_table = split_table(jnp.einsum("pq,tqs->tps", diag_inverse, down_blocks, precision=precise).reshape(-1, dof))
    return both_sweeps(LANES, start, face_types[0], coeff, stream_scale, inverse, up_table, down_table)


def solution(mesh):
    return jax.shard_map(
        per_device,
        mesh=mesh,
        in_specs=(
            P("stream", None, None, "span"),
            P("stream", None, None, "span"),
            P(None, "stream", "span"),
            P("stream", "span"),
            P(None, "stream", "span"),
            P("stream", "span"),
            P(),
            P(),
            P(),
        ),
        out_specs=P("stream", None, None, "span"),
        check_vma=False,
    )
```

```python
import functools

import jax
import jax.numpy as jnp
from jax import lax
from jax.experimental import pallas as pl
from jax.experimental.pallas import tpu as pltpu
from jax.sharding import PartitionSpec as P

precise = lax.Precision.HIGHEST
fast = lax.Precision.HIGH
LANES = 128


def padded_2(block, sides, width):
    for axis, dim in sides:
        count = lax.axis_size(axis)
        forward = [(i, i + 1) for i in range(count - 1)]
        backward = [(target, source) for source, target in forward]
        low = lax.ppermute(
            lax.slice_in_dim(block, block.shape[dim] - width, None, axis=dim), axis, forward
        )
        high = lax.ppermute(lax.slice_in_dim(block, 0, width, axis=dim), axis, backward)
        block = jnp.concatenate([low, block, high], axis=dim)
    return block


def typed_product(blocks_table, type_ids, state_in):
    products = jnp.einsum("tpq,rqw->trpw", blocks_table, state_in, precision=fast)
    kinds = jnp.arange(blocks_table.shape[0], dtype=jnp.int32)
    selector = (type_ids[None, :] == kinds[:, None]).astype(jnp.float32)
    return jnp.sum(products * selector[:, None, None, :], axis=0)


def span_block(padded, face_types, span_scale, up_blocks, offset, breadth):
    lower_side = lax.dynamic_slice_in_dim(padded, offset, breadth, 3)
    upper_side = lax.dynamic_slice_in_dim(padded, offset + 2, breadth, 3)
    lower_types = face_types[1]
    upper_types = face_types[2]
    lower_scale = span_scale[0]
    upper_scale = span_scale[1]
    results = []
    for row_index in range(padded.shape[0]):
        lower_term = lower_scale[row_index] * typed_product(
            up_blocks, lower_types[row_index], lower_side[row_index]
        )
        upper_term = upper_scale[row_index] * typed_product(
            up_blocks, upper_types[row_index], upper_side[row_index]
        )
        results.append(lower_term + upper_term)
    return jnp.stack(results)


def split_table(table):
    high = lax.reduce_precision(table, exponent_bits=8, mantissa_bits=7)
    low = table - high
    high = high.astype(jnp.bfloat16)
    low = low.astype(jnp.bfloat16)
    return jnp.concatenate([high, low, high], axis=1)


def split_masked_table(tables):
    kinds, dof, _ = tables.shape
    flat = jnp.transpose(tables, (1, 0, 2)).reshape(dof, kinds * dof)
    high = lax.reduce_precision(flat, exponent_bits=8, mantissa_bits=7)
    low = flat - high
    high = high.astype(jnp.bfloat16)
    low = low.astype(jnp.bfloat16)
    return jnp.concatenate([high, low, high], axis=1)


def kernel_masked(table_ref, types, state):
    dof = state.shape[0]
    kinds = table_ref.shape[1] // (3 * dof)
    high = state.astype(jnp.bfloat16)
    low = (state - high.astype(jnp.float32)).astype(jnp.bfloat16)
    zero = jnp.zeros_like(high)
    masks = [types == kind for kind in range(kinds)]
    highs = [jnp.where(mask, high, zero) for mask in masks]
    lows = [jnp.where(mask, low, zero) for mask in masks]
    stacked = jnp.concatenate(highs + highs + lows, axis=0)
    return jnp.dot(table_ref[...], stacked, preferred_element_type=jnp.float32)


def kernel_typed(table_ref, types, state):
    dof = state.shape[0]
    high = state.astype(jnp.bfloat16)
    low = (state - high.astype(jnp.float32)).astype(jnp.bfloat16)
    stacked = jnp.concatenate([high, high, low], axis=0)
    products = jnp.dot(table_ref[...], stacked, preferred_element_type=jnp.float32)
    picked = products[0:dof]
    for kind in range(1, table_ref.shape[0] // dof):
        picked = jnp.where(types == kind, products[kind * dof:(kind + 1) * dof], picked)
    return picked


def barrier_with_neighbours(me, length):
    barrier = pltpu.get_barrier_semaphore()

    @pl.when(me > 0)
    def _():
        pl.semaphore_signal(barrier, inc=1, device_id={"stream": me - 1},
                            device_id_type=pl.DeviceIdType.MESH)

    @pl.when(me < length - 1)
    def _():
        pl.semaphore_signal(barrier, inc=1, device_id={"stream": me + 1},
                            device_id_type=pl.DeviceIdType.MESH)

    ends = jnp.logical_or(me == 0, me == length - 1)

    @pl.when(ends)
    def _():
        pl.semaphore_wait(barrier, 1)

    @pl.when(jnp.logical_not(ends))
    def _():
        pl.semaphore_wait(barrier, 2)


def sweep_kernel(length, direction, width, grouped, start_ref, types_ref, coeff_ref, denom_ref, table_ref,
                 out_ref, recv_ref, send_ref, send_sem, recv_sem):
    me = lax.axis_index("stream")
    rows, tracers, dof, columns = start_ref.shape
    sets = tracers // grouped
    blocks = sets * (columns // width)
    if direction > 0:
        has_source = me > 0
        has_target = me < length - 1
        target = me + 1
    else:
        has_source = me < length - 1
        has_target = me > 0
        target = me - 1

    @pl.when(jnp.logical_not(has_source))
    def _():
        recv_ref[...] = jnp.zeros(recv_ref.shape, jnp.float32)

    barrier_with_neighbours(me, length)

    def copy_of(k):
        return pltpu.make_async_remote_copy(
            src_ref=send_ref.at[k],
            dst_ref=recv_ref.at[k],
            send_sem=send_sem.at[k],
            recv_sem=recv_sem.at[k],
            device_id={"stream": target},
            device_id_type=pl.DeviceIdType.MESH,
        )

    row_order = list(range(rows)) if direction > 0 else list(range(rows - 1, -1, -1))

    def gathered(ref, row, first, cols):
        return jnp.concatenate([ref[row, first + tracer, :, cols] for tracer in range(grouped)], axis=1)

    def lanes(ref, row, cols):
        return jnp.concatenate([ref[pl.ds(row, 1), cols]] * grouped, axis=1)

    def block_step(k, carry):
        first = (k % sets) * grouped
        cols = pl.ds(pl.multiple_of((k // sets) * width, width), width)

        @pl.when(has_source)
        def _():
            copy_of(k).wait_recv()

        state = recv_ref[k]
        for row in row_order:
            types = lanes(types_ref, row, cols)
            coeff = lanes(coeff_ref, row, cols)
            if direction > 0:
                state = gathered(start_ref, row, first, cols) - coeff * kernel_typed(table_ref, types, state)
                solved = state
            else:
                solved = gathered(start_ref, row, first, cols) - state / lanes(denom_ref, row, cols)
                state = coeff * kernel_typed(table_ref, types, solved)
            for tracer in range(grouped):
                out_ref[row, first + tracer, :, cols] = solved[:, tracer * width:(tracer + 1) * width]
        send_ref[k] = state

        @pl.when(has_target)
        def _():
            copy_of(k).start()

        return carry

    lax.fori_loop(0, blocks, block_step, 0)

    def drain(k, carry):
        copy_of(k).wait_send()
        return carry

    @pl.when(has_target)
    def _():
        lax.fori_loop(0, blocks, drain, 0)


def sweep(direction, collective_id, width, grouped, start, types, coeff, denom, table):
    rows, tracers, dof, columns = start.shape
    blocks = (tracers // grouped) * (columns // width)
    length = lax.axis_size("stream")
    vmem = pltpu.VMEM
    return pl.pallas_call(
        functools.partial(sweep_kernel, length, direction, width, grouped),
        out_shape=jax.ShapeDtypeStruct(start.shape, jnp.float32),
        in_specs=[pl.BlockSpec(memory_space=vmem)] * 5,
        out_specs=pl.BlockSpec(memory_space=vmem),
        scratch_shapes=[
            pltpu.VMEM((blocks, dof, grouped * width), jnp.float32),
            pltpu.VMEM((blocks, dof, grouped * width), jnp.float32),
            pltpu.SemaphoreType.DMA((blocks,)),
            pltpu.SemaphoreType.DMA((blocks,)),
        ],
        compiler_params=pltpu.CompilerParams(
            collective_id=collective_id, has_side_effects=True, vmem_limit_bytes=60 * 1024 * 1024
        ),
    )(start, types, coeff, denom, table)


def both_kernel(length, width, start_ref, types_ref, coeff_ref, scale_ref, inverse_ref, up_ref, down_ref,
                out_ref, part_ref, recv_f, send_f, recv_b, send_b, sems):
    me = lax.axis_index("stream")
    rows, tracers, dof, columns = start_ref.shape
    sets = tracers
    blocks = sets * (columns // width)
    first_dev = me == 0
    last_dev = me == length - 1

    @pl.when(first_dev)
    def _():
        recv_f[...] = jnp.zeros(recv_f.shape, jnp.float32)

    @pl.when(last_dev)
    def _():
        recv_b[...] = jnp.zeros(recv_b.shape, jnp.float32)

    barrier_with_neighbours(me, length)

    def copy_f(k):
        return pltpu.make_async_remote_copy(
            src_ref=send_f.at[k], dst_ref=recv_f.at[k], send_sem=sems.at[0, k], recv_sem=sems.at[1, k],
            device_id={"stream": me + 1}, device_id_type=pl.DeviceIdType.MESH)

    def copy_b(k):
        return pltpu.make_async_remote_copy(
            src_ref=send_b.at[k], dst_ref=recv_b.at[k], send_sem=sems.at[2, k], recv_sem=sems.at[3, k],
            device_id={"stream": me - 1}, device_id_type=pl.DeviceIdType.MESH)

    def place(k):
        tracer = k % sets
        cols = pl.ds(pl.multiple_of((k // sets) * width, width), width)
        return tracer, cols

    def forward_block(k):
        tracer, cols = place(k)

        @pl.when(jnp.logical_not(first_dev))
        def _():
            copy_f(k).wait_recv()

        state = recv_f[k]
        for row in range(rows):
            types = types_ref[pl.ds(row, 1), cols]
            coeff = coeff_ref[pl.ds(row, 1), cols]
            state = start_ref[row, tracer, :, cols] - coeff * kernel_masked(up_ref, types, state)
            part_ref[row, tracer, :, cols] = state
        send_f[k] = state

        @pl.when(jnp.logical_not(last_dev))
        def _():
            copy_f(k).start()

    def backward_block(k):
        tracer, cols = place(k)

        @pl.when(jnp.logical_not(last_dev))
        def _():
            copy_b(k).wait_recv()

        state = recv_b[k]
        for row in range(rows - 1, -1, -1):
            types = types_ref[pl.ds(row, 1), cols]
            scale = scale_ref[pl.ds(row, 1), cols]
            solved = part_ref[row, tracer, :, cols] - state * inverse_ref[pl.ds(row, 1), cols]
            out_ref[row, tracer, :, cols] = solved
            state = scale * kernel_masked(down_ref, types, solved)
        send_b[k] = state

        @pl.when(jnp.logical_not(first_dev))
        def _():
            copy_b(k).start()

    lead = jnp.minimum(jnp.maximum(((2 * (length - 1) - 2 * me) * 17) // 6, 1), blocks)
    tail = 2 * blocks - lead

    def step(s, carry):
        paired = jnp.logical_and(s >= lead, s < tail)
        odd = (s - lead) % 2 == 1

        @pl.when(s < lead)
        def _():
            forward_block(s)

        @pl.when(jnp.logical_and(paired, odd))
        def _():
            forward_block(lead + (s - lead) // 2)

        @pl.when(jnp.logical_and(paired, jnp.logical_not(odd)))
        def _():
            backward_block((s - lead) // 2)

        @pl.when(s >= tail)
        def _():
            backward_block(s - blocks)

        return carry

    lax.fori_loop(0, 2 * blocks, step, 0)

    def drain_f(k, carry):
        copy_f(k).wait_send()
        return carry

    def drain_b(k, carry):
        copy_b(k).wait_send()
        return carry

    @pl.when(jnp.logical_not(last_dev))
    def _():
        lax.fori_loop(0, blocks, drain_f, 0)

    @pl.when(jnp.logical_not(first_dev))
    def _():
        lax.fori_loop(0, blocks, drain_b, 0)


def both_sweeps(width, start, types, coeff, scale, inverse, up_table, down_table):
    rows, tracers, dof, columns = start.shape
    blocks = tracers * (columns // width)
    length = lax.axis_size("stream")
    vmem = pltpu.VMEM
    return pl.pallas_call(
        functools.partial(both_kernel, length, width),
        out_shape=jax.ShapeDtypeStruct(start.shape, jnp.float32),
        in_specs=[pl.BlockSpec(memory_space=vmem)] * 7,
        out_specs=pl.BlockSpec(memory_space=vmem),
        scratch_shapes=[
            pltpu.VMEM(start.shape, jnp.float32),
            pltpu.VMEM((blocks, dof, width), jnp.float32),
            pltpu.VMEM((blocks, dof, width), jnp.float32),
            pltpu.VMEM((blocks, dof, width), jnp.float32),
            pltpu.VMEM((blocks, dof, width), jnp.float32),
            pltpu.SemaphoreType.DMA((4, blocks)),
        ],
        compiler_params=pltpu.CompilerParams(
            collective_id=0, has_side_effects=True, vmem_limit_bytes=60 * 1024 * 1024
        ),
    )(start, types, coeff, scale, inverse, up_table, down_table)


def per_device(
    rhs, lagged, face_types, stream_scale, span_scale, absorb, up_blocks, down_blocks, diag_inverse
):
    columns = rhs.shape[3]
    dof = up_blocks.shape[1]
    padded = padded_2(lagged, (("span", 3),), 1)
    denominator = stream_scale + span_scale[0] + span_scale[1] + absorb
    span_terms = span_block(padded, face_types, span_scale, up_blocks, 0, columns)
    start = jnp.einsum("pq,nrqc->nrpc", diag_inverse, rhs - span_terms, precision=fast)
    start = start / denominator[:, None, None, :]
    coeff = stream_scale / denominator
    inverse = 1.0 / denominator
    up_table = split_masked_table(jnp.einsum("pq,tqs->tps", diag_inverse, up_blocks, precision=precise))
    down_table = split_masked_table(jnp.einsum("pq,tqs->tps", diag_inverse, down_blocks, precision=precise))
    return both_sweeps(LANES, start, face_types[0], coeff, stream_scale, inverse, up_table, down_table)


def solution(mesh):
    return jax.shard_map(
        per_device,
        mesh=mesh,
        in_specs=(
            P("stream", None, None, "span"),
            P("stream", None, None, "span"),
            P(None, "stream", "span"),
            P("stream", "span"),
            P(None, "stream", "span"),
            P("stream", "span"),
            P(),
            P(),
            P(),
        ),
        out_specs=P("stream", None, None, "span"),
        check_vma=False,
    )
```

```python
import functools

import jax
import jax.numpy as jnp
from jax import lax
from jax.experimental import pallas as pl
from jax.experimental.pallas import tpu as pltpu
from jax.sharding import PartitionSpec as P

precise = lax.Precision.HIGHEST
fast = lax.Precision.HIGH
LANES = 128


def padded_2(block, sides, width):
    for axis, dim in sides:
        count = lax.axis_size(axis)
        forward = [(i, i + 1) for i in range(count - 1)]
        backward = [(target, source) for source, target in forward]
        low = lax.ppermute(
            lax.slice_in_dim(block, block.shape[dim] - width, None, axis=dim), axis, forward
        )
        high = lax.ppermute(lax.slice_in_dim(block, 0, width, axis=dim), axis, backward)
        block = jnp.concatenate([low, block, high], axis=dim)
    return block


def typed_product(blocks_table, type_ids, state_in):
    products = jnp.einsum("tpq,rqw->trpw", blocks_table, state_in, precision=fast)
    kinds = jnp.arange(blocks_table.shape[0], dtype=jnp.int32)
    selector = (type_ids[None, :] == kinds[:, None]).astype(jnp.float32)
    return jnp.sum(products * selector[:, None, None, :], axis=0)


def span_block(padded, face_types, span_scale, up_blocks, offset, breadth):
    lower_side = lax.dynamic_slice_in_dim(padded, offset, breadth, 3)
    upper_side = lax.dynamic_slice_in_dim(padded, offset + 2, breadth, 3)
    lower_types = face_types[1]
    upper_types = face_types[2]
    lower_scale = span_scale[0]
    upper_scale = span_scale[1]
    results = []
    for row_index in range(padded.shape[0]):
        lower_term = lower_scale[row_index] * typed_product(
            up_blocks, lower_types[row_index], lower_side[row_index]
        )
        upper_term = upper_scale[row_index] * typed_product(
            up_blocks, upper_types[row_index], upper_side[row_index]
        )
        results.append(lower_term + upper_term)
    return jnp.stack(results)


def split_table(table):
    high = lax.reduce_precision(table, exponent_bits=8, mantissa_bits=7)
    low = table - high
    high = high.astype(jnp.bfloat16)
    low = low.astype(jnp.bfloat16)
    return jnp.concatenate([high, low, high], axis=1)


def split_masked_table(tables):
    kinds, dof, _ = tables.shape
    flat = jnp.transpose(tables, (1, 0, 2)).reshape(dof, kinds * dof)
    high = lax.reduce_precision(flat, exponent_bits=8, mantissa_bits=7)
    low = flat - high
    high = high.astype(jnp.bfloat16)
    low = low.astype(jnp.bfloat16)
    return jnp.concatenate([high, low, high], axis=1)


def kernel_masked(table_ref, types, state):
    dof = state.shape[0]
    kinds = table_ref.shape[1] // (3 * dof)
    high = state.astype(jnp.bfloat16)
    low = (state - high.astype(jnp.float32)).astype(jnp.bfloat16)
    zero = jnp.zeros_like(high)
    masks = [types == kind for kind in range(kinds)]
    highs = [jnp.where(mask, high, zero) for mask in masks]
    lows = [jnp.where(mask, low, zero) for mask in masks]
    stacked = jnp.concatenate(highs + highs + lows, axis=0)
    return jnp.dot(table_ref[...], stacked, preferred_element_type=jnp.float32)


def kernel_typed(table_ref, types, state):
    dof = state.shape[0]
    high = state.astype(jnp.bfloat16)
    low = (state - high.astype(jnp.float32)).astype(jnp.bfloat16)
    stacked = jnp.concatenate([high, high, low], axis=0)
    products = jnp.dot(table_ref[...], stacked, preferred_element_type=jnp.float32)
    picked = products[0:dof]
    for kind in range(1, table_ref.shape[0] // dof):
        picked = jnp.where(types == kind, products[kind * dof:(kind + 1) * dof], picked)
    return picked


def barrier_with_neighbours(me, length):
    barrier = pltpu.get_barrier_semaphore()

    @pl.when(me > 0)
    def _():
        pl.semaphore_signal(barrier, inc=1, device_id={"stream": me - 1},
                            device_id_type=pl.DeviceIdType.MESH)

    @pl.when(me < length - 1)
    def _():
        pl.semaphore_signal(barrier, inc=1, device_id={"stream": me + 1},
                            device_id_type=pl.DeviceIdType.MESH)

    ends = jnp.logical_or(me == 0, me == length - 1)

    @pl.when(ends)
    def _():
        pl.semaphore_wait(barrier, 1)

    @pl.when(jnp.logical_not(ends))
    def _():
        pl.semaphore_wait(barrier, 2)


def sweep_kernel(length, direction, width, grouped, start_ref, types_ref, coeff_ref, denom_ref, table_ref,
                 out_ref, recv_ref, send_ref, send_sem, recv_sem):
    me = lax.axis_index("stream")
    rows, tracers, dof, columns = start_ref.shape
    sets = tracers // grouped
    blocks = sets * (columns // width)
    if direction > 0:
        has_source = me > 0
        has_target = me < length - 1
        target = me + 1
    else:
        has_source = me < length - 1
        has_target = me > 0
        target = me - 1

    @pl.when(jnp.logical_not(has_source))
    def _():
        recv_ref[...] = jnp.zeros(recv_ref.shape, jnp.float32)

    barrier_with_neighbours(me, length)

    def copy_of(k):
        return pltpu.make_async_remote_copy(
            src_ref=send_ref.at[k],
            dst_ref=recv_ref.at[k],
            send_sem=send_sem.at[k],
            recv_sem=recv_sem.at[k],
            device_id={"stream": target},
            device_id_type=pl.DeviceIdType.MESH,
        )

    row_order = list(range(rows)) if direction > 0 else list(range(rows - 1, -1, -1))

    def gathered(ref, row, first, cols):
        return jnp.concatenate([ref[row, first + tracer, :, cols] for tracer in range(grouped)], axis=1)

    def lanes(ref, row, cols):
        return jnp.concatenate([ref[pl.ds(row, 1), cols]] * grouped, axis=1)

    def block_step(k, carry):
        first = (k % sets) * grouped
        cols = pl.ds(pl.multiple_of((k // sets) * width, width), width)

        @pl.when(has_source)
        def _():
            copy_of(k).wait_recv()

        state = recv_ref[k]
        for row in row_order:
            types = lanes(types_ref, row, cols)
            coeff = lanes(coeff_ref, row, cols)
            if direction > 0:
                state = gathered(start_ref, row, first, cols) - coeff * kernel_typed(table_ref, types, state)
                solved = state
            else:
                solved = gathered(start_ref, row, first, cols) - state / lanes(denom_ref, row, cols)
                state = coeff * kernel_typed(table_ref, types, solved)
            for tracer in range(grouped):
                out_ref[row, first + tracer, :, cols] = solved[:, tracer * width:(tracer + 1) * width]
        send_ref[k] = state

        @pl.when(has_target)
        def _():
            copy_of(k).start()

        return carry

    lax.fori_loop(0, blocks, block_step, 0)

    def drain(k, carry):
        copy_of(k).wait_send()
        return carry

    @pl.when(has_target)
    def _():
        lax.fori_loop(0, blocks, drain, 0)


def sweep(direction, collective_id, width, grouped, start, types, coeff, denom, table):
    rows, tracers, dof, columns = start.shape
    blocks = (tracers // grouped) * (columns // width)
    length = lax.axis_size("stream")
    vmem = pltpu.VMEM
    return pl.pallas_call(
        functools.partial(sweep_kernel, length, direction, width, grouped),
        out_shape=jax.ShapeDtypeStruct(start.shape, jnp.float32),
        in_specs=[pl.BlockSpec(memory_space=vmem)] * 5,
        out_specs=pl.BlockSpec(memory_space=vmem),
        scratch_shapes=[
            pltpu.VMEM((blocks, dof, grouped * width), jnp.float32),
            pltpu.VMEM((blocks, dof, grouped * width), jnp.float32),
            pltpu.SemaphoreType.DMA((blocks,)),
            pltpu.SemaphoreType.DMA((blocks,)),
        ],
        compiler_params=pltpu.CompilerParams(
            collective_id=collective_id, has_side_effects=True, vmem_limit_bytes=60 * 1024 * 1024
        ),
    )(start, types, coeff, denom, table)


def both_kernel(length, width, start_ref, types_ref, coeff_ref, scale_ref, inverse_ref, up_ref, down_ref,
                out_ref, part_ref, recv_f, send_f, recv_b, send_b, sems):
    me = lax.axis_index("stream")
    rows, tracers, dof, columns = start_ref.shape
    sets = tracers
    blocks = sets * (columns // width)
    first_dev = me == 0
    last_dev = me == length - 1

    @pl.when(first_dev)
    def _():
        recv_f[...] = jnp.zeros(recv_f.shape, jnp.float32)

    @pl.when(last_dev)
    def _():
        recv_b[...] = jnp.zeros(recv_b.shape, jnp.float32)

    barrier_with_neighbours(me, length)

    def copy_f(k):
        return pltpu.make_async_remote_copy(
            src_ref=send_f.at[k], dst_ref=recv_f.at[k], send_sem=sems.at[0, k], recv_sem=sems.at[1, k],
            device_id={"stream": me + 1}, device_id_type=pl.DeviceIdType.MESH)

    def copy_b(k):
        return pltpu.make_async_remote_copy(
            src_ref=send_b.at[k], dst_ref=recv_b.at[k], send_sem=sems.at[2, k], recv_sem=sems.at[3, k],
            device_id={"stream": me - 1}, device_id_type=pl.DeviceIdType.MESH)

    def place(k):
        tracer = k % sets
        cols = pl.ds(pl.multiple_of((k // sets) * width, width), width)
        return tracer, cols

    def forward_block(k):
        tracer, cols = place(k)

        @pl.when(jnp.logical_not(first_dev))
        def _():
            copy_f(k).wait_recv()

        state = recv_f[k]
        for row in range(rows):
            types = types_ref[pl.ds(row, 1), cols]
            coeff = coeff_ref[pl.ds(row, 1), cols]
            state = start_ref[row, tracer, :, cols] - coeff * kernel_masked(up_ref, types, state)
            part_ref[row, tracer, :, cols] = state
        send_f[k] = state

        @pl.when(jnp.logical_not(last_dev))
        def _():
            copy_f(k).start()

    def backward_block(k):
        tracer, cols = place(k)

        @pl.when(jnp.logical_not(last_dev))
        def _():
            copy_b(k).wait_recv()

        state = recv_b[k]
        for row in range(rows - 1, -1, -1):
            types = types_ref[pl.ds(row, 1), cols]
            scale = scale_ref[pl.ds(row, 1), cols]
            solved = part_ref[row, tracer, :, cols] - state * inverse_ref[pl.ds(row, 1), cols]
            out_ref[row, tracer, :, cols] = solved
            state = scale * kernel_masked(down_ref, types, solved)
        send_b[k] = state

        @pl.when(jnp.logical_not(first_dev))
        def _():
            copy_b(k).start()

    lead = jnp.minimum(jnp.maximum(((2 * (length - 1) - 2 * me) * 17) // 6, 1), blocks)
    tail = 2 * blocks - lead

    def step(s, carry):
        paired = jnp.logical_and(s >= lead, s < tail)
        odd = (s - lead) % 2 == 1

        @pl.when(s < lead)
        def _():
            forward_block(s)

        @pl.when(jnp.logical_and(paired, odd))
        def _():
            forward_block(lead + (s - lead) // 2)

        @pl.when(jnp.logical_and(paired, jnp.logical_not(odd)))
        def _():
            backward_block((s - lead) // 2)

        @pl.when(s >= tail)
        def _():
            backward_block(s - blocks)

        return carry

    lax.fori_loop(0, 2 * blocks, step, 0)

    def drain_f(k, carry):
        copy_f(k).wait_send()
        return carry

    def drain_b(k, carry):
        copy_b(k).wait_send()
        return carry

    @pl.when(jnp.logical_not(last_dev))
    def _():
        lax.fori_loop(0, blocks, drain_f, 0)

    @pl.when(jnp.logical_not(first_dev))
    def _():
        lax.fori_loop(0, blocks, drain_b, 0)


def both_sweeps(width, start, types, coeff, scale, inverse, up_table, down_table):
    rows, tracers, dof, columns = start.shape
    blocks = tracers * (columns // width)
    length = lax.axis_size("stream")
    vmem = pltpu.VMEM
    return pl.pallas_call(
        functools.partial(both_kernel, length, width),
        out_shape=jax.ShapeDtypeStruct(start.shape, jnp.float32),
        in_specs=[pl.BlockSpec(memory_space=vmem)] * 7,
        out_specs=pl.BlockSpec(memory_space=vmem),
        scratch_shapes=[
            pltpu.VMEM(start.shape, jnp.float32),
            pltpu.VMEM((blocks, dof, width), jnp.float32),
            pltpu.VMEM((blocks, dof, width), jnp.float32),
            pltpu.VMEM((blocks, dof, width), jnp.float32),
            pltpu.VMEM((blocks, dof, width), jnp.float32),
            pltpu.SemaphoreType.DMA((4, blocks)),
        ],
        compiler_params=pltpu.CompilerParams(
            collective_id=0, has_side_effects=True, vmem_limit_bytes=60 * 1024 * 1024
        ),
    )(start, types, coeff, scale, inverse, up_table, down_table)


def per_device(
    rhs, lagged, face_types, stream_scale, span_scale, absorb, up_blocks, down_blocks, diag_inverse
):
    columns = rhs.shape[3]
    dof = up_blocks.shape[1]
    denominator = stream_scale + span_scale[0] + span_scale[1] + absorb
    tables = jnp.einsum("pq,tqs->tps", diag_inverse, up_blocks, precision=precise)
    count = lax.axis_size("span")
    rightward = [(i, i + 1) for i in range(count - 1)]
    leftward = [(i + 1, i) for i in range(count - 1)]
    halo_low = lax.ppermute(lagged[..., columns - 1:], "span", rightward)
    halo_high = lax.ppermute(lagged[..., :1], "span", leftward)
    low_types = jnp.concatenate([face_types[1][:, 1:], face_types[1][:, :1]], axis=1)
    high_types = jnp.concatenate([face_types[2][:, -1:], face_types[2][:, :-1]], axis=1)
    low_scale = jnp.concatenate([span_scale[0][:, 1:], span_scale[0][:, :1]], axis=1)
    high_scale = jnp.concatenate([span_scale[1][:, -1:], span_scale[1][:, :-1]], axis=1)
    lows = []
    highs = []
    for row in range(rhs.shape[0]):
        lows.append(low_scale[row] * typed_product(tables, low_types[row], lagged[row]))
        highs.append(high_scale[row] * typed_product(tables, high_types[row], lagged[row]))
    lows = jnp.stack(lows)
    highs = jnp.stack(highs)
    low_edge = jnp.einsum("npq,nrq->nrp", tables[face_types[1][:, 0]], halo_low[..., 0], precision=fast)
    high_edge = jnp.einsum("npq,nrq->nrp", tables[face_types[2][:, -1]], halo_high[..., 0], precision=fast)
    low_edge = low_edge * span_scale[0][:, None, None, 0]
    high_edge = high_edge * span_scale[1][:, None, None, -1]
    lower = jnp.concatenate([low_edge[..., None], lows[..., :-1]], axis=3)
    upper = jnp.concatenate([highs[..., 1:], high_edge[..., None]], axis=3)
    start = jnp.einsum("pq,nrqc->nrpc", diag_inverse, rhs, precision=fast) - lower - upper
    start = start / denominator[:, None, None, :]
    coeff = stream_scale / denominator
    inverse = 1.0 / denominator
    up_table = split_masked_table(jnp.einsum("pq,tqs->tps", diag_inverse, up_blocks, precision=precise))
    down_table = split_masked_table(jnp.einsum("pq,tqs->tps", diag_inverse, down_blocks, precision=precise))
    return both_sweeps(LANES, start, face_types[0], coeff, stream_scale, inverse, up_table, down_table)


def solution(mesh):
    return jax.shard_map(
        per_device,
        mesh=mesh,
        in_specs=(
            P("stream", None, None, "span"),
            P("stream", None, None, "span"),
            P(None, "stream", "span"),
            P("stream", "span"),
            P(None, "stream", "span"),
            P("stream", "span"),
            P(),
            P(),
            P(),
        ),
        out_specs=P("stream", None, None, "span"),
        check_vma=False,
    )
```

```python
import functools

import jax
import jax.numpy as jnp
from jax import lax
from jax.experimental import pallas as pl
from jax.experimental.pallas import tpu as pltpu
from jax.sharding import PartitionSpec as P

precise = lax.Precision.HIGHEST
fast = lax.Precision.HIGH
LANES = 128


def padded_2(block, sides, width):
    for axis, dim in sides:
        count = lax.axis_size(axis)
        forward = [(i, i + 1) for i in range(count - 1)]
        backward = [(target, source) for source, target in forward]
        low = lax.ppermute(
            lax.slice_in_dim(block, block.shape[dim] - width, None, axis=dim), axis, forward
        )
        high = lax.ppermute(lax.slice_in_dim(block, 0, width, axis=dim), axis, backward)
        block = jnp.concatenate([low, block, high], axis=dim)
    return block


def typed_product(blocks_table, type_ids, state_in):
    products = jnp.einsum("tpq,rqw->trpw", blocks_table, state_in, precision=fast)
    kinds = jnp.arange(blocks_table.shape[0], dtype=jnp.int32)
    selector = (type_ids[None, :] == kinds[:, None]).astype(jnp.float32)
    return jnp.sum(products * selector[:, None, None, :], axis=0)


def span_block(padded, face_types, span_scale, up_blocks, offset, breadth):
    lower_side = lax.dynamic_slice_in_dim(padded, offset, breadth, 3)
    upper_side = lax.dynamic_slice_in_dim(padded, offset + 2, breadth, 3)
    lower_types = face_types[1]
    upper_types = face_types[2]
    lower_scale = span_scale[0]
    upper_scale = span_scale[1]
    results = []
    for row_index in range(padded.shape[0]):
        lower_term = lower_scale[row_index] * typed_product(
            up_blocks, lower_types[row_index], lower_side[row_index]
        )
        upper_term = upper_scale[row_index] * typed_product(
            up_blocks, upper_types[row_index], upper_side[row_index]
        )
        results.append(lower_term + upper_term)
    return jnp.stack(results)


def split_table(table):
    high = lax.reduce_precision(table, exponent_bits=8, mantissa_bits=7)
    low = table - high
    high = high.astype(jnp.bfloat16)
    low = low.astype(jnp.bfloat16)
    return jnp.concatenate([high, low, high], axis=1)


def split_masked_table(tables):
    kinds, dof, _ = tables.shape
    flat = jnp.transpose(tables, (1, 0, 2)).reshape(dof, kinds * dof)
    high = lax.reduce_precision(flat, exponent_bits=8, mantissa_bits=7)
    low = flat - high
    high = high.astype(jnp.bfloat16)
    low = low.astype(jnp.bfloat16)
    return jnp.concatenate([high, low, high], axis=1)


def kernel_masked(table_ref, types, state):
    dof = state.shape[0]
    kinds = table_ref.shape[1] // (3 * dof)
    high = state.astype(jnp.bfloat16)
    low = (state - high.astype(jnp.float32)).astype(jnp.bfloat16)
    zero = jnp.zeros_like(high)
    masks = [types == kind for kind in range(kinds)]
    highs = [jnp.where(mask, high, zero) for mask in masks]
    lows = [jnp.where(mask, low, zero) for mask in masks]
    stacked = jnp.concatenate(highs + highs + lows, axis=0)
    return jnp.dot(table_ref[...], stacked, preferred_element_type=jnp.float32)


def kernel_typed(table_ref, types, state):
    dof = state.shape[0]
    high = state.astype(jnp.bfloat16)
    low = (state - high.astype(jnp.float32)).astype(jnp.bfloat16)
    stacked = jnp.concatenate([high, high, low], axis=0)
    products = jnp.dot(table_ref[...], stacked, preferred_element_type=jnp.float32)
    picked = products[0:dof]
    for kind in range(1, table_ref.shape[0] // dof):
        picked = jnp.where(types == kind, products[kind * dof:(kind + 1) * dof], picked)
    return picked


def barrier_with_neighbours(me, length):
    barrier = pltpu.get_barrier_semaphore()

    @pl.when(me > 0)
    def _():
        pl.semaphore_signal(barrier, inc=1, device_id={"stream": me - 1},
                            device_id_type=pl.DeviceIdType.MESH)

    @pl.when(me < length - 1)
    def _():
        pl.semaphore_signal(barrier, inc=1, device_id={"stream": me + 1},
                            device_id_type=pl.DeviceIdType.MESH)

    ends = jnp.logical_or(me == 0, me == length - 1)

    @pl.when(ends)
    def _():
        pl.semaphore_wait(barrier, 1)

    @pl.when(jnp.logical_not(ends))
    def _():
        pl.semaphore_wait(barrier, 2)


def sweep_kernel(length, direction, width, grouped, start_ref, types_ref, coeff_ref, denom_ref, table_ref,
                 out_ref, recv_ref, send_ref, send_sem, recv_sem):
    me = lax.axis_index("stream")
    rows, tracers, dof, columns = start_ref.shape
    sets = tracers // grouped
    blocks = sets * (columns // width)
    if direction > 0:
        has_source = me > 0
        has_target = me < length - 1
        target = me + 1
    else:
        has_source = me < length - 1
        has_target = me > 0
        target = me - 1

    @pl.when(jnp.logical_not(has_source))
    def _():
        recv_ref[...] = jnp.zeros(recv_ref.shape, jnp.float32)

    barrier_with_neighbours(me, length)

    def copy_of(k):
        return pltpu.make_async_remote_copy(
            src_ref=send_ref.at[k],
            dst_ref=recv_ref.at[k],
            send_sem=send_sem.at[k],
            recv_sem=recv_sem.at[k],
            device_id={"stream": target},
            device_id_type=pl.DeviceIdType.MESH,
        )

    row_order = list(range(rows)) if direction > 0 else list(range(rows - 1, -1, -1))

    def gathered(ref, row, first, cols):
        return jnp.concatenate([ref[row, first + tracer, :, cols] for tracer in range(grouped)], axis=1)

    def lanes(ref, row, cols):
        return jnp.concatenate([ref[pl.ds(row, 1), cols]] * grouped, axis=1)

    def block_step(k, carry):
        first = (k % sets) * grouped
        cols = pl.ds(pl.multiple_of((k // sets) * width, width), width)

        @pl.when(has_source)
        def _():
            copy_of(k).wait_recv()

        state = recv_ref[k]
        for row in row_order:
            types = lanes(types_ref, row, cols)
            coeff = lanes(coeff_ref, row, cols)
            if direction > 0:
                state = gathered(start_ref, row, first, cols) - coeff * kernel_typed(table_ref, types, state)
                solved = state
            else:
                solved = gathered(start_ref, row, first, cols) - state / lanes(denom_ref, row, cols)
                state = coeff * kernel_typed(table_ref, types, solved)
            for tracer in range(grouped):
                out_ref[row, first + tracer, :, cols] = solved[:, tracer * width:(tracer + 1) * width]
        send_ref[k] = state

        @pl.when(has_target)
        def _():
            copy_of(k).start()

        return carry

    lax.fori_loop(0, blocks, block_step, 0)

    def drain(k, carry):
        copy_of(k).wait_send()
        return carry

    @pl.when(has_target)
    def _():
        lax.fori_loop(0, blocks, drain, 0)


def sweep(direction, collective_id, width, grouped, start, types, coeff, denom, table):
    rows, tracers, dof, columns = start.shape
    blocks = (tracers // grouped) * (columns // width)
    length = lax.axis_size("stream")
    vmem = pltpu.VMEM
    return pl.pallas_call(
        functools.partial(sweep_kernel, length, direction, width, grouped),
        out_shape=jax.ShapeDtypeStruct(start.shape, jnp.float32),
        in_specs=[pl.BlockSpec(memory_space=vmem)] * 5,
        out_specs=pl.BlockSpec(memory_space=vmem),
        scratch_shapes=[
            pltpu.VMEM((blocks, dof, grouped * width), jnp.float32),
            pltpu.VMEM((blocks, dof, grouped * width), jnp.float32),
            pltpu.SemaphoreType.DMA((blocks,)),
            pltpu.SemaphoreType.DMA((blocks,)),
        ],
        compiler_params=pltpu.CompilerParams(
            collective_id=collective_id, has_side_effects=True, vmem_limit_bytes=60 * 1024 * 1024
        ),
    )(start, types, coeff, denom, table)


def both_kernel(length, width, lend, start_ref, types_ref, coeff_ref, scale_ref, inverse_ref, up_ref, down_ref,
                out_ref, part_ref, ext_start, ext_types, ext_small, ext_part, ext_out, returned,
                recv_f, send_f, recv_b, send_b, sems, lend_sems, back_sems):
    me = lax.axis_index("stream")
    side = lax.axis_index("span")
    lender = side % 2 == 0
    partner = side + 1 - 2 * (side % 2)
    rows, tracers, dof, columns = start_ref.shape
    sets = tracers
    own = sets * (columns // width)
    lent = sets * lend
    kept = own - lent
    first_cols = columns - lend * width
    count = jnp.where(lender, kept, own + lent)
    first_dev = me == 0
    last_dev = me == length - 1

    @pl.when(first_dev)
    def _():
        recv_f[...] = jnp.zeros(recv_f.shape, jnp.float32)

    @pl.when(last_dev)
    def _():
        recv_b[...] = jnp.zeros(recv_b.shape, jnp.float32)

    barrier = pltpu.get_barrier_semaphore()
    for target in (me - 1, me + 1):
        @pl.when(jnp.logical_and(target >= 0, target < length))
        def _():
            pl.semaphore_signal(barrier, inc=1, device_id={"stream": target},
                                device_id_type=pl.DeviceIdType.MESH)
    pl.semaphore_signal(barrier, inc=1, device_id={"span": partner}, device_id_type=pl.DeviceIdType.MESH)
    ends = jnp.logical_or(first_dev, last_dev)

    @pl.when(ends)
    def _():
        pl.semaphore_wait(barrier, 2)

    @pl.when(jnp.logical_not(ends))
    def _():
        pl.semaphore_wait(barrier, 3)

    lend_cols = pl.ds(first_cols, lend * width)
    small_refs = (types_ref, coeff_ref, scale_ref, inverse_ref)

    def lend_copies():
        copies = [pltpu.make_async_remote_copy(
            src_ref=start_ref.at[:, :, :, lend_cols], dst_ref=ext_start, send_sem=lend_sems.at[0, 0],
            recv_sem=lend_sems.at[1, 0], device_id={"span": partner}, device_id_type=pl.DeviceIdType.MESH)]
        for index, ref in enumerate(small_refs):
            target = ext_types if index == 0 else ext_small.at[index - 1]
            copies.append(pltpu.make_async_remote_copy(
                src_ref=ref.at[:, lend_cols], dst_ref=target, send_sem=lend_sems.at[0, index + 1],
                recv_sem=lend_sems.at[1, index + 1], device_id={"span": partner},
                device_id_type=pl.DeviceIdType.MESH))
        return copies

    @pl.when(lender)
    def _():
        for copy in lend_copies():
            copy.start()

    def copy_f(k):
        return pltpu.make_async_remote_copy(
            src_ref=send_f.at[k], dst_ref=recv_f.at[k], send_sem=sems.at[0, k], recv_sem=sems.at[1, k],
            device_id={"stream": me + 1}, device_id_type=pl.DeviceIdType.MESH)

    def copy_b(k):
        return pltpu.make_async_remote_copy(
            src_ref=send_b.at[k], dst_ref=recv_b.at[k], send_sem=sems.at[2, k], recv_sem=sems.at[3, k],
            device_id={"stream": me - 1}, device_id_type=pl.DeviceIdType.MESH)

    def copy_back(j):
        tracer = j % sets
        cols = pl.ds(pl.multiple_of((j // sets) * width, width), width)
        return pltpu.make_async_remote_copy(
            src_ref=ext_out.at[:, tracer, :, cols], dst_ref=returned.at[:, tracer, :, cols],
            send_sem=back_sems.at[0, j], recv_sem=back_sems.at[1, j], device_id={"span": partner},
            device_id_type=pl.DeviceIdType.MESH)

    def forward_rows(k, tracer, cols, start, small, part):
        @pl.when(jnp.logical_not(first_dev))
        def _():
            copy_f(k).wait_recv()

        state = recv_f[k]
        for row in range(rows):
            types = small(0)[pl.ds(row, 1), cols]
            coeff = small(1)[pl.ds(row, 1), cols]
            state = start[row, tracer, :, cols] - coeff * kernel_masked(up_ref, types, state)
            part[row, tracer, :, cols] = state
        send_f[k] = state

        @pl.when(jnp.logical_not(last_dev))
        def _():
            copy_f(k).start()

    def backward_rows(k, tracer, cols, small, part, out):
        @pl.when(jnp.logical_not(last_dev))
        def _():
            copy_b(k).wait_recv()

        state = recv_b[k]
        for row in range(rows - 1, -1, -1):
            types = small(0)[pl.ds(row, 1), cols]
            scale = small(2)[pl.ds(row, 1), cols]
            solved = part[row, tracer, :, cols] - state * small(3)[pl.ds(row, 1), cols]
            out[row, tracer, :, cols] = solved
            state = scale * kernel_masked(down_ref, types, solved)
        send_b[k] = state

        @pl.when(jnp.logical_not(first_dev))
        def _():
            copy_b(k).start()

    def own_small(index):
        return small_refs[index]

    def ext_small_ref(index):
        return ext_types if index == 0 else ext_small.at[index - 1]

    def place(k):
        return k % sets, pl.ds(pl.multiple_of((k // sets) * width, width), width)

    def forward_block(k):
        @pl.when(k < own)
        def _():
            tracer, cols = place(k)
            forward_rows(k, tracer, cols, start_ref, own_small, part_ref)

        @pl.when(k == own)
        def _():
            for copy in lend_copies():
                copy.wait_recv()

        @pl.when(k >= own)
        def _():
            tracer, cols = place(k - own)
            forward_rows(k, tracer, cols, ext_start, ext_small_ref, ext_part)

    def backward_block(k):
        @pl.when(k < own)
        def _():
            tracer, cols = place(k)
            backward_rows(k, tracer, cols, own_small, part_ref, out_ref)

        @pl.when(k >= own)
        def _():
            tracer, cols = place(k - own)
            backward_rows(k, tracer, cols, ext_small_ref, ext_part, ext_out)
            copy_back(k - own).start()

    lead = jnp.minimum(jnp.maximum(((2 * (length - 1) - 2 * me) * 17) // 6, 1), count)
    tail = 2 * count - lead

    def step(s, carry):
        paired = jnp.logical_and(s >= lead, s < tail)
        odd = (s - lead) % 2 == 1

        @pl.when(s < lead)
        def _():
            forward_block(s)

        @pl.when(jnp.logical_and(paired, odd))
        def _():
            forward_block(lead + (s - lead) // 2)

        @pl.when(jnp.logical_and(paired, jnp.logical_not(odd)))
        def _():
            backward_block((s - lead) // 2)

        @pl.when(s >= tail)
        def _():
            backward_block(s - count)

        return carry

    lax.fori_loop(0, 2 * count, step, 0)

    def drain_f(k, carry):
        copy_f(k).wait_send()
        return carry

    def drain_b(k, carry):
        copy_b(k).wait_send()
        return carry

    @pl.when(jnp.logical_not(last_dev))
    def _():
        lax.fori_loop(0, count, drain_f, 0)

    @pl.when(jnp.logical_not(first_dev))
    def _():
        lax.fori_loop(0, count, drain_b, 0)

    def drain_back(j, carry):
        copy_back(j).wait_send()
        return carry

    def take_back(j, carry):
        copy_back(j).wait_recv()
        return carry

    @pl.when(lender)
    def _():
        for copy in lend_copies():
            copy.wait_send()
        lax.fori_loop(0, lent, take_back, 0)
        out_ref[:, :, :, lend_cols] = returned[...]

    @pl.when(jnp.logical_not(lender))
    def _():
        lax.fori_loop(0, lent, drain_back, 0)


def both_sweeps(width, start, types, coeff, scale, inverse, up_table, down_table):
    rows, tracers, dof, columns = start.shape
    groups = columns // width
    lend = max(1, groups * 3 // 8)
    blocks = tracers * (groups + lend)
    lent = tracers * lend
    length = lax.axis_size("stream")
    vmem = pltpu.VMEM
    ext_shape = (rows, tracers, dof, lend * width)
    return pl.pallas_call(
        functools.partial(both_kernel, length, width, lend),
        out_shape=jax.ShapeDtypeStruct(start.shape, jnp.float32),
        in_specs=[pl.BlockSpec(memory_space=vmem)] * 7,
        out_specs=pl.BlockSpec(memory_space=vmem),
        scratch_shapes=[
            pltpu.VMEM(start.shape, jnp.float32),
            pltpu.VMEM(ext_shape, jnp.float32),
            pltpu.VMEM((rows, lend * width), jnp.int32),
            pltpu.VMEM((3, rows, lend * width), jnp.float32),
            pltpu.VMEM(ext_shape, jnp.float32),
            pltpu.VMEM(ext_shape, jnp.float32),
            pltpu.VMEM(ext_shape, jnp.float32),
            pltpu.VMEM((blocks, dof, width), jnp.float32),
            pltpu.VMEM((blocks, dof, width), jnp.float32),
            pltpu.VMEM((blocks, dof, width), jnp.float32),
            pltpu.VMEM((blocks, dof, width), jnp.float32),
            pltpu.SemaphoreType.DMA((4, blocks)),
            pltpu.SemaphoreType.DMA((2, 5)),
            pltpu.SemaphoreType.DMA((2, lent)),
        ],
        compiler_params=pltpu.CompilerParams(
            collective_id=0, has_side_effects=True, vmem_limit_bytes=60 * 1024 * 1024
        ),
    )(start, types, coeff, scale, inverse, up_table, down_table)


def per_device(
    rhs, lagged, face_types, stream_scale, span_scale, absorb, up_blocks, down_blocks, diag_inverse
):
    columns = rhs.shape[3]
    dof = up_blocks.shape[1]
    padded = padded_2(lagged, (("span", 3),), 1)
    denominator = stream_scale + span_scale[0] + span_scale[1] + absorb
    span_terms = span_block(padded, face_types, span_scale, up_blocks, 0, columns)
    start = jnp.einsum("pq,nrqc->nrpc", diag_inverse, rhs - span_terms, precision=fast)
    start = start / denominator[:, None, None, :]
    coeff = stream_scale / denominator
    inverse = 1.0 / denominator
    up_table = split_masked_table(jnp.einsum("pq,tqs->tps", diag_inverse, up_blocks, precision=precise))
    down_table = split_masked_table(jnp.einsum("pq,tqs->tps", diag_inverse, down_blocks, precision=precise))
    small = [face_types[0], coeff, stream_scale, inverse]
    return both_sweeps(LANES, start, *small, up_table, down_table)


def solution(mesh):
    return jax.shard_map(
        per_device,
        mesh=mesh,
        in_specs=(
            P("stream", None, None, "span"),
            P("stream", None, None, "span"),
            P(None, "stream", "span"),
            P("stream", "span"),
            P(None, "stream", "span"),
            P("stream", "span"),
            P(),
            P(),
            P(),
        ),
        out_specs=P("stream", None, None, "span"),
        check_vma=False,
    )
```

```python
import functools

import jax
import jax.numpy as jnp
from jax import lax
from jax.experimental import pallas as pl
from jax.experimental.pallas import tpu as pltpu
from jax.sharding import PartitionSpec as P

precise = lax.Precision.HIGHEST
fast = lax.Precision.HIGH
LANES = 128


def padded_2(block, sides, width):
    for axis, dim in sides:
        count = lax.axis_size(axis)
        forward = [(i, i + 1) for i in range(count - 1)]
        backward = [(target, source) for source, target in forward]
        low = lax.ppermute(
            lax.slice_in_dim(block, block.shape[dim] - width, None, axis=dim), axis, forward
        )
        high = lax.ppermute(lax.slice_in_dim(block, 0, width, axis=dim), axis, backward)
        block = jnp.concatenate([low, block, high], axis=dim)
    return block


def typed_product(blocks_table, type_ids, state_in):
    products = jnp.einsum("tpq,rqw->trpw", blocks_table, state_in, precision=fast)
    kinds = jnp.arange(blocks_table.shape[0], dtype=jnp.int32)
    selector = (type_ids[None, :] == kinds[:, None]).astype(jnp.float32)
    return jnp.sum(products * selector[:, None, None, :], axis=0)


def span_block(padded, face_types, span_scale, up_blocks, offset, breadth):
    lower_side = lax.dynamic_slice_in_dim(padded, offset, breadth, 3)
    upper_side = lax.dynamic_slice_in_dim(padded, offset + 2, breadth, 3)
    lower_types = face_types[1]
    upper_types = face_types[2]
    lower_scale = span_scale[0]
    upper_scale = span_scale[1]
    results = []
    for row_index in range(padded.shape[0]):
        lower_term = lower_scale[row_index] * typed_product(
            up_blocks, lower_types[row_index], lower_side[row_index]
        )
        upper_term = upper_scale[row_index] * typed_product(
            up_blocks, upper_types[row_index], upper_side[row_index]
        )
        results.append(lower_term + upper_term)
    return jnp.stack(results)


def split_table(table):
    high = lax.reduce_precision(table, exponent_bits=8, mantissa_bits=7)
    low = table - high
    high = high.astype(jnp.bfloat16)
    low = low.astype(jnp.bfloat16)
    return jnp.concatenate([high, low, high], axis=1)


def split_masked_table(tables):
    kinds, dof, _ = tables.shape
    flat = jnp.transpose(tables, (1, 0, 2)).reshape(dof, kinds * dof)
    high = lax.reduce_precision(flat, exponent_bits=8, mantissa_bits=7)
    low = flat - high
    high = high.astype(jnp.bfloat16)
    low = low.astype(jnp.bfloat16)
    return jnp.concatenate([high, low, high], axis=1)


def kernel_masked(table_ref, types, state):
    dof = state.shape[0]
    kinds = table_ref.shape[1] // (3 * dof)
    high = state.astype(jnp.bfloat16)
    low = (state - high.astype(jnp.float32)).astype(jnp.bfloat16)
    zero = jnp.zeros_like(high)
    masks = [types == kind for kind in range(kinds)]
    highs = [jnp.where(mask, high, zero) for mask in masks]
    lows = [jnp.where(mask, low, zero) for mask in masks]
    stacked = jnp.concatenate(highs + highs + lows, axis=0)
    return jnp.dot(table_ref[...], stacked, preferred_element_type=jnp.float32)


def kernel_typed(table_ref, types, state):
    dof = state.shape[0]
    high = state.astype(jnp.bfloat16)
    low = (state - high.astype(jnp.float32)).astype(jnp.bfloat16)
    stacked = jnp.concatenate([high, high, low], axis=0)
    products = jnp.dot(table_ref[...], stacked, preferred_element_type=jnp.float32)
    picked = products[0:dof]
    for kind in range(1, table_ref.shape[0] // dof):
        picked = jnp.where(types == kind, products[kind * dof:(kind + 1) * dof], picked)
    return picked


def barrier_with_neighbours(me, length):
    barrier = pltpu.get_barrier_semaphore()

    @pl.when(me > 0)
    def _():
        pl.semaphore_signal(barrier, inc=1, device_id={"stream": me - 1},
                            device_id_type=pl.DeviceIdType.MESH)

    @pl.when(me < length - 1)
    def _():
        pl.semaphore_signal(barrier, inc=1, device_id={"stream": me + 1},
                            device_id_type=pl.DeviceIdType.MESH)

    ends = jnp.logical_or(me == 0, me == length - 1)

    @pl.when(ends)
    def _():
        pl.semaphore_wait(barrier, 1)

    @pl.when(jnp.logical_not(ends))
    def _():
        pl.semaphore_wait(barrier, 2)


def sweep_kernel(length, direction, width, grouped, start_ref, types_ref, coeff_ref, denom_ref, table_ref,
                 out_ref, recv_ref, send_ref, send_sem, recv_sem):
    me = lax.axis_index("stream")
    rows, tracers, dof, columns = start_ref.shape
    sets = tracers // grouped
    blocks = sets * (columns // width)
    if direction > 0:
        has_source = me > 0
        has_target = me < length - 1
        target = me + 1
    else:
        has_source = me < length - 1
        has_target = me > 0
        target = me - 1

    @pl.when(jnp.logical_not(has_source))
    def _():
        recv_ref[...] = jnp.zeros(recv_ref.shape, jnp.float32)

    barrier_with_neighbours(me, length)

    def copy_of(k):
        return pltpu.make_async_remote_copy(
            src_ref=send_ref.at[k],
            dst_ref=recv_ref.at[k],
            send_sem=send_sem.at[k],
            recv_sem=recv_sem.at[k],
            device_id={"stream": target},
            device_id_type=pl.DeviceIdType.MESH,
        )

    row_order = list(range(rows)) if direction > 0 else list(range(rows - 1, -1, -1))

    def gathered(ref, row, first, cols):
        return jnp.concatenate([ref[row, first + tracer, :, cols] for tracer in range(grouped)], axis=1)

    def lanes(ref, row, cols):
        return jnp.concatenate([ref[pl.ds(row, 1), cols]] * grouped, axis=1)

    def block_step(k, carry):
        first = (k % sets) * grouped
        cols = pl.ds(pl.multiple_of((k // sets) * width, width), width)

        @pl.when(has_source)
        def _():
            copy_of(k).wait_recv()

        state = recv_ref[k]
        for row in row_order:
            types = lanes(types_ref, row, cols)
            coeff = lanes(coeff_ref, row, cols)
            if direction > 0:
                state = gathered(start_ref, row, first, cols) - coeff * kernel_typed(table_ref, types, state)
                solved = state
            else:
                solved = gathered(start_ref, row, first, cols) - state / lanes(denom_ref, row, cols)
                state = coeff * kernel_typed(table_ref, types, solved)
            for tracer in range(grouped):
                out_ref[row, first + tracer, :, cols] = solved[:, tracer * width:(tracer + 1) * width]
        send_ref[k] = state

        @pl.when(has_target)
        def _():
            copy_of(k).start()

        return carry

    lax.fori_loop(0, blocks, block_step, 0)

    def drain(k, carry):
        copy_of(k).wait_send()
        return carry

    @pl.when(has_target)
    def _():
        lax.fori_loop(0, blocks, drain, 0)


def sweep(direction, collective_id, width, grouped, start, types, coeff, denom, table):
    rows, tracers, dof, columns = start.shape
    blocks = (tracers // grouped) * (columns // width)
    length = lax.axis_size("stream")
    vmem = pltpu.VMEM
    return pl.pallas_call(
        functools.partial(sweep_kernel, length, direction, width, grouped),
        out_shape=jax.ShapeDtypeStruct(start.shape, jnp.float32),
        in_specs=[pl.BlockSpec(memory_space=vmem)] * 5,
        out_specs=pl.BlockSpec(memory_space=vmem),
        scratch_shapes=[
            pltpu.VMEM((blocks, dof, grouped * width), jnp.float32),
            pltpu.VMEM((blocks, dof, grouped * width), jnp.float32),
            pltpu.SemaphoreType.DMA((blocks,)),
            pltpu.SemaphoreType.DMA((blocks,)),
        ],
        compiler_params=pltpu.CompilerParams(
            collective_id=collective_id, has_side_effects=True, vmem_limit_bytes=60 * 1024 * 1024
        ),
    )(start, types, coeff, denom, table)


def both_kernel(length, width, lend, start_ref, types_ref, coeff_ref, scale_ref, inverse_ref, up_ref, down_ref,
                out_ref, part_ref, ext_start, ext_types, ext_small, ext_part, ext_out, returned,
                recv_f, send_f, recv_b, send_b, sems, lend_sems, back_sems):
    me = lax.axis_index("stream")
    side = lax.axis_index("span")
    lender = side % 2 == 0
    partner = side + 1 - 2 * (side % 2)
    rows, tracers, dof, columns = start_ref.shape
    sets = tracers
    own = sets * (columns // width)
    lent = sets * lend
    kept = own - lent
    first_cols = columns - lend * width
    count = jnp.where(lender, kept, own + lent)
    first_dev = me == 0
    last_dev = me == length - 1

    @pl.when(first_dev)
    def _():
        recv_f[...] = jnp.zeros(recv_f.shape, jnp.float32)

    @pl.when(last_dev)
    def _():
        recv_b[...] = jnp.zeros(recv_b.shape, jnp.float32)

    barrier = pltpu.get_barrier_semaphore()
    for target in (me - 1, me + 1):
        @pl.when(jnp.logical_and(target >= 0, target < length))
        def _():
            pl.semaphore_signal(barrier, inc=1, device_id={"stream": target},
                                device_id_type=pl.DeviceIdType.MESH)
    pl.semaphore_signal(barrier, inc=1, device_id={"span": partner}, device_id_type=pl.DeviceIdType.MESH)
    ends = jnp.logical_or(first_dev, last_dev)

    @pl.when(ends)
    def _():
        pl.semaphore_wait(barrier, 2)

    @pl.when(jnp.logical_not(ends))
    def _():
        pl.semaphore_wait(barrier, 3)

    lend_cols = pl.ds(first_cols, lend * width)
    small_refs = (types_ref, coeff_ref, scale_ref, inverse_ref)

    def lend_copies():
        copies = [pltpu.make_async_remote_copy(
            src_ref=start_ref.at[:, :, :, lend_cols], dst_ref=ext_start, send_sem=lend_sems.at[0, 0],
            recv_sem=lend_sems.at[1, 0], device_id={"span": partner}, device_id_type=pl.DeviceIdType.MESH)]
        for index, ref in enumerate(small_refs):
            target = ext_types if index == 0 else ext_small.at[index - 1]
            copies.append(pltpu.make_async_remote_copy(
                src_ref=ref.at[:, lend_cols], dst_ref=target, send_sem=lend_sems.at[0, index + 1],
                recv_sem=lend_sems.at[1, index + 1], device_id={"span": partner},
                device_id_type=pl.DeviceIdType.MESH))
        return copies

    @pl.when(lender)
    def _():
        for copy in lend_copies():
            copy.start()

    def copy_f(k):
        return pltpu.make_async_remote_copy(
            src_ref=send_f.at[k], dst_ref=recv_f.at[k], send_sem=sems.at[0, k], recv_sem=sems.at[1, k],
            device_id={"stream": me + 1}, device_id_type=pl.DeviceIdType.MESH)

    def copy_b(k):
        return pltpu.make_async_remote_copy(
            src_ref=send_b.at[k], dst_ref=recv_b.at[k], send_sem=sems.at[2, k], recv_sem=sems.at[3, k],
            device_id={"stream": me - 1}, device_id_type=pl.DeviceIdType.MESH)

    def copy_back(j):
        tracer = j % sets
        cols = pl.ds(pl.multiple_of((j // sets) * width, width), width)
        return pltpu.make_async_remote_copy(
            src_ref=ext_out.at[:, tracer, :, cols], dst_ref=returned.at[:, tracer, :, cols],
            send_sem=back_sems.at[0, j], recv_sem=back_sems.at[1, j], device_id={"span": partner},
            device_id_type=pl.DeviceIdType.MESH)

    def forward_rows(k, tracer, cols, start, small, part):
        @pl.when(jnp.logical_not(first_dev))
        def _():
            copy_f(k).wait_recv()

        state = recv_f[k]
        for row in range(rows):
            types = small(0)[pl.ds(row, 1), cols]
            coeff = small(1)[pl.ds(row, 1), cols]
            state = start[row, tracer, :, cols] - coeff * kernel_masked(up_ref, types, state)
            part[row, tracer, :, cols] = state
        send_f[k] = state

        @pl.when(jnp.logical_not(last_dev))
        def _():
            copy_f(k).start()

    def backward_rows(k, tracer, cols, small, part, out):
        @pl.when(jnp.logical_not(last_dev))
        def _():
            copy_b(k).wait_recv()

        state = recv_b[k]
        for row in range(rows - 1, -1, -1):
            types = small(0)[pl.ds(row, 1), cols]
            scale = small(2)[pl.ds(row, 1), cols]
            solved = part[row, tracer, :, cols] - state * small(3)[pl.ds(row, 1), cols]
            out[row, tracer, :, cols] = solved
            state = scale * kernel_masked(down_ref, types, solved)
        send_b[k] = state

        @pl.when(jnp.logical_not(first_dev))
        def _():
            copy_b(k).start()

    def own_small(index):
        return small_refs[index]

    def ext_small_ref(index):
        return ext_types if index == 0 else ext_small.at[index - 1]

    def place(k):
        return k % sets, pl.ds(pl.multiple_of((k // sets) * width, width), width)

    def forward_block(k):
        @pl.when(k < own)
        def _():
            tracer, cols = place(k)
            forward_rows(k, tracer, cols, start_ref, own_small, part_ref)

        @pl.when(k == own)
        def _():
            for copy in lend_copies():
                copy.wait_recv()

        @pl.when(k >= own)
        def _():
            tracer, cols = place(k - own)
            forward_rows(k, tracer, cols, ext_start, ext_small_ref, ext_part)

    def backward_block(k):
        @pl.when(k < own)
        def _():
            tracer, cols = place(k)
            backward_rows(k, tracer, cols, own_small, part_ref, out_ref)

        @pl.when(k >= own)
        def _():
            tracer, cols = place(k - own)
            backward_rows(k, tracer, cols, ext_small_ref, ext_part, ext_out)
            copy_back(k - own).start()

    lead = jnp.minimum(jnp.maximum(((2 * (length - 1) - 2 * me) * 17) // 6, 1), count)
    tail = 2 * count - lead

    def step(s, carry):
        paired = jnp.logical_and(s >= lead, s < tail)
        odd = (s - lead) % 2 == 1

        @pl.when(s < lead)
        def _():
            forward_block(s)

        @pl.when(jnp.logical_and(paired, odd))
        def _():
            forward_block(lead + (s - lead) // 2)

        @pl.when(jnp.logical_and(paired, jnp.logical_not(odd)))
        def _():
            backward_block((s - lead) // 2)

        @pl.when(s >= tail)
        def _():
            backward_block(s - count)

        return carry

    lax.fori_loop(0, 2 * count, step, 0)

    def drain_f(k, carry):
        copy_f(k).wait_send()
        return carry

    def drain_b(k, carry):
        copy_b(k).wait_send()
        return carry

    @pl.when(jnp.logical_not(last_dev))
    def _():
        lax.fori_loop(0, count, drain_f, 0)

    @pl.when(jnp.logical_not(first_dev))
    def _():
        lax.fori_loop(0, count, drain_b, 0)

    def drain_back(j, carry):
        copy_back(j).wait_send()
        return carry

    def take_back(j, carry):
        copy_back(j).wait_recv()
        return carry

    @pl.when(lender)
    def _():
        for copy in lend_copies():
            copy.wait_send()
        lax.fori_loop(0, lent, take_back, 0)
        out_ref[:, :, :, lend_cols] = returned[...]

    @pl.when(jnp.logical_not(lender))
    def _():
        lax.fori_loop(0, lent, drain_back, 0)


def both_sweeps(width, start, types, coeff, scale, inverse, up_table, down_table):
    rows, tracers, dof, columns = start.shape
    groups = columns // width
    lend = max(1, groups // 2)
    blocks = tracers * (groups + lend)
    lent = tracers * lend
    length = lax.axis_size("stream")
    vmem = pltpu.VMEM
    ext_shape = (rows, tracers, dof, lend * width)
    return pl.pallas_call(
        functools.partial(both_kernel, length, width, lend),
        out_shape=jax.ShapeDtypeStruct(start.shape, jnp.float32),
        in_specs=[pl.BlockSpec(memory_space=vmem)] * 7,
        out_specs=pl.BlockSpec(memory_space=vmem),
        scratch_shapes=[
            pltpu.VMEM(start.shape, jnp.float32),
            pltpu.VMEM(ext_shape, jnp.float32),
            pltpu.VMEM((rows, lend * width), jnp.int32),
            pltpu.VMEM((3, rows, lend * width), jnp.float32),
            pltpu.VMEM(ext_shape, jnp.float32),
            pltpu.VMEM(ext_shape, jnp.float32),
            pltpu.VMEM(ext_shape, jnp.float32),
            pltpu.VMEM((blocks, dof, width), jnp.float32),
            pltpu.VMEM((blocks, dof, width), jnp.float32),
            pltpu.VMEM((blocks, dof, width), jnp.float32),
            pltpu.VMEM((blocks, dof, width), jnp.float32),
            pltpu.SemaphoreType.DMA((4, blocks)),
            pltpu.SemaphoreType.DMA((2, 5)),
            pltpu.SemaphoreType.DMA((2, lent)),
        ],
        compiler_params=pltpu.CompilerParams(
            collective_id=0, has_side_effects=True, vmem_limit_bytes=60 * 1024 * 1024
        ),
    )(start, types, coeff, scale, inverse, up_table, down_table)


def per_device(
    rhs, lagged, face_types, stream_scale, span_scale, absorb, up_blocks, down_blocks, diag_inverse
):
    columns = rhs.shape[3]
    dof = up_blocks.shape[1]
    padded = padded_2(lagged, (("span", 3),), 1)
    denominator = stream_scale + span_scale[0] + span_scale[1] + absorb
    span_terms = span_block(padded, face_types, span_scale, up_blocks, 0, columns)
    start = jnp.einsum("pq,nrqc->nrpc", diag_inverse, rhs - span_terms, precision=fast)
    start = start / denominator[:, None, None, :]
    coeff = stream_scale / denominator
    inverse = 1.0 / denominator
    up_table = split_masked_table(jnp.einsum("pq,tqs->tps", diag_inverse, up_blocks, precision=precise))
    down_table = split_masked_table(jnp.einsum("pq,tqs->tps", diag_inverse, down_blocks, precision=precise))
    small = [face_types[0], coeff, stream_scale, inverse]
    return both_sweeps(LANES, start, *small, up_table, down_table)


def solution(mesh):
    return jax.shard_map(
        per_device,
        mesh=mesh,
        in_specs=(
            P("stream", None, None, "span"),
            P("stream", None, None, "span"),
            P(None, "stream", "span"),
            P("stream", "span"),
            P(None, "stream", "span"),
            P("stream", "span"),
            P(),
            P(),
            P(),
        ),
        out_specs=P("stream", None, None, "span"),
        check_vma=False,
    )
```

```python
import functools

import jax
import jax.numpy as jnp
from jax import lax
from jax.experimental import pallas as pl
from jax.experimental.pallas import tpu as pltpu
from jax.sharding import PartitionSpec as P

precise = lax.Precision.HIGHEST
fast = lax.Precision.HIGH
LANES = 128


def padded_2(block, sides, width):
    for axis, dim in sides:
        count = lax.axis_size(axis)
        forward = [(i, i + 1) for i in range(count - 1)]
        backward = [(target, source) for source, target in forward]
        low = lax.ppermute(
            lax.slice_in_dim(block, block.shape[dim] - width, None, axis=dim), axis, forward
        )
        high = lax.ppermute(lax.slice_in_dim(block, 0, width, axis=dim), axis, backward)
        block = jnp.concatenate([low, block, high], axis=dim)
    return block


def typed_product(blocks_table, type_ids, state_in):
    products = jnp.einsum("tpq,rqw->trpw", blocks_table, state_in, precision=fast)
    kinds = jnp.arange(blocks_table.shape[0], dtype=jnp.int32)
    selector = (type_ids[None, :] == kinds[:, None]).astype(jnp.float32)
    return jnp.sum(products * selector[:, None, None, :], axis=0)


def span_block(padded, face_types, span_scale, up_blocks, offset, breadth):
    lower_side = lax.dynamic_slice_in_dim(padded, offset, breadth, 3)
    upper_side = lax.dynamic_slice_in_dim(padded, offset + 2, breadth, 3)
    lower_types = face_types[1]
    upper_types = face_types[2]
    lower_scale = span_scale[0]
    upper_scale = span_scale[1]
    results = []
    for row_index in range(padded.shape[0]):
        lower_term = lower_scale[row_index] * typed_product(
            up_blocks, lower_types[row_index], lower_side[row_index]
        )
        upper_term = upper_scale[row_index] * typed_product(
            up_blocks, upper_types[row_index], upper_side[row_index]
        )
        results.append(lower_term + upper_term)
    return jnp.stack(results)


def split_table(table):
    high = lax.reduce_precision(table, exponent_bits=8, mantissa_bits=7)
    low = table - high
    high = high.astype(jnp.bfloat16)
    low = low.astype(jnp.bfloat16)
    return jnp.concatenate([high, low, high], axis=1)


def split_masked_table(tables):
    kinds, dof, _ = tables.shape
    flat = jnp.transpose(tables, (1, 0, 2)).reshape(dof, kinds * dof)
    high = lax.reduce_precision(flat, exponent_bits=8, mantissa_bits=7)
    low = flat - high
    high = high.astype(jnp.bfloat16)
    low = low.astype(jnp.bfloat16)
    return jnp.concatenate([high, low, high], axis=1)


def kernel_masked(table_ref, types, state):
    dof = state.shape[0]
    kinds = table_ref.shape[1] // (3 * dof)
    high = state.astype(jnp.bfloat16)
    low = (state - high.astype(jnp.float32)).astype(jnp.bfloat16)
    zero = jnp.zeros_like(high)
    masks = [types == kind for kind in range(kinds)]
    highs = [jnp.where(mask, high, zero) for mask in masks]
    lows = [jnp.where(mask, low, zero) for mask in masks]
    stacked = jnp.concatenate(highs + highs + lows, axis=0)
    return jnp.dot(table_ref[...], stacked, preferred_element_type=jnp.float32)


def kernel_typed(table_ref, types, state):
    dof = state.shape[0]
    high = state.astype(jnp.bfloat16)
    low = (state - high.astype(jnp.float32)).astype(jnp.bfloat16)
    stacked = jnp.concatenate([high, high, low], axis=0)
    products = jnp.dot(table_ref[...], stacked, preferred_element_type=jnp.float32)
    picked = products[0:dof]
    for kind in range(1, table_ref.shape[0] // dof):
        picked = jnp.where(types == kind, products[kind * dof:(kind + 1) * dof], picked)
    return picked


def barrier_with_neighbours(me, length):
    barrier = pltpu.get_barrier_semaphore()

    @pl.when(me > 0)
    def _():
        pl.semaphore_signal(barrier, inc=1, device_id={"stream": me - 1},
                            device_id_type=pl.DeviceIdType.MESH)

    @pl.when(me < length - 1)
    def _():
        pl.semaphore_signal(barrier, inc=1, device_id={"stream": me + 1},
                            device_id_type=pl.DeviceIdType.MESH)

    ends = jnp.logical_or(me == 0, me == length - 1)

    @pl.when(ends)
    def _():
        pl.semaphore_wait(barrier, 1)

    @pl.when(jnp.logical_not(ends))
    def _():
        pl.semaphore_wait(barrier, 2)


def sweep_kernel(length, direction, width, grouped, start_ref, types_ref, coeff_ref, denom_ref, table_ref,
                 out_ref, recv_ref, send_ref, send_sem, recv_sem):
    me = lax.axis_index("stream")
    rows, tracers, dof, columns = start_ref.shape
    sets = tracers // grouped
    blocks = sets * (columns // width)
    if direction > 0:
        has_source = me > 0
        has_target = me < length - 1
        target = me + 1
    else:
        has_source = me < length - 1
        has_target = me > 0
        target = me - 1

    @pl.when(jnp.logical_not(has_source))
    def _():
        recv_ref[...] = jnp.zeros(recv_ref.shape, jnp.float32)

    barrier_with_neighbours(me, length)

    def copy_of(k):
        return pltpu.make_async_remote_copy(
            src_ref=send_ref.at[k],
            dst_ref=recv_ref.at[k],
            send_sem=send_sem.at[k],
            recv_sem=recv_sem.at[k],
            device_id={"stream": target},
            device_id_type=pl.DeviceIdType.MESH,
        )

    row_order = list(range(rows)) if direction > 0 else list(range(rows - 1, -1, -1))

    def gathered(ref, row, first, cols):
        return jnp.concatenate([ref[row, first + tracer, :, cols] for tracer in range(grouped)], axis=1)

    def lanes(ref, row, cols):
        return jnp.concatenate([ref[pl.ds(row, 1), cols]] * grouped, axis=1)

    def block_step(k, carry):
        first = (k % sets) * grouped
        cols = pl.ds(pl.multiple_of((k // sets) * width, width), width)

        @pl.when(has_source)
        def _():
            copy_of(k).wait_recv()

        state = recv_ref[k]
        for row in row_order:
            types = lanes(types_ref, row, cols)
            coeff = lanes(coeff_ref, row, cols)
            if direction > 0:
                state = gathered(start_ref, row, first, cols) - coeff * kernel_typed(table_ref, types, state)
                solved = state
            else:
                solved = gathered(start_ref, row, first, cols) - state / lanes(denom_ref, row, cols)
                state = coeff * kernel_typed(table_ref, types, solved)
            for tracer in range(grouped):
                out_ref[row, first + tracer, :, cols] = solved[:, tracer * width:(tracer + 1) * width]
        send_ref[k] = state

        @pl.when(has_target)
        def _():
            copy_of(k).start()

        return carry

    lax.fori_loop(0, blocks, block_step, 0)

    def drain(k, carry):
        copy_of(k).wait_send()
        return carry

    @pl.when(has_target)
    def _():
        lax.fori_loop(0, blocks, drain, 0)


def sweep(direction, collective_id, width, grouped, start, types, coeff, denom, table):
    rows, tracers, dof, columns = start.shape
    blocks = (tracers // grouped) * (columns // width)
    length = lax.axis_size("stream")
    vmem = pltpu.VMEM
    return pl.pallas_call(
        functools.partial(sweep_kernel, length, direction, width, grouped),
        out_shape=jax.ShapeDtypeStruct(start.shape, jnp.float32),
        in_specs=[pl.BlockSpec(memory_space=vmem)] * 5,
        out_specs=pl.BlockSpec(memory_space=vmem),
        scratch_shapes=[
            pltpu.VMEM((blocks, dof, grouped * width), jnp.float32),
            pltpu.VMEM((blocks, dof, grouped * width), jnp.float32),
            pltpu.SemaphoreType.DMA((blocks,)),
            pltpu.SemaphoreType.DMA((blocks,)),
        ],
        compiler_params=pltpu.CompilerParams(
            collective_id=collective_id, has_side_effects=True, vmem_limit_bytes=60 * 1024 * 1024
        ),
    )(start, types, coeff, denom, table)


def both_kernel(length, width, lend, start_ref, types_ref, coeff_ref, scale_ref, inverse_ref, up_ref, down_ref,
                out_ref, part_ref, ext_start, ext_types, ext_small, ext_part, ext_out, returned,
                recv_f, send_f, recv_b, send_b, sems, lend_sems, back_sems):
    me = lax.axis_index("stream")
    side = lax.axis_index("span")
    lender = side % 2 == 0
    partner = side + 1 - 2 * (side % 2)
    rows, tracers, dof, columns = start_ref.shape
    sets = tracers
    own = sets * (columns // width)
    lent = sets * lend
    kept = own - lent
    first_cols = columns - lend * width
    count = jnp.where(lender, kept, own + lent)
    first_dev = me == 0
    last_dev = me == length - 1

    @pl.when(first_dev)
    def _():
        recv_f[...] = jnp.zeros(recv_f.shape, jnp.float32)

    @pl.when(last_dev)
    def _():
        recv_b[...] = jnp.zeros(recv_b.shape, jnp.float32)

    barrier = pltpu.get_barrier_semaphore()
    for target in (me - 1, me + 1):
        @pl.when(jnp.logical_and(target >= 0, target < length))
        def _():
            pl.semaphore_signal(barrier, inc=1, device_id={"stream": target},
                                device_id_type=pl.DeviceIdType.MESH)
    pl.semaphore_signal(barrier, inc=1, device_id={"span": partner}, device_id_type=pl.DeviceIdType.MESH)
    ends = jnp.logical_or(first_dev, last_dev)

    @pl.when(ends)
    def _():
        pl.semaphore_wait(barrier, 2)

    @pl.when(jnp.logical_not(ends))
    def _():
        pl.semaphore_wait(barrier, 3)

    lend_cols = pl.ds(first_cols, lend * width)
    small_refs = (types_ref, coeff_ref, scale_ref, inverse_ref)

    def lend_copies():
        copies = [pltpu.make_async_remote_copy(
            src_ref=start_ref.at[:, :, :, lend_cols], dst_ref=ext_start, send_sem=lend_sems.at[0, 0],
            recv_sem=lend_sems.at[1, 0], device_id={"span": partner}, device_id_type=pl.DeviceIdType.MESH)]
        for index, ref in enumerate(small_refs):
            target = ext_types if index == 0 else ext_small.at[index - 1]
            copies.append(pltpu.make_async_remote_copy(
                src_ref=ref.at[:, lend_cols], dst_ref=target, send_sem=lend_sems.at[0, index + 1],
                recv_sem=lend_sems.at[1, index + 1], device_id={"span": partner},
                device_id_type=pl.DeviceIdType.MESH))
        return copies

    @pl.when(lender)
    def _():
        for copy in lend_copies():
            copy.start()

    def copy_f(k):
        return pltpu.make_async_remote_copy(
            src_ref=send_f.at[k], dst_ref=recv_f.at[k], send_sem=sems.at[0, k], recv_sem=sems.at[1, k],
            device_id={"stream": me + 1}, device_id_type=pl.DeviceIdType.MESH)

    def copy_b(k):
        return pltpu.make_async_remote_copy(
            src_ref=send_b.at[k], dst_ref=recv_b.at[k], send_sem=sems.at[2, k], recv_sem=sems.at[3, k],
            device_id={"stream": me - 1}, device_id_type=pl.DeviceIdType.MESH)

    def copy_back(j):
        tracer = j % sets
        cols = pl.ds(pl.multiple_of((j // sets) * width, width), width)
        return pltpu.make_async_remote_copy(
            src_ref=ext_out.at[:, tracer, :, cols], dst_ref=returned.at[:, tracer, :, cols],
            send_sem=back_sems.at[0, j], recv_sem=back_sems.at[1, j], device_id={"span": partner},
            device_id_type=pl.DeviceIdType.MESH)

    def forward_rows(k, tracer, cols, start, small, part):
        @pl.when(jnp.logical_not(first_dev))
        def _():
            copy_f(k).wait_recv()

        state = recv_f[k]
        for row in range(rows):
            types = small(0)[pl.ds(row, 1), cols]
            coeff = small(1)[pl.ds(row, 1), cols]
            state = start[row, tracer, :, cols] - coeff * kernel_masked(up_ref, types, state)
            part[row, tracer, :, cols] = state
        send_f[k] = state

        @pl.when(jnp.logical_not(last_dev))
        def _():
            copy_f(k).start()

    def backward_rows(k, tracer, cols, small, part, out):
        @pl.when(jnp.logical_not(last_dev))
        def _():
            copy_b(k).wait_recv()

        state = recv_b[k]
        for row in range(rows - 1, -1, -1):
            types = small(0)[pl.ds(row, 1), cols]
            scale = small(2)[pl.ds(row, 1), cols]
            solved = part[row, tracer, :, cols] - state * small(3)[pl.ds(row, 1), cols]
            out[row, tracer, :, cols] = solved
            state = scale * kernel_masked(down_ref, types, solved)
        send_b[k] = state

        @pl.when(jnp.logical_not(first_dev))
        def _():
            copy_b(k).start()

    def own_small(index):
        return small_refs[index]

    def ext_small_ref(index):
        return ext_types if index == 0 else ext_small.at[index - 1]

    def place(k):
        return k % sets, pl.ds(pl.multiple_of((k // sets) * width, width), width)

    def forward_block(k):
        @pl.when(k < own)
        def _():
            tracer, cols = place(k)
            forward_rows(k, tracer, cols, start_ref, own_small, part_ref)

        @pl.when(k == own)
        def _():
            for copy in lend_copies():
                copy.wait_recv()

        @pl.when(k >= own)
        def _():
            tracer, cols = place(k - own)
            forward_rows(k, tracer, cols, ext_start, ext_small_ref, ext_part)

    def backward_block(k):
        @pl.when(k < own)
        def _():
            tracer, cols = place(k)
            backward_rows(k, tracer, cols, own_small, part_ref, out_ref)

        @pl.when(k >= own)
        def _():
            tracer, cols = place(k - own)
            backward_rows(k, tracer, cols, ext_small_ref, ext_part, ext_out)
            copy_back(k - own).start()

    lead = jnp.minimum(jnp.maximum(((2 * (length - 1) - 2 * me) * 17) // 6, 1), count)
    tail = 2 * count - lead

    def step(s, carry):
        paired = jnp.logical_and(s >= lead, s < tail)
        odd = (s - lead) % 2 == 1

        @pl.when(s < lead)
        def _():
            forward_block(s)

        @pl.when(jnp.logical_and(paired, odd))
        def _():
            forward_block(lead + (s - lead) // 2)

        @pl.when(jnp.logical_and(paired, jnp.logical_not(odd)))
        def _():
            backward_block((s - lead) // 2)

        @pl.when(s >= tail)
        def _():
            backward_block(s - count)

        return carry

    lax.fori_loop(0, 2 * count, step, 0)

    def drain_f(k, carry):
        copy_f(k).wait_send()
        return carry

    def drain_b(k, carry):
        copy_b(k).wait_send()
        return carry

    @pl.when(jnp.logical_not(last_dev))
    def _():
        lax.fori_loop(0, count, drain_f, 0)

    @pl.when(jnp.logical_not(first_dev))
    def _():
        lax.fori_loop(0, count, drain_b, 0)

    def drain_back(j, carry):
        copy_back(j).wait_send()
        return carry

    def take_back(j, carry):
        copy_back(j).wait_recv()
        return carry

    @pl.when(lender)
    def _():
        for copy in lend_copies():
            copy.wait_send()
        lax.fori_loop(0, lent, take_back, 0)
        out_ref[:, :, :, lend_cols] = returned[...]

    @pl.when(jnp.logical_not(lender))
    def _():
        lax.fori_loop(0, lent, drain_back, 0)


def both_sweeps(width, start, types, coeff, scale, inverse, up_table, down_table):
    rows, tracers, dof, columns = start.shape
    groups = columns // width
    lend = max(1, groups * 5 // 8)
    blocks = tracers * (groups + lend)
    lent = tracers * lend
    length = lax.axis_size("stream")
    vmem = pltpu.VMEM
    ext_shape = (rows, tracers, dof, lend * width)
    return pl.pallas_call(
        functools.partial(both_kernel, length, width, lend),
        out_shape=jax.ShapeDtypeStruct(start.shape, jnp.float32),
        in_specs=[pl.BlockSpec(memory_space=vmem)] * 7,
        out_specs=pl.BlockSpec(memory_space=vmem),
        scratch_shapes=[
            pltpu.VMEM(start.shape, jnp.float32),
            pltpu.VMEM(ext_shape, jnp.float32),
            pltpu.VMEM((rows, lend * width), jnp.int32),
            pltpu.VMEM((3, rows, lend * width), jnp.float32),
            pltpu.VMEM(ext_shape, jnp.float32),
            pltpu.VMEM(ext_shape, jnp.float32),
            pltpu.VMEM(ext_shape, jnp.float32),
            pltpu.VMEM((blocks, dof, width), jnp.float32),
            pltpu.VMEM((blocks, dof, width), jnp.float32),
            pltpu.VMEM((blocks, dof, width), jnp.float32),
            pltpu.VMEM((blocks, dof, width), jnp.float32),
            pltpu.SemaphoreType.DMA((4, blocks)),
            pltpu.SemaphoreType.DMA((2, 5)),
            pltpu.SemaphoreType.DMA((2, lent)),
        ],
        compiler_params=pltpu.CompilerParams(
            collective_id=0, has_side_effects=True, vmem_limit_bytes=60 * 1024 * 1024
        ),
    )(start, types, coeff, scale, inverse, up_table, down_table)


def per_device(
    rhs, lagged, face_types, stream_scale, span_scale, absorb, up_blocks, down_blocks, diag_inverse
):
    columns = rhs.shape[3]
    dof = up_blocks.shape[1]
    padded = padded_2(lagged, (("span", 3),), 1)
    denominator = stream_scale + span_scale[0] + span_scale[1] + absorb
    span_terms = span_block(padded, face_types, span_scale, up_blocks, 0, columns)
    start = jnp.einsum("pq,nrqc->nrpc", diag_inverse, rhs - span_terms, precision=fast)
    start = start / denominator[:, None, None, :]
    coeff = stream_scale / denominator
    inverse = 1.0 / denominator
    up_table = split_masked_table(jnp.einsum("pq,tqs->tps", diag_inverse, up_blocks, precision=precise))
    down_table = split_masked_table(jnp.einsum("pq,tqs->tps", diag_inverse, down_blocks, precision=precise))
    small = [face_types[0], coeff, stream_scale, inverse]
    return both_sweeps(LANES, start, *small, up_table, down_table)


def solution(mesh):
    return jax.shard_map(
        per_device,
        mesh=mesh,
        in_specs=(
            P("stream", None, None, "span"),
            P("stream", None, None, "span"),
            P(None, "stream", "span"),
            P("stream", "span"),
            P(None, "stream", "span"),
            P("stream", "span"),
            P(),
            P(),
            P(),
        ),
        out_specs=P("stream", None, None, "span"),
        check_vma=False,
    )
```

```python
import functools

import jax
import jax.numpy as jnp
from jax import lax
from jax.experimental import pallas as pl
from jax.experimental.pallas import tpu as pltpu
from jax.sharding import PartitionSpec as P

precise = lax.Precision.HIGHEST
fast = lax.Precision.HIGH
LANES = 128


def padded_2(block, sides, width):
    for axis, dim in sides:
        count = lax.axis_size(axis)
        forward = [(i, i + 1) for i in range(count - 1)]
        backward = [(target, source) for source, target in forward]
        low = lax.ppermute(
            lax.slice_in_dim(block, block.shape[dim] - width, None, axis=dim), axis, forward
        )
        high = lax.ppermute(lax.slice_in_dim(block, 0, width, axis=dim), axis, backward)
        block = jnp.concatenate([low, block, high], axis=dim)
    return block


def typed_product(blocks_table, type_ids, state_in):
    products = jnp.einsum("tpq,rqw->trpw", blocks_table, state_in, precision=fast)
    kinds = jnp.arange(blocks_table.shape[0], dtype=jnp.int32)
    selector = (type_ids[None, :] == kinds[:, None]).astype(jnp.float32)
    return jnp.sum(products * selector[:, None, None, :], axis=0)


def span_block(padded, face_types, span_scale, up_blocks, offset, breadth):
    lower_side = lax.dynamic_slice_in_dim(padded, offset, breadth, 3)
    upper_side = lax.dynamic_slice_in_dim(padded, offset + 2, breadth, 3)
    lower_types = face_types[1]
    upper_types = face_types[2]
    lower_scale = span_scale[0]
    upper_scale = span_scale[1]
    results = []
    for row_index in range(padded.shape[0]):
        lower_term = lower_scale[row_index] * typed_product(
            up_blocks, lower_types[row_index], lower_side[row_index]
        )
        upper_term = upper_scale[row_index] * typed_product(
            up_blocks, upper_types[row_index], upper_side[row_index]
        )
        results.append(lower_term + upper_term)
    return jnp.stack(results)


def split_table(table):
    high = lax.reduce_precision(table, exponent_bits=8, mantissa_bits=7)
    low = table - high
    high = high.astype(jnp.bfloat16)
    low = low.astype(jnp.bfloat16)
    return jnp.concatenate([high, low, high], axis=1)


def split_masked_table(tables):
    kinds, dof, _ = tables.shape
    flat = jnp.transpose(tables, (1, 0, 2)).reshape(dof, kinds * dof)
    high = lax.reduce_precision(flat, exponent_bits=8, mantissa_bits=7)
    low = flat - high
    high = high.astype(jnp.bfloat16)
    low = low.astype(jnp.bfloat16)
    return jnp.concatenate([high, low, high], axis=1)


def kernel_masked(table_ref, types, state):
    dof = state.shape[0]
    kinds = table_ref.shape[1] // (3 * dof)
    high = state.astype(jnp.bfloat16)
    low = (state - high.astype(jnp.float32)).astype(jnp.bfloat16)
    zero = jnp.zeros_like(high)
    masks = [types == kind for kind in range(kinds)]
    highs = [jnp.where(mask, high, zero) for mask in masks]
    lows = [jnp.where(mask, low, zero) for mask in masks]
    stacked = jnp.concatenate(highs + highs + lows, axis=0)
    return jnp.dot(table_ref[...], stacked, preferred_element_type=jnp.float32)


def kernel_typed(table_ref, types, state):
    dof = state.shape[0]
    high = state.astype(jnp.bfloat16)
    low = (state - high.astype(jnp.float32)).astype(jnp.bfloat16)
    stacked = jnp.concatenate([high, high, low], axis=0)
    products = jnp.dot(table_ref[...], stacked, preferred_element_type=jnp.float32)
    picked = products[0:dof]
    for kind in range(1, table_ref.shape[0] // dof):
        picked = jnp.where(types == kind, products[kind * dof:(kind + 1) * dof], picked)
    return picked


def barrier_with_neighbours(me, length):
    barrier = pltpu.get_barrier_semaphore()

    @pl.when(me > 0)
    def _():
        pl.semaphore_signal(barrier, inc=1, device_id={"stream": me - 1},
                            device_id_type=pl.DeviceIdType.MESH)

    @pl.when(me < length - 1)
    def _():
        pl.semaphore_signal(barrier, inc=1, device_id={"stream": me + 1},
                            device_id_type=pl.DeviceIdType.MESH)

    ends = jnp.logical_or(me == 0, me == length - 1)

    @pl.when(ends)
    def _():
        pl.semaphore_wait(barrier, 1)

    @pl.when(jnp.logical_not(ends))
    def _():
        pl.semaphore_wait(barrier, 2)


def sweep_kernel(length, direction, width, grouped, start_ref, types_ref, coeff_ref, denom_ref, table_ref,
                 out_ref, recv_ref, send_ref, send_sem, recv_sem):
    me = lax.axis_index("stream")
    rows, tracers, dof, columns = start_ref.shape
    sets = tracers // grouped
    blocks = sets * (columns // width)
    if direction > 0:
        has_source = me > 0
        has_target = me < length - 1
        target = me + 1
    else:
        has_source = me < length - 1
        has_target = me > 0
        target = me - 1

    @pl.when(jnp.logical_not(has_source))
    def _():
        recv_ref[...] = jnp.zeros(recv_ref.shape, jnp.float32)

    barrier_with_neighbours(me, length)

    def copy_of(k):
        return pltpu.make_async_remote_copy(
            src_ref=send_ref.at[k],
            dst_ref=recv_ref.at[k],
            send_sem=send_sem.at[k],
            recv_sem=recv_sem.at[k],
            device_id={"stream": target},
            device_id_type=pl.DeviceIdType.MESH,
        )

    row_order = list(range(rows)) if direction > 0 else list(range(rows - 1, -1, -1))

    def gathered(ref, row, first, cols):
        return jnp.concatenate([ref[row, first + tracer, :, cols] for tracer in range(grouped)], axis=1)

    def lanes(ref, row, cols):
        return jnp.concatenate([ref[pl.ds(row, 1), cols]] * grouped, axis=1)

    def block_step(k, carry):
        first = (k % sets) * grouped
        cols = pl.ds(pl.multiple_of((k // sets) * width, width), width)

        @pl.when(has_source)
        def _():
            copy_of(k).wait_recv()

        state = recv_ref[k]
        for row in row_order:
            types = lanes(types_ref, row, cols)
            coeff = lanes(coeff_ref, row, cols)
            if direction > 0:
                state = gathered(start_ref, row, first, cols) - coeff * kernel_typed(table_ref, types, state)
                solved = state
            else:
                solved = gathered(start_ref, row, first, cols) - state / lanes(denom_ref, row, cols)
                state = coeff * kernel_typed(table_ref, types, solved)
            for tracer in range(grouped):
                out_ref[row, first + tracer, :, cols] = solved[:, tracer * width:(tracer + 1) * width]
        send_ref[k] = state

        @pl.when(has_target)
        def _():
            copy_of(k).start()

        return carry

    lax.fori_loop(0, blocks, block_step, 0)

    def drain(k, carry):
        copy_of(k).wait_send()
        return carry

    @pl.when(has_target)
    def _():
        lax.fori_loop(0, blocks, drain, 0)


def sweep(direction, collective_id, width, grouped, start, types, coeff, denom, table):
    rows, tracers, dof, columns = start.shape
    blocks = (tracers // grouped) * (columns // width)
    length = lax.axis_size("stream")
    vmem = pltpu.VMEM
    return pl.pallas_call(
        functools.partial(sweep_kernel, length, direction, width, grouped),
        out_shape=jax.ShapeDtypeStruct(start.shape, jnp.float32),
        in_specs=[pl.BlockSpec(memory_space=vmem)] * 5,
        out_specs=pl.BlockSpec(memory_space=vmem),
        scratch_shapes=[
            pltpu.VMEM((blocks, dof, grouped * width), jnp.float32),
            pltpu.VMEM((blocks, dof, grouped * width), jnp.float32),
            pltpu.SemaphoreType.DMA((blocks,)),
            pltpu.SemaphoreType.DMA((blocks,)),
        ],
        compiler_params=pltpu.CompilerParams(
            collective_id=collective_id, has_side_effects=True, vmem_limit_bytes=60 * 1024 * 1024
        ),
    )(start, types, coeff, denom, table)


def both_kernel(length, width, lend, start_ref, types_ref, coeff_ref, scale_ref, inverse_ref, up_ref, down_ref,
                out_ref, part_ref, ext_start, ext_types, ext_small, ext_part, ext_out, returned,
                recv_f, send_f, recv_b, send_b, sems, lend_sems, back_sems):
    me = lax.axis_index("stream")
    side = lax.axis_index("span")
    lender = side % 2 == 0
    partner = side + 1 - 2 * (side % 2)
    rows, tracers, dof, columns = start_ref.shape
    sets = tracers
    own = sets * (columns // width)
    lent = sets * lend
    kept = own - lent
    first_cols = columns - lend * width
    count = jnp.where(lender, kept, own + lent)
    first_dev = me == 0
    last_dev = me == length - 1

    @pl.when(first_dev)
    def _():
        recv_f[...] = jnp.zeros(recv_f.shape, jnp.float32)

    @pl.when(last_dev)
    def _():
        recv_b[...] = jnp.zeros(recv_b.shape, jnp.float32)

    barrier = pltpu.get_barrier_semaphore()
    for target in (me - 1, me + 1):
        @pl.when(jnp.logical_and(target >= 0, target < length))
        def _():
            pl.semaphore_signal(barrier, inc=1, device_id={"stream": target},
                                device_id_type=pl.DeviceIdType.MESH)
    pl.semaphore_signal(barrier, inc=1, device_id={"span": partner}, device_id_type=pl.DeviceIdType.MESH)
    ends = jnp.logical_or(first_dev, last_dev)

    @pl.when(ends)
    def _():
        pl.semaphore_wait(barrier, 2)

    @pl.when(jnp.logical_not(ends))
    def _():
        pl.semaphore_wait(barrier, 3)

    lend_cols = pl.ds(first_cols, lend * width)
    small_refs = (types_ref, coeff_ref, scale_ref, inverse_ref)

    def lend_copies():
        copies = [pltpu.make_async_remote_copy(
            src_ref=start_ref.at[:, :, :, lend_cols], dst_ref=ext_start, send_sem=lend_sems.at[0, 0],
            recv_sem=lend_sems.at[1, 0], device_id={"span": partner}, device_id_type=pl.DeviceIdType.MESH)]
        for index, ref in enumerate(small_refs):
            target = ext_types if index == 0 else ext_small.at[index - 1]
            copies.append(pltpu.make_async_remote_copy(
                src_ref=ref.at[:, lend_cols], dst_ref=target, send_sem=lend_sems.at[0, index + 1],
                recv_sem=lend_sems.at[1, index + 1], device_id={"span": partner},
                device_id_type=pl.DeviceIdType.MESH))
        return copies

    @pl.when(lender)
    def _():
        for copy in lend_copies():
            copy.start()

    def copy_f(k):
        return pltpu.make_async_remote_copy(
            src_ref=send_f.at[k], dst_ref=recv_f.at[k], send_sem=sems.at[0, k], recv_sem=sems.at[1, k],
            device_id={"stream": me + 1}, device_id_type=pl.DeviceIdType.MESH)

    def copy_b(k):
        return pltpu.make_async_remote_copy(
            src_ref=send_b.at[k], dst_ref=recv_b.at[k], send_sem=sems.at[2, k], recv_sem=sems.at[3, k],
            device_id={"stream": me - 1}, device_id_type=pl.DeviceIdType.MESH)

    def copy_back(j):
        tracer = j % sets
        cols = pl.ds(pl.multiple_of((j // sets) * width, width), width)
        return pltpu.make_async_remote_copy(
            src_ref=ext_out.at[:, tracer, :, cols], dst_ref=returned.at[:, tracer, :, cols],
            send_sem=back_sems.at[0, j], recv_sem=back_sems.at[1, j], device_id={"span": partner},
            device_id_type=pl.DeviceIdType.MESH)

    def forward_rows(k, tracer, cols, start, small, part):
        @pl.when(jnp.logical_not(first_dev))
        def _():
            copy_f(k).wait_recv()

        state = recv_f[k]
        for row in range(rows):
            types = small(0)[pl.ds(row, 1), cols]
            coeff = small(1)[pl.ds(row, 1), cols]
            state = start[row, tracer, :, cols] - coeff * kernel_masked(up_ref, types, state)
            part[row, tracer, :, cols] = state
        send_f[k] = state

        @pl.when(jnp.logical_not(last_dev))
        def _():
            copy_f(k).start()

    def backward_rows(k, tracer, cols, small, part, out):
        @pl.when(jnp.logical_not(last_dev))
        def _():
            copy_b(k).wait_recv()

        state = recv_b[k]
        for row in range(rows - 1, -1, -1):
            types = small(0)[pl.ds(row, 1), cols]
            scale = small(2)[pl.ds(row, 1), cols]
            solved = part[row, tracer, :, cols] - state * small(3)[pl.ds(row, 1), cols]
            out[row, tracer, :, cols] = solved
            state = scale * kernel_masked(down_ref, types, solved)
        send_b[k] = state

        @pl.when(jnp.logical_not(first_dev))
        def _():
            copy_b(k).start()

    def own_small(index):
        return small_refs[index]

    def ext_small_ref(index):
        return ext_types if index == 0 else ext_small.at[index - 1]

    def place(k):
        return k % sets, pl.ds(pl.multiple_of((k // sets) * width, width), width)

    def forward_block(k):
        @pl.when(k < own)
        def _():
            tracer, cols = place(k)
            forward_rows(k, tracer, cols, start_ref, own_small, part_ref)

        @pl.when(k == own)
        def _():
            for copy in lend_copies():
                copy.wait_recv()

        @pl.when(k >= own)
        def _():
            tracer, cols = place(k - own)
            forward_rows(k, tracer, cols, ext_start, ext_small_ref, ext_part)

    def backward_block(k):
        @pl.when(k < own)
        def _():
            tracer, cols = place(k)
            backward_rows(k, tracer, cols, own_small, part_ref, out_ref)

        @pl.when(k >= own)
        def _():
            tracer, cols = place(k - own)
            backward_rows(k, tracer, cols, ext_small_ref, ext_part, ext_out)
            copy_back(k - own).start()

    lead = jnp.minimum(jnp.maximum((2 * (length - 1) - 2 * me) * 4, 1), count)
    tail = 2 * count - lead

    def step(s, carry):
        paired = jnp.logical_and(s >= lead, s < tail)
        odd = (s - lead) % 2 == 1

        @pl.when(s < lead)
        def _():
            forward_block(s)

        @pl.when(jnp.logical_and(paired, odd))
        def _():
            forward_block(lead + (s - lead) // 2)

        @pl.when(jnp.logical_and(paired, jnp.logical_not(odd)))
        def _():
            backward_block((s - lead) // 2)

        @pl.when(s >= tail)
        def _():
            backward_block(s - count)

        return carry

    lax.fori_loop(0, 2 * count, step, 0)

    def drain_f(k, carry):
        copy_f(k).wait_send()
        return carry

    def drain_b(k, carry):
        copy_b(k).wait_send()
        return carry

    @pl.when(jnp.logical_not(last_dev))
    def _():
        lax.fori_loop(0, count, drain_f, 0)

    @pl.when(jnp.logical_not(first_dev))
    def _():
        lax.fori_loop(0, count, drain_b, 0)

    def drain_back(j, carry):
        copy_back(j).wait_send()
        return carry

    def take_back(j, carry):
        copy_back(j).wait_recv()
        return carry

    @pl.when(lender)
    def _():
        for copy in lend_copies():
            copy.wait_send()
        lax.fori_loop(0, lent, take_back, 0)
        out_ref[:, :, :, lend_cols] = returned[...]

    @pl.when(jnp.logical_not(lender))
    def _():
        lax.fori_loop(0, lent, drain_back, 0)


def both_sweeps(width, start, types, coeff, scale, inverse, up_table, down_table):
    rows, tracers, dof, columns = start.shape
    groups = columns // width
    lend = max(1, groups * 5 // 8)
    blocks = tracers * (groups + lend)
    lent = tracers * lend
    length = lax.axis_size("stream")
    vmem = pltpu.VMEM
    ext_shape = (rows, tracers, dof, lend * width)
    return pl.pallas_call(
        functools.partial(both_kernel, length, width, lend),
        out_shape=jax.ShapeDtypeStruct(start.shape, jnp.float32),
        in_specs=[pl.BlockSpec(memory_space=vmem)] * 7,
        out_specs=pl.BlockSpec(memory_space=vmem),
        scratch_shapes=[
            pltpu.VMEM(start.shape, jnp.float32),
            pltpu.VMEM(ext_shape, jnp.float32),
            pltpu.VMEM((rows, lend * width), jnp.int32),
            pltpu.VMEM((3, rows, lend * width), jnp.float32),
            pltpu.VMEM(ext_shape, jnp.float32),
            pltpu.VMEM(ext_shape, jnp.float32),
            pltpu.VMEM(ext_shape, jnp.float32),
            pltpu.VMEM((blocks, dof, width), jnp.float32),
            pltpu.VMEM((blocks, dof, width), jnp.float32),
            pltpu.VMEM((blocks, dof, width), jnp.float32),
            pltpu.VMEM((blocks, dof, width), jnp.float32),
            pltpu.SemaphoreType.DMA((4, blocks)),
            pltpu.SemaphoreType.DMA((2, 5)),
            pltpu.SemaphoreType.DMA((2, lent)),
        ],
        compiler_params=pltpu.CompilerParams(
            collective_id=0, has_side_effects=True, vmem_limit_bytes=60 * 1024 * 1024
        ),
    )(start, types, coeff, scale, inverse, up_table, down_table)


def per_device(
    rhs, lagged, face_types, stream_scale, span_scale, absorb, up_blocks, down_blocks, diag_inverse
):
    columns = rhs.shape[3]
    dof = up_blocks.shape[1]
    padded = padded_2(lagged, (("span", 3),), 1)
    denominator = stream_scale + span_scale[0] + span_scale[1] + absorb
    span_terms = span_block(padded, face_types, span_scale, up_blocks, 0, columns)
    start = jnp.einsum("pq,nrqc->nrpc", diag_inverse, rhs - span_terms, precision=fast)
    start = start / denominator[:, None, None, :]
    coeff = stream_scale / denominator
    inverse = 1.0 / denominator
    up_table = split_masked_table(jnp.einsum("pq,tqs->tps", diag_inverse, up_blocks, precision=precise))
    down_table = split_masked_table(jnp.einsum("pq,tqs->tps", diag_inverse, down_blocks, precision=precise))
    small = [face_types[0], coeff, stream_scale, inverse]
    return both_sweeps(LANES, start, *small, up_table, down_table)


def solution(mesh):
    return jax.shard_map(
        per_device,
        mesh=mesh,
        in_specs=(
            P("stream", None, None, "span"),
            P("stream", None, None, "span"),
            P(None, "stream", "span"),
            P("stream", "span"),
            P(None, "stream", "span"),
            P("stream", "span"),
            P(),
            P(),
            P(),
        ),
        out_specs=P("stream", None, None, "span"),
        check_vma=False,
    )
```

```python
import functools

import jax
import jax.numpy as jnp
from jax import lax
from jax.experimental import pallas as pl
from jax.experimental.pallas import tpu as pltpu
from jax.sharding import PartitionSpec as P

precise = lax.Precision.HIGHEST
fast = lax.Precision.HIGH
LANES = 128


def padded_2(block, sides, width):
    for axis, dim in sides:
        count = lax.axis_size(axis)
        forward = [(i, i + 1) for i in range(count - 1)]
        backward = [(target, source) for source, target in forward]
        low = lax.ppermute(
            lax.slice_in_dim(block, block.shape[dim] - width, None, axis=dim), axis, forward
        )
        high = lax.ppermute(lax.slice_in_dim(block, 0, width, axis=dim), axis, backward)
        block = jnp.concatenate([low, block, high], axis=dim)
    return block


def typed_product(blocks_table, type_ids, state_in):
    products = jnp.einsum("tpq,rqw->trpw", blocks_table, state_in, precision=fast)
    kinds = jnp.arange(blocks_table.shape[0], dtype=jnp.int32)
    selector = (type_ids[None, :] == kinds[:, None]).astype(jnp.float32)
    return jnp.sum(products * selector[:, None, None, :], axis=0)


def span_block(padded, face_types, span_scale, up_blocks, offset, breadth):
    lower_side = lax.dynamic_slice_in_dim(padded, offset, breadth, 3)
    upper_side = lax.dynamic_slice_in_dim(padded, offset + 2, breadth, 3)
    lower_types = face_types[1]
    upper_types = face_types[2]
    lower_scale = span_scale[0]
    upper_scale = span_scale[1]
    results = []
    for row_index in range(padded.shape[0]):
        lower_term = lower_scale[row_index] * typed_product(
            up_blocks, lower_types[row_index], lower_side[row_index]
        )
        upper_term = upper_scale[row_index] * typed_product(
            up_blocks, upper_types[row_index], upper_side[row_index]
        )
        results.append(lower_term + upper_term)
    return jnp.stack(results)


def split_table(table):
    high = lax.reduce_precision(table, exponent_bits=8, mantissa_bits=7)
    low = table - high
    high = high.astype(jnp.bfloat16)
    low = low.astype(jnp.bfloat16)
    return jnp.concatenate([high, low, high], axis=1)


def split_masked_table(tables):
    kinds, dof, _ = tables.shape
    flat = jnp.transpose(tables, (1, 0, 2)).reshape(dof, kinds * dof)
    high = lax.reduce_precision(flat, exponent_bits=8, mantissa_bits=7)
    low = flat - high
    high = high.astype(jnp.bfloat16)
    low = low.astype(jnp.bfloat16)
    return jnp.concatenate([high, low, high], axis=1)


def kernel_masked(table_ref, types, state):
    dof = state.shape[0]
    kinds = table_ref.shape[1] // (3 * dof)
    high = state.astype(jnp.bfloat16)
    low = (state - high.astype(jnp.float32)).astype(jnp.bfloat16)
    zero = jnp.zeros_like(high)
    masks = [types == kind for kind in range(kinds)]
    highs = [jnp.where(mask, high, zero) for mask in masks]
    lows = [jnp.where(mask, low, zero) for mask in masks]
    stacked = jnp.concatenate(highs + highs + lows, axis=0)
    return jnp.dot(table_ref[...], stacked, preferred_element_type=jnp.float32)


def kernel_typed(table_ref, types, state):
    dof = state.shape[0]
    high = state.astype(jnp.bfloat16)
    low = (state - high.astype(jnp.float32)).astype(jnp.bfloat16)
    stacked = jnp.concatenate([high, high, low], axis=0)
    products = jnp.dot(table_ref[...], stacked, preferred_element_type=jnp.float32)
    picked = products[0:dof]
    for kind in range(1, table_ref.shape[0] // dof):
        picked = jnp.where(types == kind, products[kind * dof:(kind + 1) * dof], picked)
    return picked


def barrier_with_neighbours(me, length):
    barrier = pltpu.get_barrier_semaphore()

    @pl.when(me > 0)
    def _():
        pl.semaphore_signal(barrier, inc=1, device_id={"stream": me - 1},
                            device_id_type=pl.DeviceIdType.MESH)

    @pl.when(me < length - 1)
    def _():
        pl.semaphore_signal(barrier, inc=1, device_id={"stream": me + 1},
                            device_id_type=pl.DeviceIdType.MESH)

    ends = jnp.logical_or(me == 0, me == length - 1)

    @pl.when(ends)
    def _():
        pl.semaphore_wait(barrier, 1)

    @pl.when(jnp.logical_not(ends))
    def _():
        pl.semaphore_wait(barrier, 2)


def sweep_kernel(length, direction, width, grouped, start_ref, types_ref, coeff_ref, denom_ref, table_ref,
                 out_ref, recv_ref, send_ref, send_sem, recv_sem):
    me = lax.axis_index("stream")
    rows, tracers, dof, columns = start_ref.shape
    sets = tracers // grouped
    blocks = sets * (columns // width)
    if direction > 0:
        has_source = me > 0
        has_target = me < length - 1
        target = me + 1
    else:
        has_source = me < length - 1
        has_target = me > 0
        target = me - 1

    @pl.when(jnp.logical_not(has_source))
    def _():
        recv_ref[...] = jnp.zeros(recv_ref.shape, jnp.float32)

    barrier_with_neighbours(me, length)

    def copy_of(k):
        return pltpu.make_async_remote_copy(
            src_ref=send_ref.at[k],
            dst_ref=recv_ref.at[k],
            send_sem=send_sem.at[k],
            recv_sem=recv_sem.at[k],
            device_id={"stream": target},
            device_id_type=pl.DeviceIdType.MESH,
        )

    row_order = list(range(rows)) if direction > 0 else list(range(rows - 1, -1, -1))

    def gathered(ref, row, first, cols):
        return jnp.concatenate([ref[row, first + tracer, :, cols] for tracer in range(grouped)], axis=1)

    def lanes(ref, row, cols):
        return jnp.concatenate([ref[pl.ds(row, 1), cols]] * grouped, axis=1)

    def block_step(k, carry):
        first = (k % sets) * grouped
        cols = pl.ds(pl.multiple_of((k // sets) * width, width), width)

        @pl.when(has_source)
        def _():
            copy_of(k).wait_recv()

        state = recv_ref[k]
        for row in row_order:
            types = lanes(types_ref, row, cols)
            coeff = lanes(coeff_ref, row, cols)
            if direction > 0:
                state = gathered(start_ref, row, first, cols) - coeff * kernel_typed(table_ref, types, state)
                solved = state
            else:
                solved = gathered(start_ref, row, first, cols) - state / lanes(denom_ref, row, cols)
                state = coeff * kernel_typed(table_ref, types, solved)
            for tracer in range(grouped):
                out_ref[row, first + tracer, :, cols] = solved[:, tracer * width:(tracer + 1) * width]
        send_ref[k] = state

        @pl.when(has_target)
        def _():
            copy_of(k).start()

        return carry

    lax.fori_loop(0, blocks, block_step, 0)

    def drain(k, carry):
        copy_of(k).wait_send()
        return carry

    @pl.when(has_target)
    def _():
        lax.fori_loop(0, blocks, drain, 0)


def sweep(direction, collective_id, width, grouped, start, types, coeff, denom, table):
    rows, tracers, dof, columns = start.shape
    blocks = (tracers // grouped) * (columns // width)
    length = lax.axis_size("stream")
    vmem = pltpu.VMEM
    return pl.pallas_call(
        functools.partial(sweep_kernel, length, direction, width, grouped),
        out_shape=jax.ShapeDtypeStruct(start.shape, jnp.float32),
        in_specs=[pl.BlockSpec(memory_space=vmem)] * 5,
        out_specs=pl.BlockSpec(memory_space=vmem),
        scratch_shapes=[
            pltpu.VMEM((blocks, dof, grouped * width), jnp.float32),
            pltpu.VMEM((blocks, dof, grouped * width), jnp.float32),
            pltpu.SemaphoreType.DMA((blocks,)),
            pltpu.SemaphoreType.DMA((blocks,)),
        ],
        compiler_params=pltpu.CompilerParams(
            collective_id=collective_id, has_side_effects=True, vmem_limit_bytes=60 * 1024 * 1024
        ),
    )(start, types, coeff, denom, table)


def both_kernel(length, width, lend, start_ref, types_ref, coeff_ref, scale_ref, inverse_ref, up_ref, down_ref,
                out_ref, part_ref, ext_start, ext_types, ext_small, ext_part, ext_out,
                recv_f, send_f, recv_b, send_b, sems, lend_sems, back_sems):
    me = lax.axis_index("stream")
    side = lax.axis_index("span")
    lender = side % 2 == 0
    partner = side + 1 - 2 * (side % 2)
    rows, tracers, dof, columns = start_ref.shape
    sets = tracers
    own = sets * (columns // width)
    lent = sets * lend
    kept = own - lent
    first_cols = columns - lend * width
    count = jnp.where(lender, kept, own + lent)
    first_dev = me == 0
    last_dev = me == length - 1

    @pl.when(first_dev)
    def _():
        recv_f[...] = jnp.zeros(recv_f.shape, jnp.float32)

    @pl.when(last_dev)
    def _():
        recv_b[...] = jnp.zeros(recv_b.shape, jnp.float32)

    barrier = pltpu.get_barrier_semaphore()
    for target in (me - 1, me + 1):
        @pl.when(jnp.logical_and(target >= 0, target < length))
        def _():
            pl.semaphore_signal(barrier, inc=1, device_id={"stream": target},
                                device_id_type=pl.DeviceIdType.MESH)
    pl.semaphore_signal(barrier, inc=1, device_id={"span": partner}, device_id_type=pl.DeviceIdType.MESH)
    ends = jnp.logical_or(first_dev, last_dev)

    @pl.when(ends)
    def _():
        pl.semaphore_wait(barrier, 2)

    @pl.when(jnp.logical_not(ends))
    def _():
        pl.semaphore_wait(barrier, 3)

    lend_cols = pl.ds(first_cols, lend * width)
    small_refs = (types_ref, coeff_ref, scale_ref, inverse_ref)

    def lend_copies():
        copies = [pltpu.make_async_remote_copy(
            src_ref=start_ref.at[:, :, :, lend_cols], dst_ref=ext_start, send_sem=lend_sems.at[0, 0],
            recv_sem=lend_sems.at[1, 0], device_id={"span": partner}, device_id_type=pl.DeviceIdType.MESH)]
        for index, ref in enumerate(small_refs):
            target = ext_types if index == 0 else ext_small.at[index - 1]
            copies.append(pltpu.make_async_remote_copy(
                src_ref=ref.at[:, lend_cols], dst_ref=target, send_sem=lend_sems.at[0, index + 1],
                recv_sem=lend_sems.at[1, index + 1], device_id={"span": partner},
                device_id_type=pl.DeviceIdType.MESH))
        return copies

    @pl.when(lender)
    def _():
        for copy in lend_copies():
            copy.start()

    def copy_f(k):
        return pltpu.make_async_remote_copy(
            src_ref=send_f.at[k], dst_ref=recv_f.at[k], send_sem=sems.at[0, k], recv_sem=sems.at[1, k],
            device_id={"stream": me + 1}, device_id_type=pl.DeviceIdType.MESH)

    def copy_b(k):
        return pltpu.make_async_remote_copy(
            src_ref=send_b.at[k], dst_ref=recv_b.at[k], send_sem=sems.at[2, k], recv_sem=sems.at[3, k],
            device_id={"stream": me - 1}, device_id_type=pl.DeviceIdType.MESH)

    def copy_back(j):
        tracer = j % sets
        cols = pl.ds(pl.multiple_of((j // sets) * width, width), width)
        home = pl.ds(pl.multiple_of(first_cols + (j // sets) * width, width), width)
        return pltpu.make_async_remote_copy(
            src_ref=ext_out.at[:, tracer, :, cols], dst_ref=out_ref.at[:, tracer, :, home],
            send_sem=back_sems.at[0, j], recv_sem=back_sems.at[1, j], device_id={"span": partner},
            device_id_type=pl.DeviceIdType.MESH)

    def forward_rows(k, tracer, cols, start, small, part):
        @pl.when(jnp.logical_not(first_dev))
        def _():
            copy_f(k).wait_recv()

        state = recv_f[k]
        for row in range(rows):
            types = small(0)[pl.ds(row, 1), cols]
            coeff = small(1)[pl.ds(row, 1), cols]
            state = start[row, tracer, :, cols] - coeff * kernel_masked(up_ref, types, state)
            part[row, tracer, :, cols] = state
        send_f[k] = state

        @pl.when(jnp.logical_not(last_dev))
        def _():
            copy_f(k).start()

    def backward_rows(k, tracer, cols, small, part, out):
        @pl.when(jnp.logical_not(last_dev))
        def _():
            copy_b(k).wait_recv()

        state = recv_b[k]
        for row in range(rows - 1, -1, -1):
            types = small(0)[pl.ds(row, 1), cols]
            scale = small(2)[pl.ds(row, 1), cols]
            solved = part[row, tracer, :, cols] - state * small(3)[pl.ds(row, 1), cols]
            out[row, tracer, :, cols] = solved
            state = scale * kernel_masked(down_ref, types, solved)
        send_b[k] = state

        @pl.when(jnp.logical_not(first_dev))
        def _():
            copy_b(k).start()

    def own_small(index):
        return small_refs[index]

    def ext_small_ref(index):
        return ext_types if index == 0 else ext_small.at[index - 1]

    def place(k):
        return k % sets, pl.ds(pl.multiple_of((k // sets) * width, width), width)

    def forward_block(k):
        @pl.when(k < own)
        def _():
            tracer, cols = place(k)
            forward_rows(k, tracer, cols, start_ref, own_small, part_ref)

        @pl.when(k == own)
        def _():
            for copy in lend_copies():
                copy.wait_recv()

        @pl.when(k >= own)
        def _():
            tracer, cols = place(k - own)
            forward_rows(k, tracer, cols, ext_start, ext_small_ref, ext_part)

    def backward_block(k):
        @pl.when(k < own)
        def _():
            tracer, cols = place(k)
            backward_rows(k, tracer, cols, own_small, part_ref, out_ref)

        @pl.when(k >= own)
        def _():
            tracer, cols = place(k - own)
            backward_rows(k, tracer, cols, ext_small_ref, ext_part, ext_out)
            copy_back(k - own).start()

    lead = jnp.minimum(jnp.maximum((2 * (length - 1) - 2 * me) * 4, 1), count)
    tail = 2 * count - lead

    def step(s, carry):
        paired = jnp.logical_and(s >= lead, s < tail)
        odd = (s - lead) % 2 == 1

        @pl.when(s < lead)
        def _():
            forward_block(s)

        @pl.when(jnp.logical_and(paired, odd))
        def _():
            forward_block(lead + (s - lead) // 2)

        @pl.when(jnp.logical_and(paired, jnp.logical_not(odd)))
        def _():
            backward_block((s - lead) // 2)

        @pl.when(s >= tail)
        def _():
            backward_block(s - count)

        return carry

    lax.fori_loop(0, 2 * count, step, 0)

    def drain_f(k, carry):
        copy_f(k).wait_send()
        return carry

    def drain_b(k, carry):
        copy_b(k).wait_send()
        return carry

    @pl.when(jnp.logical_not(last_dev))
    def _():
        lax.fori_loop(0, count, drain_f, 0)

    @pl.when(jnp.logical_not(first_dev))
    def _():
        lax.fori_loop(0, count, drain_b, 0)

    def drain_back(j, carry):
        copy_back(j).wait_send()
        return carry

    def take_back(j, carry):
        copy_back(j).wait_recv()
        return carry

    @pl.when(lender)
    def _():
        for copy in lend_copies():
            copy.wait_send()
        lax.fori_loop(0, lent, take_back, 0)

    @pl.when(jnp.logical_not(lender))
    def _():
        lax.fori_loop(0, lent, drain_back, 0)


def both_sweeps(width, start, types, coeff, scale, inverse, up_table, down_table):
    rows, tracers, dof, columns = start.shape
    groups = columns // width
    lend = max(1, groups * 5 // 8)
    blocks = tracers * (groups + lend)
    lent = tracers * lend
    length = lax.axis_size("stream")
    vmem = pltpu.VMEM
    ext_shape = (rows, tracers, dof, lend * width)
    return pl.pallas_call(
        functools.partial(both_kernel, length, width, lend),
        out_shape=jax.ShapeDtypeStruct(start.shape, jnp.float32),
        in_specs=[pl.BlockSpec(memory_space=vmem)] * 7,
        out_specs=pl.BlockSpec(memory_space=vmem),
        scratch_shapes=[
            pltpu.VMEM(start.shape, jnp.float32),
            pltpu.VMEM(ext_shape, jnp.float32),
            pltpu.VMEM((rows, lend * width), jnp.int32),
            pltpu.VMEM((3, rows, lend * width), jnp.float32),
            pltpu.VMEM(ext_shape, jnp.float32),
            pltpu.VMEM(ext_shape, jnp.float32),
            pltpu.VMEM((blocks, dof, width), jnp.float32),
            pltpu.VMEM((blocks, dof, width), jnp.float32),
            pltpu.VMEM((blocks, dof, width), jnp.float32),
            pltpu.VMEM((blocks, dof, width), jnp.float32),
            pltpu.SemaphoreType.DMA((4, blocks)),
            pltpu.SemaphoreType.DMA((2, 5)),
            pltpu.SemaphoreType.DMA((2, lent)),
        ],
        compiler_params=pltpu.CompilerParams(
            collective_id=0, has_side_effects=True, vmem_limit_bytes=60 * 1024 * 1024
        ),
    )(start, types, coeff, scale, inverse, up_table, down_table)


def per_device(
    rhs, lagged, face_types, stream_scale, span_scale, absorb, up_blocks, down_blocks, diag_inverse
):
    columns = rhs.shape[3]
    dof = up_blocks.shape[1]
    padded = padded_2(lagged, (("span", 3),), 1)
    denominator = stream_scale + span_scale[0] + span_scale[1] + absorb
    span_terms = span_block(padded, face_types, span_scale, up_blocks, 0, columns)
    start = jnp.einsum("pq,nrqc->nrpc", diag_inverse, rhs - span_terms, precision=fast)
    start = start / denominator[:, None, None, :]
    coeff = stream_scale / denominator
    inverse = 1.0 / denominator
    up_table = split_masked_table(jnp.einsum("pq,tqs->tps", diag_inverse, up_blocks, precision=precise))
    down_table = split_masked_table(jnp.einsum("pq,tqs->tps", diag_inverse, down_blocks, precision=precise))
    small = [face_types[0], coeff, stream_scale, inverse]
    return both_sweeps(LANES, start, *small, up_table, down_table)


def solution(mesh):
    return jax.shard_map(
        per_device,
        mesh=mesh,
        in_specs=(
            P("stream", None, None, "span"),
            P("stream", None, None, "span"),
            P(None, "stream", "span"),
            P("stream", "span"),
            P(None, "stream", "span"),
            P("stream", "span"),
            P(),
            P(),
            P(),
        ),
        out_specs=P("stream", None, None, "span"),
        check_vma=False,
    )
```

```python
import functools

import jax
import jax.numpy as jnp
from jax import lax
from jax.experimental import pallas as pl
from jax.experimental.pallas import tpu as pltpu
from jax.sharding import PartitionSpec as P

precise = lax.Precision.HIGHEST
fast = lax.Precision.HIGH
LANES = 128


def padded_2(block, sides, width):
    for axis, dim in sides:
        count = lax.axis_size(axis)
        forward = [(i, i + 1) for i in range(count - 1)]
        backward = [(target, source) for source, target in forward]
        low = lax.ppermute(
            lax.slice_in_dim(block, block.shape[dim] - width, None, axis=dim), axis, forward
        )
        high = lax.ppermute(lax.slice_in_dim(block, 0, width, axis=dim), axis, backward)
        block = jnp.concatenate([low, block, high], axis=dim)
    return block


def typed_product(blocks_table, type_ids, state_in):
    products = jnp.einsum("tpq,rqw->trpw", blocks_table, state_in, precision=fast)
    kinds = jnp.arange(blocks_table.shape[0], dtype=jnp.int32)
    selector = (type_ids[None, :] == kinds[:, None]).astype(jnp.float32)
    return jnp.sum(products * selector[:, None, None, :], axis=0)


def span_block(padded, face_types, span_scale, up_blocks, offset, breadth):
    lower_side = lax.dynamic_slice_in_dim(padded, offset, breadth, 3)
    upper_side = lax.dynamic_slice_in_dim(padded, offset + 2, breadth, 3)
    lower_types = face_types[1]
    upper_types = face_types[2]
    lower_scale = span_scale[0]
    upper_scale = span_scale[1]
    results = []
    for row_index in range(padded.shape[0]):
        lower_term = lower_scale[row_index] * typed_product(
            up_blocks, lower_types[row_index], lower_side[row_index]
        )
        upper_term = upper_scale[row_index] * typed_product(
            up_blocks, upper_types[row_index], upper_side[row_index]
        )
        results.append(lower_term + upper_term)
    return jnp.stack(results)


def split_table(table):
    high = lax.reduce_precision(table, exponent_bits=8, mantissa_bits=7)
    low = table - high
    high = high.astype(jnp.bfloat16)
    low = low.astype(jnp.bfloat16)
    return jnp.concatenate([high, low, high], axis=1)


def split_masked_table(tables):
    kinds, dof, _ = tables.shape
    flat = jnp.transpose(tables, (1, 0, 2)).reshape(dof, kinds * dof)
    high = lax.reduce_precision(flat, exponent_bits=8, mantissa_bits=7)
    low = flat - high
    high = high.astype(jnp.bfloat16)
    low = low.astype(jnp.bfloat16)
    return jnp.concatenate([high, low, high], axis=1)


def kernel_masked(table_ref, types, state):
    dof = state.shape[0]
    kinds = table_ref.shape[1] // (3 * dof)
    high = state.astype(jnp.bfloat16)
    low = (state - high.astype(jnp.float32)).astype(jnp.bfloat16)
    zero = jnp.zeros_like(high)
    masks = [types == kind for kind in range(kinds)]
    highs = [jnp.where(mask, high, zero) for mask in masks]
    lows = [jnp.where(mask, low, zero) for mask in masks]
    stacked = jnp.concatenate(highs + highs + lows, axis=0)
    return jnp.dot(table_ref[...], stacked, preferred_element_type=jnp.float32)


def kernel_typed(table_ref, types, state):
    dof = state.shape[0]
    high = state.astype(jnp.bfloat16)
    low = (state - high.astype(jnp.float32)).astype(jnp.bfloat16)
    stacked = jnp.concatenate([high, high, low], axis=0)
    products = jnp.dot(table_ref[...], stacked, preferred_element_type=jnp.float32)
    picked = products[0:dof]
    for kind in range(1, table_ref.shape[0] // dof):
        picked = jnp.where(types == kind, products[kind * dof:(kind + 1) * dof], picked)
    return picked


def barrier_with_neighbours(me, length):
    barrier = pltpu.get_barrier_semaphore()

    @pl.when(me > 0)
    def _():
        pl.semaphore_signal(barrier, inc=1, device_id={"stream": me - 1},
                            device_id_type=pl.DeviceIdType.MESH)

    @pl.when(me < length - 1)
    def _():
        pl.semaphore_signal(barrier, inc=1, device_id={"stream": me + 1},
                            device_id_type=pl.DeviceIdType.MESH)

    ends = jnp.logical_or(me == 0, me == length - 1)

    @pl.when(ends)
    def _():
        pl.semaphore_wait(barrier, 1)

    @pl.when(jnp.logical_not(ends))
    def _():
        pl.semaphore_wait(barrier, 2)


def sweep_kernel(length, direction, width, grouped, start_ref, types_ref, coeff_ref, denom_ref, table_ref,
                 out_ref, recv_ref, send_ref, send_sem, recv_sem):
    me = lax.axis_index("stream")
    rows, tracers, dof, columns = start_ref.shape
    sets = tracers // grouped
    blocks = sets * (columns // width)
    if direction > 0:
        has_source = me > 0
        has_target = me < length - 1
        target = me + 1
    else:
        has_source = me < length - 1
        has_target = me > 0
        target = me - 1

    @pl.when(jnp.logical_not(has_source))
    def _():
        recv_ref[...] = jnp.zeros(recv_ref.shape, jnp.float32)

    barrier_with_neighbours(me, length)

    def copy_of(k):
        return pltpu.make_async_remote_copy(
            src_ref=send_ref.at[k],
            dst_ref=recv_ref.at[k],
            send_sem=send_sem.at[k],
            recv_sem=recv_sem.at[k],
            device_id={"stream": target},
            device_id_type=pl.DeviceIdType.MESH,
        )

    row_order = list(range(rows)) if direction > 0 else list(range(rows - 1, -1, -1))

    def gathered(ref, row, first, cols):
        return jnp.concatenate([ref[row, first + tracer, :, cols] for tracer in range(grouped)], axis=1)

    def lanes(ref, row, cols):
        return jnp.concatenate([ref[pl.ds(row, 1), cols]] * grouped, axis=1)

    def block_step(k, carry):
        first = (k % sets) * grouped
        cols = pl.ds(pl.multiple_of((k // sets) * width, width), width)

        @pl.when(has_source)
        def _():
            copy_of(k).wait_recv()

        state = recv_ref[k]
        for row in row_order:
            types = lanes(types_ref, row, cols)
            coeff = lanes(coeff_ref, row, cols)
            if direction > 0:
                state = gathered(start_ref, row, first, cols) - coeff * kernel_typed(table_ref, types, state)
                solved = state
            else:
                solved = gathered(start_ref, row, first, cols) - state / lanes(denom_ref, row, cols)
                state = coeff * kernel_typed(table_ref, types, solved)
            for tracer in range(grouped):
                out_ref[row, first + tracer, :, cols] = solved[:, tracer * width:(tracer + 1) * width]
        send_ref[k] = state

        @pl.when(has_target)
        def _():
            copy_of(k).start()

        return carry

    lax.fori_loop(0, blocks, block_step, 0)

    def drain(k, carry):
        copy_of(k).wait_send()
        return carry

    @pl.when(has_target)
    def _():
        lax.fori_loop(0, blocks, drain, 0)


def sweep(direction, collective_id, width, grouped, start, types, coeff, denom, table):
    rows, tracers, dof, columns = start.shape
    blocks = (tracers // grouped) * (columns // width)
    length = lax.axis_size("stream")
    vmem = pltpu.VMEM
    return pl.pallas_call(
        functools.partial(sweep_kernel, length, direction, width, grouped),
        out_shape=jax.ShapeDtypeStruct(start.shape, jnp.float32),
        in_specs=[pl.BlockSpec(memory_space=vmem)] * 5,
        out_specs=pl.BlockSpec(memory_space=vmem),
        scratch_shapes=[
            pltpu.VMEM((blocks, dof, grouped * width), jnp.float32),
            pltpu.VMEM((blocks, dof, grouped * width), jnp.float32),
            pltpu.SemaphoreType.DMA((blocks,)),
            pltpu.SemaphoreType.DMA((blocks,)),
        ],
        compiler_params=pltpu.CompilerParams(
            collective_id=collective_id, has_side_effects=True, vmem_limit_bytes=60 * 1024 * 1024
        ),
    )(start, types, coeff, denom, table)


def both_kernel(length, width, lend, start_ref, faces_ref, coeff_ref, scale_ref, inverse_ref, tables_ref,
                out_ref, part_ref, ext_start, ext_types, ext_small, ext_part, ext_out,
                recv_f, send_f, recv_b, send_b, sems, lend_sems, back_sems):
    types_ref = faces_ref.at[0]
    half = tables_ref.shape[1] // 2
    up_ref = tables_ref.at[:, pl.ds(0, half)]
    down_ref = tables_ref.at[:, pl.ds(half, half)]
    me = lax.axis_index("stream")
    side = lax.axis_index("span")
    lender = side % 2 == 0
    partner = side + 1 - 2 * (side % 2)
    rows, tracers, dof, columns = start_ref.shape
    sets = tracers
    own = sets * (columns // width)
    lent = sets * lend
    kept = own - lent
    first_cols = columns - lend * width
    count = jnp.where(lender, kept, own + lent)
    first_dev = me == 0
    last_dev = me == length - 1

    @pl.when(first_dev)
    def _():
        recv_f[...] = jnp.zeros(recv_f.shape, jnp.float32)

    @pl.when(last_dev)
    def _():
        recv_b[...] = jnp.zeros(recv_b.shape, jnp.float32)

    barrier = pltpu.get_barrier_semaphore()
    for target in (me - 1, me + 1):
        @pl.when(jnp.logical_and(target >= 0, target < length))
        def _():
            pl.semaphore_signal(barrier, inc=1, device_id={"stream": target},
                                device_id_type=pl.DeviceIdType.MESH)
    pl.semaphore_signal(barrier, inc=1, device_id={"span": partner}, device_id_type=pl.DeviceIdType.MESH)
    ends = jnp.logical_or(first_dev, last_dev)

    @pl.when(ends)
    def _():
        pl.semaphore_wait(barrier, 2)

    @pl.when(jnp.logical_not(ends))
    def _():
        pl.semaphore_wait(barrier, 3)

    lend_cols = pl.ds(first_cols, lend * width)
    small_refs = (types_ref, coeff_ref, scale_ref, inverse_ref)

    def lend_copies():
        copies = [pltpu.make_async_remote_copy(
            src_ref=start_ref.at[:, :, :, lend_cols], dst_ref=ext_start, send_sem=lend_sems.at[0, 0],
            recv_sem=lend_sems.at[1, 0], device_id={"span": partner}, device_id_type=pl.DeviceIdType.MESH)]
        for index, ref in enumerate(small_refs):
            target = ext_types if index == 0 else ext_small.at[index - 1]
            copies.append(pltpu.make_async_remote_copy(
                src_ref=ref.at[:, lend_cols], dst_ref=target, send_sem=lend_sems.at[0, index + 1],
                recv_sem=lend_sems.at[1, index + 1], device_id={"span": partner},
                device_id_type=pl.DeviceIdType.MESH))
        return copies

    @pl.when(lender)
    def _():
        for copy in lend_copies():
            copy.start()

    def copy_f(k):
        return pltpu.make_async_remote_copy(
            src_ref=send_f.at[k], dst_ref=recv_f.at[k], send_sem=sems.at[0, k], recv_sem=sems.at[1, k],
            device_id={"stream": me + 1}, device_id_type=pl.DeviceIdType.MESH)

    def copy_b(k):
        return pltpu.make_async_remote_copy(
            src_ref=send_b.at[k], dst_ref=recv_b.at[k], send_sem=sems.at[2, k], recv_sem=sems.at[3, k],
            device_id={"stream": me - 1}, device_id_type=pl.DeviceIdType.MESH)

    def copy_back(j):
        tracer = j % sets
        cols = pl.ds(pl.multiple_of((j // sets) * width, width), width)
        home = pl.ds(pl.multiple_of(first_cols + (j // sets) * width, width), width)
        return pltpu.make_async_remote_copy(
            src_ref=ext_out.at[:, tracer, :, cols], dst_ref=out_ref.at[:, tracer, :, home],
            send_sem=back_sems.at[0, j], recv_sem=back_sems.at[1, j], device_id={"span": partner},
            device_id_type=pl.DeviceIdType.MESH)

    def forward_rows(k, tracer, cols, start, small, part):
        @pl.when(jnp.logical_not(first_dev))
        def _():
            copy_f(k).wait_recv()

        state = recv_f[k]
        for row in range(rows):
            types = small(0)[pl.ds(row, 1), cols]
            coeff = small(1)[pl.ds(row, 1), cols]
            state = start[row, tracer, :, cols] - coeff * kernel_masked(up_ref, types, state)
            part[row, tracer, :, cols] = state
        send_f[k] = state

        @pl.when(jnp.logical_not(last_dev))
        def _():
            copy_f(k).start()

    def backward_rows(k, tracer, cols, small, part, out):
        @pl.when(jnp.logical_not(last_dev))
        def _():
            copy_b(k).wait_recv()

        state = recv_b[k]
        for row in range(rows - 1, -1, -1):
            types = small(0)[pl.ds(row, 1), cols]
            scale = small(2)[pl.ds(row, 1), cols]
            solved = part[row, tracer, :, cols] - state * small(3)[pl.ds(row, 1), cols]
            out[row, tracer, :, cols] = solved
            state = scale * kernel_masked(down_ref, types, solved)
        send_b[k] = state

        @pl.when(jnp.logical_not(first_dev))
        def _():
            copy_b(k).start()

    def own_small(index):
        return small_refs[index]

    def ext_small_ref(index):
        return ext_types if index == 0 else ext_small.at[index - 1]

    def place(k):
        return k % sets, pl.ds(pl.multiple_of((k // sets) * width, width), width)

    def forward_block(k):
        @pl.when(k < own)
        def _():
            tracer, cols = place(k)
            forward_rows(k, tracer, cols, start_ref, own_small, part_ref)

        @pl.when(k == own)
        def _():
            for copy in lend_copies():
                copy.wait_recv()

        @pl.when(k >= own)
        def _():
            tracer, cols = place(k - own)
            forward_rows(k, tracer, cols, ext_start, ext_small_ref, ext_part)

    def backward_block(k):
        @pl.when(k < own)
        def _():
            tracer, cols = place(k)
            backward_rows(k, tracer, cols, own_small, part_ref, out_ref)

        @pl.when(k >= own)
        def _():
            tracer, cols = place(k - own)
            backward_rows(k, tracer, cols, ext_small_ref, ext_part, ext_out)
            copy_back(k - own).start()

    lead = jnp.minimum(jnp.maximum((2 * (length - 1) - 2 * me) * 4, 1), count)
    tail = 2 * count - lead

    def step(s, carry):
        paired = jnp.logical_and(s >= lead, s < tail)
        odd = (s - lead) % 2 == 1

        @pl.when(s < lead)
        def _():
            forward_block(s)

        @pl.when(jnp.logical_and(paired, odd))
        def _():
            forward_block(lead + (s - lead) // 2)

        @pl.when(jnp.logical_and(paired, jnp.logical_not(odd)))
        def _():
            backward_block((s - lead) // 2)

        @pl.when(s >= tail)
        def _():
            backward_block(s - count)

        return carry

    lax.fori_loop(0, 2 * count, step, 0)

    def drain_f(k, carry):
        copy_f(k).wait_send()
        return carry

    def drain_b(k, carry):
        copy_b(k).wait_send()
        return carry

    @pl.when(jnp.logical_not(last_dev))
    def _():
        lax.fori_loop(0, count, drain_f, 0)

    @pl.when(jnp.logical_not(first_dev))
    def _():
        lax.fori_loop(0, count, drain_b, 0)

    def drain_back(j, carry):
        copy_back(j).wait_send()
        return carry

    def take_back(j, carry):
        copy_back(j).wait_recv()
        return carry

    @pl.when(lender)
    def _():
        for copy in lend_copies():
            copy.wait_send()
        lax.fori_loop(0, lent, take_back, 0)

    @pl.when(jnp.logical_not(lender))
    def _():
        lax.fori_loop(0, lent, drain_back, 0)


def both_sweeps(width, start, types, coeff, scale, inverse, tables):
    rows, tracers, dof, columns = start.shape
    groups = columns // width
    lend = max(1, groups * 5 // 8)
    blocks = tracers * (groups + lend)
    lent = tracers * lend
    length = lax.axis_size("stream")
    vmem = pltpu.VMEM
    ext_shape = (rows, tracers, dof, lend * width)
    return pl.pallas_call(
        functools.partial(both_kernel, length, width, lend),
        out_shape=jax.ShapeDtypeStruct(start.shape, jnp.float32),
        in_specs=[pl.BlockSpec(memory_space=vmem)] * 6,
        out_specs=pl.BlockSpec(memory_space=vmem),
        scratch_shapes=[
            pltpu.VMEM(start.shape, jnp.float32),
            pltpu.VMEM(ext_shape, jnp.float32),
            pltpu.VMEM((rows, lend * width), jnp.int32),
            pltpu.VMEM((3, rows, lend * width), jnp.float32),
            pltpu.VMEM(ext_shape, jnp.float32),
            pltpu.VMEM(ext_shape, jnp.float32),
            pltpu.VMEM((blocks, dof, width), jnp.float32),
            pltpu.VMEM((blocks, dof, width), jnp.float32),
            pltpu.VMEM((blocks, dof, width), jnp.float32),
            pltpu.VMEM((blocks, dof, width), jnp.float32),
            pltpu.SemaphoreType.DMA((4, blocks)),
            pltpu.SemaphoreType.DMA((2, 5)),
            pltpu.SemaphoreType.DMA((2, lent)),
        ],
        compiler_params=pltpu.CompilerParams(
            collective_id=0, has_side_effects=True, vmem_limit_bytes=60 * 1024 * 1024
        ),
    )(start, types, coeff, scale, inverse, tables)


def per_device(
    rhs, lagged, face_types, stream_scale, span_scale, absorb, up_blocks, down_blocks, diag_inverse
):
    columns = rhs.shape[3]
    dof = up_blocks.shape[1]
    padded = padded_2(lagged, (("span", 3),), 1)
    denominator = stream_scale + span_scale[0] + span_scale[1] + absorb
    span_terms = span_block(padded, face_types, span_scale, up_blocks, 0, columns)
    start = jnp.einsum("pq,nrqc->nrpc", diag_inverse, rhs - span_terms, precision=fast)
    start = start / denominator[:, None, None, :]
    coeff = stream_scale / denominator
    inverse = 1.0 / denominator
    both = jnp.einsum("pq,tqs->tps", diag_inverse, jnp.concatenate([up_blocks, down_blocks]), precision=precise)
    kinds = up_blocks.shape[0]
    flat = jnp.transpose(both, (1, 0, 2)).reshape(dof, 2 * kinds * dof)
    high = lax.reduce_precision(flat, exponent_bits=8, mantissa_bits=7)
    low = (flat - high).astype(jnp.bfloat16)
    high = high.astype(jnp.bfloat16)
    width = kinds * dof
    pieces = []
    for part in (slice(0, width), slice(width, 2 * width)):
        pieces += [high[:, part], low[:, part], high[:, part]]
    tables = jnp.concatenate(pieces, axis=1)
    small = [face_types, coeff, stream_scale, inverse]
    return both_sweeps(LANES, start, *small, tables)


def solution(mesh):
    return jax.shard_map(
        per_device,
        mesh=mesh,
        in_specs=(
            P("stream", None, None, "span"),
            P("stream", None, None, "span"),
            P(None, "stream", "span"),
            P("stream", "span"),
            P(None, "stream", "span"),
            P("stream", "span"),
            P(),
            P(),
            P(),
        ),
        out_specs=P("stream", None, None, "span"),
        check_vma=False,
    )
```

```python
import functools

import jax
import jax.numpy as jnp
from jax import lax
from jax.experimental import pallas as pl
from jax.experimental.pallas import tpu as pltpu
from jax.sharding import PartitionSpec as P

precise = lax.Precision.HIGHEST
fast = lax.Precision.HIGH
LANES = 128


def padded_2(block, sides, width):
    for axis, dim in sides:
        count = lax.axis_size(axis)
        forward = [(i, i + 1) for i in range(count - 1)]
        backward = [(target, source) for source, target in forward]
        low = lax.ppermute(
            lax.slice_in_dim(block, block.shape[dim] - width, None, axis=dim), axis, forward
        )
        high = lax.ppermute(lax.slice_in_dim(block, 0, width, axis=dim), axis, backward)
        block = jnp.concatenate([low, block, high], axis=dim)
    return block


def typed_product(blocks_table, type_ids, state_in):
    products = jnp.einsum("tpq,rqw->trpw", blocks_table, state_in, precision=fast)
    kinds = jnp.arange(blocks_table.shape[0], dtype=jnp.int32)
    selector = (type_ids[None, :] == kinds[:, None]).astype(jnp.float32)
    return jnp.sum(products * selector[:, None, None, :], axis=0)


def span_block(padded, face_types, span_scale, up_blocks, offset, breadth):
    lower_side = lax.dynamic_slice_in_dim(padded, offset, breadth, 3)
    upper_side = lax.dynamic_slice_in_dim(padded, offset + 2, breadth, 3)
    lower_types = face_types[1]
    upper_types = face_types[2]
    lower_scale = span_scale[0]
    upper_scale = span_scale[1]
    results = []
    for row_index in range(padded.shape[0]):
        lower_term = lower_scale[row_index] * typed_product(
            up_blocks, lower_types[row_index], lower_side[row_index]
        )
        upper_term = upper_scale[row_index] * typed_product(
            up_blocks, upper_types[row_index], upper_side[row_index]
        )
        results.append(lower_term + upper_term)
    return jnp.stack(results)


def split_table(table):
    high = lax.reduce_precision(table, exponent_bits=8, mantissa_bits=7)
    low = table - high
    high = high.astype(jnp.bfloat16)
    low = low.astype(jnp.bfloat16)
    return jnp.concatenate([high, low, high], axis=1)


def split_masked_table(tables):
    kinds, dof, _ = tables.shape
    flat = jnp.transpose(tables, (1, 0, 2)).reshape(dof, kinds * dof)
    high = lax.reduce_precision(flat, exponent_bits=8, mantissa_bits=7)
    low = flat - high
    high = high.astype(jnp.bfloat16)
    low = low.astype(jnp.bfloat16)
    return jnp.concatenate([high, low, high], axis=1)


def kernel_masked(table_ref, types, state):
    dof = state.shape[0]
    kinds = table_ref.shape[1] // (3 * dof)
    high = state.astype(jnp.bfloat16)
    low = (state - high.astype(jnp.float32)).astype(jnp.bfloat16)
    zero = jnp.zeros_like(high)
    masks = [types == kind for kind in range(kinds)]
    highs = [jnp.where(mask, high, zero) for mask in masks]
    lows = [jnp.where(mask, low, zero) for mask in masks]
    stacked = jnp.concatenate(highs + highs + lows, axis=0)
    return jnp.dot(table_ref[...], stacked, preferred_element_type=jnp.float32)


def kernel_typed(table_ref, types, state):
    dof = state.shape[0]
    high = state.astype(jnp.bfloat16)
    low = (state - high.astype(jnp.float32)).astype(jnp.bfloat16)
    stacked = jnp.concatenate([high, high, low], axis=0)
    products = jnp.dot(table_ref[...], stacked, preferred_element_type=jnp.float32)
    picked = products[0:dof]
    for kind in range(1, table_ref.shape[0] // dof):
        picked = jnp.where(types == kind, products[kind * dof:(kind + 1) * dof], picked)
    return picked


def barrier_with_neighbours(me, length):
    barrier = pltpu.get_barrier_semaphore()

    @pl.when(me > 0)
    def _():
        pl.semaphore_signal(barrier, inc=1, device_id={"stream": me - 1},
                            device_id_type=pl.DeviceIdType.MESH)

    @pl.when(me < length - 1)
    def _():
        pl.semaphore_signal(barrier, inc=1, device_id={"stream": me + 1},
                            device_id_type=pl.DeviceIdType.MESH)

    ends = jnp.logical_or(me == 0, me == length - 1)

    @pl.when(ends)
    def _():
        pl.semaphore_wait(barrier, 1)

    @pl.when(jnp.logical_not(ends))
    def _():
        pl.semaphore_wait(barrier, 2)


def sweep_kernel(length, direction, width, grouped, start_ref, types_ref, coeff_ref, denom_ref, table_ref,
                 out_ref, recv_ref, send_ref, send_sem, recv_sem):
    me = lax.axis_index("stream")
    rows, tracers, dof, columns = start_ref.shape
    sets = tracers // grouped
    blocks = sets * (columns // width)
    if direction > 0:
        has_source = me > 0
        has_target = me < length - 1
        target = me + 1
    else:
        has_source = me < length - 1
        has_target = me > 0
        target = me - 1

    @pl.when(jnp.logical_not(has_source))
    def _():
        recv_ref[...] = jnp.zeros(recv_ref.shape, jnp.float32)

    barrier_with_neighbours(me, length)

    def copy_of(k):
        return pltpu.make_async_remote_copy(
            src_ref=send_ref.at[k],
            dst_ref=recv_ref.at[k],
            send_sem=send_sem.at[k],
            recv_sem=recv_sem.at[k],
            device_id={"stream": target},
            device_id_type=pl.DeviceIdType.MESH,
        )

    row_order = list(range(rows)) if direction > 0 else list(range(rows - 1, -1, -1))

    def gathered(ref, row, first, cols):
        return jnp.concatenate([ref[row, first + tracer, :, cols] for tracer in range(grouped)], axis=1)

    def lanes(ref, row, cols):
        return jnp.concatenate([ref[pl.ds(row, 1), cols]] * grouped, axis=1)

    def block_step(k, carry):
        first = (k % sets) * grouped
        cols = pl.ds(pl.multiple_of((k // sets) * width, width), width)

        @pl.when(has_source)
        def _():
            copy_of(k).wait_recv()

        state = recv_ref[k]
        for row in row_order:
            types = lanes(types_ref, row, cols)
            coeff = lanes(coeff_ref, row, cols)
            if direction > 0:
                state = gathered(start_ref, row, first, cols) - coeff * kernel_typed(table_ref, types, state)
                solved = state
            else:
                solved = gathered(start_ref, row, first, cols) - state / lanes(denom_ref, row, cols)
                state = coeff * kernel_typed(table_ref, types, solved)
            for tracer in range(grouped):
                out_ref[row, first + tracer, :, cols] = solved[:, tracer * width:(tracer + 1) * width]
        send_ref[k] = state

        @pl.when(has_target)
        def _():
            copy_of(k).start()

        return carry

    lax.fori_loop(0, blocks, block_step, 0)

    def drain(k, carry):
        copy_of(k).wait_send()
        return carry

    @pl.when(has_target)
    def _():
        lax.fori_loop(0, blocks, drain, 0)


def sweep(direction, collective_id, width, grouped, start, types, coeff, denom, table):
    rows, tracers, dof, columns = start.shape
    blocks = (tracers // grouped) * (columns // width)
    length = lax.axis_size("stream")
    vmem = pltpu.VMEM
    return pl.pallas_call(
        functools.partial(sweep_kernel, length, direction, width, grouped),
        out_shape=jax.ShapeDtypeStruct(start.shape, jnp.float32),
        in_specs=[pl.BlockSpec(memory_space=vmem)] * 5,
        out_specs=pl.BlockSpec(memory_space=vmem),
        scratch_shapes=[
            pltpu.VMEM((blocks, dof, grouped * width), jnp.float32),
            pltpu.VMEM((blocks, dof, grouped * width), jnp.float32),
            pltpu.SemaphoreType.DMA((blocks,)),
            pltpu.SemaphoreType.DMA((blocks,)),
        ],
        compiler_params=pltpu.CompilerParams(
            collective_id=collective_id, has_side_effects=True, vmem_limit_bytes=60 * 1024 * 1024
        ),
    )(start, types, coeff, denom, table)


def both_kernel(length, width, lend, start_ref, faces_ref, ratios_ref, scale_ref, tables_ref,
                out_ref, part_ref, ext_start, ext_types, ext_small, ext_part, ext_out,
                recv_f, send_f, recv_b, send_b, sems, lend_sems, back_sems):
    types_ref = faces_ref.at[0]
    coeff_ref = ratios_ref.at[0]
    inverse_ref = ratios_ref.at[1]
    half = tables_ref.shape[1] // 2
    up_ref = tables_ref.at[:, pl.ds(0, half)]
    down_ref = tables_ref.at[:, pl.ds(half, half)]
    me = lax.axis_index("stream")
    side = lax.axis_index("span")
    lender = side % 2 == 0
    partner = side + 1 - 2 * (side % 2)
    rows, tracers, dof, columns = start_ref.shape
    sets = tracers
    own = sets * (columns // width)
    lent = sets * lend
    kept = own - lent
    first_cols = columns - lend * width
    count = jnp.where(lender, kept, own + lent)
    first_dev = me == 0
    last_dev = me == length - 1

    @pl.when(first_dev)
    def _():
        recv_f[...] = jnp.zeros(recv_f.shape, jnp.float32)

    @pl.when(last_dev)
    def _():
        recv_b[...] = jnp.zeros(recv_b.shape, jnp.float32)

    barrier = pltpu.get_barrier_semaphore()
    for target in (me - 1, me + 1):
        @pl.when(jnp.logical_and(target >= 0, target < length))
        def _():
            pl.semaphore_signal(barrier, inc=1, device_id={"stream": target},
                                device_id_type=pl.DeviceIdType.MESH)
    pl.semaphore_signal(barrier, inc=1, device_id={"span": partner}, device_id_type=pl.DeviceIdType.MESH)
    ends = jnp.logical_or(first_dev, last_dev)

    @pl.when(ends)
    def _():
        pl.semaphore_wait(barrier, 2)

    @pl.when(jnp.logical_not(ends))
    def _():
        pl.semaphore_wait(barrier, 3)

    lend_cols = pl.ds(first_cols, lend * width)
    small_refs = (types_ref, coeff_ref, scale_ref, inverse_ref)

    def lend_copies():
        copies = [pltpu.make_async_remote_copy(
            src_ref=start_ref.at[:, :, :, lend_cols], dst_ref=ext_start, send_sem=lend_sems.at[0, 0],
            recv_sem=lend_sems.at[1, 0], device_id={"span": partner}, device_id_type=pl.DeviceIdType.MESH)]
        for index, ref in enumerate(small_refs):
            target = ext_types if index == 0 else ext_small.at[index - 1]
            copies.append(pltpu.make_async_remote_copy(
                src_ref=ref.at[:, lend_cols], dst_ref=target, send_sem=lend_sems.at[0, index + 1],
                recv_sem=lend_sems.at[1, index + 1], device_id={"span": partner},
                device_id_type=pl.DeviceIdType.MESH))
        return copies

    @pl.when(lender)
    def _():
        for copy in lend_copies():
            copy.start()

    def copy_f(k):
        return pltpu.make_async_remote_copy(
            src_ref=send_f.at[k], dst_ref=recv_f.at[k], send_sem=sems.at[0, k], recv_sem=sems.at[1, k],
            device_id={"stream": me + 1}, device_id_type=pl.DeviceIdType.MESH)

    def copy_b(k):
        return pltpu.make_async_remote_copy(
            src_ref=send_b.at[k], dst_ref=recv_b.at[k], send_sem=sems.at[2, k], recv_sem=sems.at[3, k],
            device_id={"stream": me - 1}, device_id_type=pl.DeviceIdType.MESH)

    def copy_back(j):
        tracer = j % sets
        cols = pl.ds(pl.multiple_of((j // sets) * width, width), width)
        home = pl.ds(pl.multiple_of(first_cols + (j // sets) * width, width), width)
        return pltpu.make_async_remote_copy(
            src_ref=ext_out.at[:, tracer, :, cols], dst_ref=out_ref.at[:, tracer, :, home],
            send_sem=back_sems.at[0, j], recv_sem=back_sems.at[1, j], device_id={"span": partner},
            device_id_type=pl.DeviceIdType.MESH)

    def forward_rows(k, tracer, cols, start, small, part):
        @pl.when(jnp.logical_not(first_dev))
        def _():
            copy_f(k).wait_recv()

        state = recv_f[k]
        for row in range(rows):
            types = small(0)[pl.ds(row, 1), cols]
            coeff = small(1)[pl.ds(row, 1), cols]
            state = start[row, tracer, :, cols] - coeff * kernel_masked(up_ref, types, state)
            part[row, tracer, :, cols] = state
        send_f[k] = state

        @pl.when(jnp.logical_not(last_dev))
        def _():
            copy_f(k).start()

    def backward_rows(k, tracer, cols, small, part, out):
        @pl.when(jnp.logical_not(last_dev))
        def _():
            copy_b(k).wait_recv()

        state = recv_b[k]
        for row in range(rows - 1, -1, -1):
            types = small(0)[pl.ds(row, 1), cols]
            scale = small(2)[pl.ds(row, 1), cols]
            solved = part[row, tracer, :, cols] - state * small(3)[pl.ds(row, 1), cols]
            out[row, tracer, :, cols] = solved
            state = scale * kernel_masked(down_ref, types, solved)
        send_b[k] = state

        @pl.when(jnp.logical_not(first_dev))
        def _():
            copy_b(k).start()

    def own_small(index):
        return small_refs[index]

    def ext_small_ref(index):
        return ext_types if index == 0 else ext_small.at[index - 1]

    def place(k):
        return k % sets, pl.ds(pl.multiple_of((k // sets) * width, width), width)

    def forward_block(k):
        @pl.when(k < own)
        def _():
            tracer, cols = place(k)
            forward_rows(k, tracer, cols, start_ref, own_small, part_ref)

        @pl.when(k == own)
        def _():
            for copy in lend_copies():
                copy.wait_recv()

        @pl.when(k >= own)
        def _():
            tracer, cols = place(k - own)
            forward_rows(k, tracer, cols, ext_start, ext_small_ref, ext_part)

    def backward_block(k):
        @pl.when(k < own)
        def _():
            tracer, cols = place(k)
            backward_rows(k, tracer, cols, own_small, part_ref, out_ref)

        @pl.when(k >= own)
        def _():
            tracer, cols = place(k - own)
            backward_rows(k, tracer, cols, ext_small_ref, ext_part, ext_out)
            copy_back(k - own).start()

    lead = jnp.minimum(jnp.maximum((2 * (length - 1) - 2 * me) * 4, 1), count)
    tail = 2 * count - lead

    def step(s, carry):
        paired = jnp.logical_and(s >= lead, s < tail)
        odd = (s - lead) % 2 == 1

        @pl.when(s < lead)
        def _():
            forward_block(s)

        @pl.when(jnp.logical_and(paired, odd))
        def _():
            forward_block(lead + (s - lead) // 2)

        @pl.when(jnp.logical_and(paired, jnp.logical_not(odd)))
        def _():
            backward_block((s - lead) // 2)

        @pl.when(s >= tail)
        def _():
            backward_block(s - count)

        return carry

    lax.fori_loop(0, 2 * count, step, 0)

    def drain_f(k, carry):
        copy_f(k).wait_send()
        return carry

    def drain_b(k, carry):
        copy_b(k).wait_send()
        return carry

    @pl.when(jnp.logical_not(last_dev))
    def _():
        lax.fori_loop(0, count, drain_f, 0)

    @pl.when(jnp.logical_not(first_dev))
    def _():
        lax.fori_loop(0, count, drain_b, 0)

    def drain_back(j, carry):
        copy_back(j).wait_send()
        return carry

    def take_back(j, carry):
        copy_back(j).wait_recv()
        return carry

    @pl.when(lender)
    def _():
        for copy in lend_copies():
            copy.wait_send()
        lax.fori_loop(0, lent, take_back, 0)

    @pl.when(jnp.logical_not(lender))
    def _():
        lax.fori_loop(0, lent, drain_back, 0)


def both_sweeps(width, start, types, ratios, scale, tables):
    rows, tracers, dof, columns = start.shape
    groups = columns // width
    lend = max(1, groups * 5 // 8)
    blocks = tracers * (groups + lend)
    lent = tracers * lend
    length = lax.axis_size("stream")
    vmem = pltpu.VMEM
    ext_shape = (rows, tracers, dof, lend * width)
    return pl.pallas_call(
        functools.partial(both_kernel, length, width, lend),
        out_shape=jax.ShapeDtypeStruct(start.shape, jnp.float32),
        in_specs=[pl.BlockSpec(memory_space=vmem)] * 5,
        out_specs=pl.BlockSpec(memory_space=vmem),
        scratch_shapes=[
            pltpu.VMEM(start.shape, jnp.float32),
            pltpu.VMEM(ext_shape, jnp.float32),
            pltpu.VMEM((rows, lend * width), jnp.int32),
            pltpu.VMEM((3, rows, lend * width), jnp.float32),
            pltpu.VMEM(ext_shape, jnp.float32),
            pltpu.VMEM(ext_shape, jnp.float32),
            pltpu.VMEM((blocks, dof, width), jnp.float32),
            pltpu.VMEM((blocks, dof, width), jnp.float32),
            pltpu.VMEM((blocks, dof, width), jnp.float32),
            pltpu.VMEM((blocks, dof, width), jnp.float32),
            pltpu.SemaphoreType.DMA((4, blocks)),
            pltpu.SemaphoreType.DMA((2, 5)),
            pltpu.SemaphoreType.DMA((2, lent)),
        ],
        compiler_params=pltpu.CompilerParams(
            collective_id=0, has_side_effects=True, vmem_limit_bytes=60 * 1024 * 1024
        ),
    )(start, types, ratios, scale, tables)


def per_device(
    rhs, lagged, face_types, stream_scale, span_scale, absorb, up_blocks, down_blocks, diag_inverse
):
    columns = rhs.shape[3]
    dof = up_blocks.shape[1]
    padded = padded_2(lagged, (("span", 3),), 1)
    denominator = stream_scale + span_scale[0] + span_scale[1] + absorb
    span_terms = span_block(padded, face_types, span_scale, up_blocks, 0, columns)
    start = jnp.einsum("pq,nrqc->nrpc", diag_inverse, rhs - span_terms, precision=fast)
    start = start / denominator[:, None, None, :]
    ratios = jnp.stack([stream_scale, jnp.ones_like(stream_scale)]) / denominator
    both = jnp.einsum("pq,tqs->tps", diag_inverse, jnp.concatenate([up_blocks, down_blocks]), precision=precise)
    kinds = up_blocks.shape[0]
    flat = jnp.transpose(both, (1, 0, 2)).reshape(dof, 2 * kinds * dof)
    high = lax.reduce_precision(flat, exponent_bits=8, mantissa_bits=7)
    low = (flat - high).astype(jnp.bfloat16)
    high = high.astype(jnp.bfloat16)
    width = kinds * dof
    pieces = []
    for part in (slice(0, width), slice(width, 2 * width)):
        pieces += [high[:, part], low[:, part], high[:, part]]
    tables = jnp.concatenate(pieces, axis=1)
    small = [face_types, ratios, stream_scale]
    return both_sweeps(LANES, start, *small, tables)


def solution(mesh):
    return jax.shard_map(
        per_device,
        mesh=mesh,
        in_specs=(
            P("stream", None, None, "span"),
            P("stream", None, None, "span"),
            P(None, "stream", "span"),
            P("stream", "span"),
            P(None, "stream", "span"),
            P("stream", "span"),
            P(),
            P(),
            P(),
        ),
        out_specs=P("stream", None, None, "span"),
        check_vma=False,
    )
```
